32 devices in a mesh: dp: 4 (over z), chan: 8 (over y, x, core).
Axes of the slice: x: 2, y: 2, z: 4, core: 2. Of those that a mesh axis runs over, the one named last changes fastest.
Arguments:
- images: float32 [3, 32768], P(None, 'dp'), may hold values from -56 to 56
- frame_kinds: int32 [8], P('dp'), may hold values from 1 to 2
- series_len: int32 [8, 4], P('dp'), may hold values from 1 to 4
- probes: float32 [3, 32768], P(None, 'dp'), may hold values from -6 to 6
- cot_z: float32 [3, 32768], P(None, 'dp'), may hold values from -6 to 6
- cot_logdet: float32 [8, 4], P('dp'), may hold values from -4 to 4
- weight1: float32 [512, 27], P('chan'), may hold values from -6 to 6
- weight2: float32 [512, 512], P(None, 'chan'), may hold values from -6 to 6
- weight3: float32 [27, 512], P(None, 'chan'), may hold values from -6 to 6
- biases: float32 [2, 512], P(None, 'chan'), may hold values from 0 to 2.5
- small_params: float32 [3, 3], replicated, may hold values from -2 to 2
- power_u1: float32 [512], P('chan'), may hold values from -6 to 6
- power_u2: float32 [512], replicated, may hold values from -6 to 6
- power_u3: float32 [3], replicated, may hold values from -3 to 3
- moment_w1: float32 [512, 27], P('chan'), may hold values from -0.0014648438 to 0.0014648438
- second_w1: float32 [512, 27], P('chan'), may hold values from 5.3405763e-08 to 2.0980835e-07
- moment_w2: float32 [512, 512], P(None, 'chan'), may hold values from -0.0017089844 to 0.0017089844
- second_w2: float32 [512, 512], P(None, 'chan'), may hold values from 6.866455e-08 to 2.822876e-07
- moment_w3: float32 [27, 512], P(None, 'chan'), may hold values from -0.0234375 to 0.0234375
- second_w3: float32 [27, 512], P(None, 'chan'), may hold values from 1.1328125e-05 to 4.4921875e-05
- moment_bias: float32 [2, 512], P(None, 'chan'), may hold values from -0.0017089844 to 0.0017089844
- second_bias: float32 [2, 512], P(None, 'chan'), may hold values from 6.866455e-08 to 2.822876e-07
- moment_small: float32 [3, 3], replicated, may hold values from -0.625 to 0.625
- second_small: float32 [3, 3], replicated, may hold values from 0.0082 to 0.033
Outputs:
- z_out: float32 [3, 32768], P(None, 'dp')
- logdet: float32 [8, 4], P('dp')
- grad_input: float32 [3, 32768], P(None, 'dp')
- grad_norm: float32 [], replicated
- new_weight1: float32 [512, 27], P('chan')
- new_moment1: float32 [512, 27], P('chan')
- new_second1: float32 [512, 27], P('chan')
- new_weight2: float32 [512, 512], P(None, 'chan')
- new_moment2: float32 [512, 512], P(None, 'chan')
- new_second2: float32 [512, 512], P(None, 'chan')
- new_weight3: float32 [27, 512], P(None, 'chan')
- new_moment3: float32 [27, 512], P(None, 'chan')
- new_second3: float32 [27, 512], P(None, 'chan')
- clipped_bias: float32 [2, 512], P(None, 'chan')
- new_moment_bias: float32 [2, 512], P(None, 'chan')
- new_second_bias: float32 [2, 512], P(None, 'chan')
- new_small: float32 [3, 3], replicated
- new_moment_small: float32 [3, 3], replicated
- new_second_small: float32 [3, 3], replicated
- low_weight1: bfloat16 [512, 27], P('chan')
- low_weight2: bfloat16 [512, 512], P(None, 'chan')
- low_weight3: bfloat16 [27, 512], P(None, 'chan')
- new_u1: float32 [512], P('chan')
- new_v1: float32 [27], replicated
- new_u2: float32 [512], replicated
- new_v2: float32 [512], P('chan')
- new_u3: float32 [3], replicated
- new_v3: float32 [9, 512], P(None, 'chan')
The draws below stay inside these ranges and needn't reach their ends.
Inputs may be any that keep to these rules, and one draw needn't show every extreme that they name: `frame_kinds`: 1: one 64 x 64 image; 2: four 32 x 32 images. `series_len`: slots of kind-1 frames other than slot 0 hold no image.
All inputs are finite; a program needn't handle non-finite values.
Results may differ from the reference program's by a relative error of at most 0.0094.
Values may be sent and summed in bfloat16 or wider, within the bound.
No kernel may reach another device: no remote copies, remote signals or barrier semaphores. Data moves between devices by JAX's collectives and lax.ppermute only.
A program may use at most 192 MiB of HBM per device.

```python
import math
import jax
import jax.numpy as jnp
from jax import lax

CH = 512
NMAX = 4
STEP = 7
FRAMES = 8
PIX = 32768


def channel_ramp(count):
    top_ratio = 3.0
    position = lax.iota(jnp.float32, count) / (count - 1.0)
    return jnp.exp(jnp.log(top_ratio) * position) / (0.5 * (1.0 + top_ratio))


def first_weight(key):
    raw = jnp.clip(jax.random.normal(jax.random.fold_in(key, 101), (CH, 27), jnp.float32), -6.0, 6.0) * 27.0 ** (-0.5)
    return jnp.clip(raw * channel_ramp(CH)[:, None], -6.0, 6.0)


def draw_weight1(key, part):
    return first_weight(key)


def draw_weight2(key, part):
    noise = jnp.clip(jax.random.normal(jax.random.fold_in(key, 202), (CH, CH), jnp.float32), -6.0, 6.0) * (0.6 * CH ** (-0.5))
    base = jnp.eye(CH, dtype=jnp.float32) + noise
    return jnp.clip(base * channel_ramp(CH)[None, :], -6.0, 6.0)


def draw_weight3(key, part):
    first = first_weight(key)
    flipped = first.reshape(CH, 3, 9)[:, :, ::-1].reshape(CH, 27).T
    noise = jnp.clip(jax.random.normal(jax.random.fold_in(key, 303), (27, CH), jnp.float32), -6.0, 6.0) * (9.0 * CH) ** (-0.5)
    return jnp.clip(1.5 * CH ** (-0.5) * flipped + noise, -6.0, 6.0)


def with_ends(array, key, low, high):
    dims = array.shape
    index_at = [jax.random.randint(jax.random.fold_in(key, axis), (), 0, dims[axis]) for axis in range(len(dims))]
    array = array.at[tuple(index_at)].set(low)
    longest = dims.index(max(dims))
    index_at[longest] = (index_at[longest] + 1) % dims[longest]
    return array.at[tuple(index_at)].set(high)


def steps_of(stream_key, dims, cuts, low, largest):
    loudness = 1.0
    for dim, blocks in cuts:
        heights = jax.random.uniform(jax.random.fold_in(jax.random.fold_in(stream_key, 6), dim), (blocks,), jnp.float32, low / len(cuts), largest / len(cuts))
        loudness = loudness * jnp.repeat(jnp.exp(heights), dims[dim] // blocks).reshape((-1,) + (1,) * (len(dims) - 1 - dim))
    return loudness


def centred(stream_key, shape, width, reach, split=(), kind=jnp.bfloat16):
    loudness = steps_of(stream_key, shape, split, -0.22, 0.18) if split else 1.0
    entries = jax.random.normal(stream_key, shape, jnp.float32) * width * loudness
    return jnp.minimum(jnp.maximum(entries, -reach), reach).astype(kind)


def setup_inputs(seed: int = 0) -> dict:
    seeds = jax.random.split(jax.random.key(seed), 25)
    images = centred(seeds[0], (3, PIX), 14.0, 56.0, ((1, 4),), jnp.float32)
    frame_kinds = with_ends(jax.random.randint(seeds[1], (FRAMES,), 1, 3), jax.random.fold_in(seeds[1], 1), 1, 2).astype(jnp.int32)
    series_len = with_ends(jax.random.randint(seeds[2], (FRAMES, 4), 1, NMAX + 1), jax.random.fold_in(seeds[2], 1), 1, NMAX).astype(jnp.int32)
    probes = centred(seeds[3], (3, PIX), 1.0, 6.0, ((1, 4),), jnp.float32)
    cot_z = centred(seeds[4], (3, PIX), 1.0, 6.0, ((1, 4),), jnp.float32)
    cot_logdet = centred(seeds[5], (FRAMES, 4), 1.0, 4.0, ((0, 4),), jnp.float32)
    weight1 = draw_weight1(jax.random.fold_in(seeds[24], 71), 0)
    weight2 = draw_weight2(jax.random.fold_in(seeds[24], 71), 0)
    weight3 = draw_weight3(jax.random.fold_in(seeds[24], 71), 0)
    biases = jnp.clip(2.5 * jax.random.uniform(seeds[9], (2, CH), jnp.float32) ** steps_of(seeds[9], (2, CH), ((1, 8),), -0.2, 0.2), 0.0, 2.5)
    small_params = centred(seeds[10], (3, 3), 0.5, 2.0, (), jnp.float32)
    power_u1 = centred(seeds[11], (CH,), 1.0, 6.0, ((0, 8),), jnp.float32)
    power_u2 = centred(seeds[12], (CH,), 1.0, 6.0, (), jnp.float32)
    power_u3 = centred(seeds[13], (3,), 1.0, 3.0, (), jnp.float32)
    moment_w1 = centred(seeds[14], (CH, 27), (0.13 / CH), 0.0014648438, ((0, 8),), jnp.float32)
    second_w1 = jnp.clip(jnp.exp(math.log(2.0980834847250662e-07) - 1.3682758 * jax.random.uniform(seeds[15], (CH, 27), jnp.float32) ** steps_of(seeds[15], (CH, 27), ((0, 8),), -0.2, 0.2)), 5.340576336720915e-08, 2.0980834847250662e-07)
    moment_w2 = centred(seeds[16], (CH, CH), (0.15 / CH), 0.0017089844, ((1, 8),), jnp.float32)
    second_w2 = jnp.clip(jnp.exp(math.log(2.822876012942288e-07) - 1.4136934 * jax.random.uniform(seeds[17], (CH, CH), jnp.float32) ** steps_of(seeds[17], (CH, CH), ((1, 8),), -0.2, 0.2)), 6.866454782539222e-08, 2.822876012942288e-07)
    moment_w3 = centred(seeds[18], (27, CH), (0.084 / CH ** 0.5), 0.0234375, ((1, 8),), jnp.float32)
    second_w3 = jnp.clip(jnp.exp(math.log(4.492187508731149e-05) - 1.3776363 * jax.random.uniform(seeds[19], (27, CH), jnp.float32) ** steps_of(seeds[19], (27, CH), ((1, 8),), -0.2, 0.2)), 1.132812485593604e-05, 4.492187508731149e-05)
    moment_bias = centred(seeds[20], (2, CH), (0.15 / CH), 0.0017089844, ((1, 8),), jnp.float32)
    second_bias = jnp.clip(jnp.exp(math.log(2.822876012942288e-07) - 1.4136934 * jax.random.uniform(seeds[21], (2, CH), jnp.float32) ** steps_of(seeds[21], (2, CH), ((1, 8),), -0.2, 0.2)), 6.866454782539222e-08, 2.822876012942288e-07)
    moment_small = centred(seeds[22], (3, 3), 0.1, 0.625, (), jnp.float32)
    second_small = jnp.clip(jnp.exp(jax.random.uniform(seeds[23], (3, 3), jnp.float32, math.log(0.0082), math.log(0.033))), 0.0082, 0.033)
    return dict(images=images, frame_kinds=frame_kinds, series_len=series_len, probes=probes, cot_z=cot_z, cot_logdet=cot_logdet, weight1=weight1, weight2=weight2, weight3=weight3, biases=biases, small_params=small_params, power_u1=power_u1, power_u2=power_u2, power_u3=power_u3, moment_w1=moment_w1, second_w1=second_w1, moment_w2=moment_w2, second_w2=second_w2, moment_w3=moment_w3, second_w3=second_w3, moment_bias=moment_bias, second_bias=second_bias, moment_small=moment_small, second_small=second_small)


SHRINK = 0.98
LR_RATE = 0.05
BETA_ONE = 0.5
BETA_TWO = 0.55
ADAM_EPS = 1e-08
DECAY = 0.01
CLIP_LIMIT = 1.0
TAP_SHIFTS = ((-1, -1), (-1, 0), (-1, 1), (0, -1), (0, 0), (0, 1), (1, -1), (1, 0), (1, 1))

@jax.custom_vjp
def low(v):
    return lax.optimization_barrier(v.astype(jnp.bfloat16)).astype(jnp.float32)

@jax.custom_vjp
def low_back(v):
    return v

def low_keep(v):
    return (low(v), None)

def low_pass(kept, grad):
    return (grad,)

def back_keep(v):
    return (v, None)

def back_low(kept, grad):
    return (low(grad),)
low.defvjp(low_keep, low_pass)
low_back.defvjp(back_keep, back_low)

def precise_dot(left_mat, right_mat):
    return jnp.dot(left_mat, right_mat, precision=lax.Precision.HIGHEST)

def lipswish(values):
    return values * jax.nn.sigmoid(values) / 1.1

def swish_slope(values):
    sigm = jax.nn.sigmoid(values)
    return (sigm + values * sigm * (1.0 - sigm)) / 1.1

def make_masks(frame_kinds):
    total_pix = frame_kinds.shape[0] * 4096
    positions = lax.iota(jnp.int32, total_pix)
    kind_pix = jnp.repeat(frame_kinds, 4096)
    whole = kind_pix == 1
    pix_row = positions // 64 % 64
    pix_col = positions % 64
    pix_row = jnp.where(whole, pix_row, pix_row % 32)
    pix_col = jnp.where(whole, pix_col, pix_col % 32)
    limit = jnp.where(whole, 64, 32)
    mask_list = []
    for shift_y, shift_x in TAP_SHIFTS:
        inside = (pix_row + shift_y >= 0) & (pix_row + shift_y < limit) & (pix_col + shift_x >= 0) & (pix_col + shift_x < limit)
        mask_list.append(inside.astype(jnp.float32))
    return jnp.stack(mask_list)

def gather_taps(planes, tap_masks):
    pieces = []
    for tap_index, shift_pair in enumerate(TAP_SHIFTS):
        offset = shift_pair[0] * 64 + shift_pair[1]
        pieces.append(jnp.roll(planes, -offset, axis=1) * tap_masks[tap_index])
    return jnp.stack(pieces, axis=1).reshape(planes.shape[0] * 9, planes.shape[1])

def combine_taps(tap_values, tap_masks):
    shaped = tap_values.reshape(-1, 9, tap_values.shape[1])
    result = jnp.zeros((shaped.shape[0], shaped.shape[2]), tap_values.dtype)
    for tap_index, shift_pair in enumerate(TAP_SHIFTS):
        offset = shift_pair[0] * 64 + shift_pair[1]
        result = result + jnp.roll(shaped[:, tap_index], -offset, axis=1) * tap_masks[tap_index]
    return result

def slot_sum(values, frame_kinds):
    frames = frame_kinds.shape[0]
    quads = values.reshape(frames, 2, 32, 2, 32).sum(axis=(2, 4)).reshape(frames, 4)
    whole = quads.sum(axis=1)
    first_slot = lax.iota(jnp.int32, 4) == 0
    return jnp.where(frame_kinds[:, None] == 2, quads, jnp.where(first_slot[None, :], whole[:, None], 0.0))

def pixel_counts(frame_kinds):
    first_slot = lax.iota(jnp.int32, 4) == 0
    return jnp.where(frame_kinds[:, None] == 2, 1024.0, jnp.where(first_slot[None, :], 4096.0, 0.0)).astype(jnp.float32)

def normalize(values):
    return values / jnp.sqrt(jnp.sum(values * values) + 1e-12)

def power_iterate(weight1, weight2, weight3, power_u1, power_u2, power_u3):
    weight_cube = weight3.reshape(3, 9, weight3.shape[1])
    for power_step in range(2):
        vec_one = normalize(precise_dot(weight1.T, power_u1))
        vec_two = normalize(precise_dot(weight2.T, power_u2))
        vec_three = normalize(jnp.einsum('otc,o->tc', weight_cube, power_u3, precision=lax.Precision.HIGHEST))
        power_u1 = normalize(precise_dot(weight1, vec_one))
        power_u2 = normalize(precise_dot(weight2, vec_two))
        power_u3 = normalize(jnp.einsum('otc,tc->o', weight_cube, vec_three, precision=lax.Precision.HIGHEST))
    return (power_u1, vec_one, power_u2, vec_two, power_u3, vec_three)

def moment_step(grad, moment, second):
    new_moment = BETA_ONE * moment + (1.0 - BETA_ONE) * grad
    new_second = BETA_TWO * second + (1.0 - BETA_TWO) * grad * grad
    return (new_moment, new_second)

def adam_step(param, grad, moment, second):
    new_moment, new_second = moment_step(grad, moment, second)
    fix_one = 1.0 - BETA_ONE ** STEP
    fix_two = 1.0 - BETA_TWO ** STEP
    update = new_moment / fix_one / (jnp.sqrt(new_second / fix_two) + ADAM_EPS) + DECAY * param
    return (param - LR_RATE * update, new_moment, new_second)

def reference(images, frame_kinds, series_len, probes, cot_z, cot_logdet, weight1, weight2, weight3, biases, small_params, power_u1, power_u2, power_u3, moment_w1, second_w1, moment_w2, second_w2, moment_w3, second_w3, moment_bias, second_bias, moment_small, second_small):
    tap_masks = make_masks(frame_kinds)
    counts = pixel_counts(frame_kinds)
    new_u1, new_v1, new_u2, new_v2, new_u3, new_v3 = power_iterate(weight1, weight2, weight3, power_u1, power_u2, power_u3)
    series_coef = []
    for series_step in range(NMAX):
        term_sign = (-1.0) ** series_step / (series_step + 1)
        series_coef.append(jnp.where(series_len >= series_step + 1, term_sign, 0.0).astype(jnp.float32))

    def network(images, small_params, weight1, weight2, weight3, biases):
        act_scale = jnp.exp(small_params[1])[:, None]
        normed = (images + small_params[0][:, None]) * act_scale
        mapped_one = precise_dot(weight1, new_v1)
        mapped_two = precise_dot(weight2, new_v2)
        mapped_three = jnp.einsum('otc,tc->o', weight3.reshape(3, 9, weight3.shape[1]), new_v3, precision=lax.Precision.HIGHEST)
        wn_one = low(SHRINK * weight1 / jnp.sqrt(jnp.sum(mapped_one * mapped_one)))
        wn_two = low(SHRINK * weight2 / jnp.sqrt(jnp.sum(mapped_two * mapped_two)))
        wn_three = low(SHRINK * weight3 / jnp.sqrt(jnp.sum(mapped_three * mapped_three)))
        slope_zero = swish_slope(normed)
        taps_in = low(gather_taps(lipswish(normed), tap_masks))
        act_one = low_back(precise_dot(wn_one, taps_in)) + biases[0][:, None]
        slope_one = swish_slope(act_one)
        hidden_one = low(lipswish(act_one))
        act_two = low_back(precise_dot(wn_two, hidden_one)) + biases[1][:, None]
        slope_two = swish_slope(act_two)
        hidden_two = low(lipswish(act_two))
        branch = low_back(precise_dot(wn_three, hidden_two))
        z_out = normed + combine_taps(branch, tap_masks) + small_params[2][:, None]
        logdet = counts * jnp.sum(small_params[1])
        current = probes
        for series_step in range(NMAX):
            tan_taps = low(gather_taps(slope_zero * current, tap_masks))
            tan_one = low(slope_one * low_back(precise_dot(wn_one, tan_taps)))
            tan_two = low(slope_two * low_back(precise_dot(wn_two, tan_one)))
            current = combine_taps(low_back(precise_dot(wn_three, tan_two)), tap_masks)
            logdet = logdet + series_coef[series_step] * slot_sum(lax.optimization_barrier(jnp.sum(probes * current, axis=0)), frame_kinds)
        return (z_out, logdet)
    (z_out, logdet), pullback = jax.vjp(network, images, small_params, weight1, weight2, weight3, biases)
    grad_x, grad_small, grad_w1, grad_w2, grad_w3, grad_bias = pullback((cot_z, cot_logdet))
    square = jnp.sum(grad_w1 * grad_w1) + jnp.sum(grad_w2 * grad_w2) + jnp.sum(grad_w3 * grad_w3)
    square = square + jnp.sum(grad_bias * grad_bias) + jnp.sum(grad_small * grad_small)
    grad_norm = jnp.sqrt(square)
    factor = jnp.minimum(1.0, CLIP_LIMIT / (grad_norm + 1e-06))
    new_weight1, new_moment1, new_second1 = adam_step(weight1, factor * grad_w1, moment_w1, second_w1)
    new_weight2, new_moment2, new_second2 = adam_step(weight2, factor * grad_w2, moment_w2, second_w2)
    new_weight3, new_moment3, new_second3 = adam_step(weight3, factor * grad_w3, moment_w3, second_w3)
    clipped_bias = factor * grad_bias
    new_moment_bias, new_second_bias = moment_step(clipped_bias, moment_bias, second_bias)
    new_small, new_moment_small, new_second_small = adam_step(small_params, factor * grad_small, moment_small, second_small)
    return (z_out, logdet, grad_x, grad_norm, new_weight1, new_moment1, new_second1, new_weight2, new_moment2, new_second2, new_weight3, new_moment3, new_second3, clipped_bias, new_moment_bias, new_second_bias, new_small, new_moment_small, new_second_small, new_weight1.astype(jnp.bfloat16), new_weight2.astype(jnp.bfloat16), new_weight3.astype(jnp.bfloat16), new_u1, new_v1, new_u2, new_v2, new_u3, new_v3)
```

```python
import functools

import jax
import jax.numpy as jnp
from jax import lax
from jax.experimental import pallas as pl
from jax.experimental.pallas import tpu as pltpu
from jax.sharding import PartitionSpec as P

NMAX = 4
STEP = 7
SHRINK = 0.98
LR_RATE = 0.05
BETA_ONE = 0.5
BETA_TWO = 0.55
ADAM_EPS = 1e-08
DECAY = 0.01
CLIP_LIMIT = 1.0

WIDTH = 64
FRAME = 4096
BLOCK = 256
HALO = 2 * NMAX * WIDTH
LANES = 128
TAP_ROWS = 72
F32 = jnp.float32
BF16 = jnp.bfloat16
HIGH = lax.Precision.HIGHEST


def iota(shape, dim):
    return lax.broadcasted_iota(jnp.int32, shape, dim)


def dot_nn(left, right, precision=None):
    return lax.dot_general(
        left, right, (((1,), (0,)), ((), ())), precision=precision, preferred_element_type=F32
    )


def dot_nt(left, right, precision=None):
    return lax.dot_general(
        left, right, (((1,), (1,)), ((), ())), precision=precision, preferred_element_type=F32
    )


def dot_tn(left, right, precision=None):
    return lax.dot_general(
        left, right, (((0,), (0,)), ((), ())), precision=precision, preferred_element_type=F32
    )


def spread_one():
    row = iota((27, LANES), 0)
    return (iota((27, LANES), 1) == (row % 9) * 8 + row // 9).astype(F32)


def spread_three():
    row = iota((27, LANES), 0)
    return (iota((27, LANES), 1) == (8 - row % 9) * 8 + 4 + row // 9).astype(F32)


def lane_is_one(lane):
    return (lane % 8 < 3) & (lane < TAP_ROWS)


def lane_is_three(lane):
    return (lane % 8 >= 4) & (lane % 8 < 7) & (lane < TAP_ROWS)


def pack_kernel(w1_ref, w2_ref, w3_ref, bias_ref, u1_ref, out_ref):
    channels = w2_ref.shape[0]
    out_ref[:, 0:channels] = w2_ref[...].T
    tile = dot_nn(w1_ref[...], spread_one(), HIGH) + dot_tn(w3_ref[...], spread_three(), HIGH)
    lane = iota((1, LANES), 1)
    for index, row in enumerate((u1_ref[...], bias_ref[0:1, :], bias_ref[1:2, :])):
        column = jnp.broadcast_to(row, (8, row.shape[1])).T[:, 0:1]
        tile = jnp.where(lane == TAP_ROWS + index, column, tile)
    out_ref[:, channels:] = tile


def col_taps(state, masks):
    size = state.shape[1]
    row_up, row_down, col_left, col_right = masks
    left = col_left * pltpu.roll(state, 1, 1)
    right = col_right * pltpu.roll(state, size - 1, 1)
    pieces = []
    for shift_y in (-1, 0, 1):
        for plane in (left, state, right):
            if shift_y == -1:
                plane = row_up * pltpu.roll(plane, WIDTH, 1)
            if shift_y == 1:
                plane = row_down * pltpu.roll(plane, size - WIDTH, 1)
            pieces.append(plane)
    return pieces


def comb_taps(q_ref, lanes, masks):
    size = lanes.size
    row_up, row_down, col_left, col_right = masks
    result = None
    for shift_y in (-1, 0, 1):
        base = 24 * (shift_y + 1)
        line = (
            col_left * pltpu.roll(q_ref[base : base + 8, lanes], 1, 1)
            + q_ref[base + 8 : base + 16, lanes]
            + col_right * pltpu.roll(q_ref[base + 16 : base + 24, lanes], size - 1, 1)
        )
        if shift_y == -1:
            line = row_up * pltpu.roll(line, WIDTH, 1)
        if shift_y == 1:
            line = row_down * pltpu.roll(line, size - WIDTH, 1)
        result = line if result is None else result + line
    return result


def normed_by(values, square):
    return values / jnp.sqrt(square + 1e-12)


def main_kernel(
    index_ref, x0_ref, x1_ref, u2_ref, u3_ref, planes_ref, small_ref,
    keep_ref, send_ref, cols_ref, rows_ref, og_ref,
    w_s, w13_s, w2_s, w2t_s, wout_s, bias_s, taps_s, sl1_s, sl2_s, cv1_s, cv2_s,
    lin1_s, lin2_s, gt1_s, gt2_s, acc1_s, acc2_s, tan1_s, tan2_s, g1_s, g2_s, hid1_s, hid2_s,
    q_s, q0_s, comb_s, *, own, channels, chips,
):
    me = index_ref[0]
    rows_own = channels // (2 * chips)
    region = own + 2 * HALO
    all_sum = functools.partial(jnp.sum, keepdims=True)

    for m in range(chips):
        for b, ref in ((0, x0_ref), (1, x1_ref)):
            w_s[jnp.bitwise_xor(me, 2 * m + b)] = ref[m]
    tile = w_s[:, :, channels:].reshape(channels, LANES)
    w2t = w_s[:, :, 0:channels].reshape(channels, channels)
    lane = iota((1, LANES), 1)
    is_one = lane_is_one(lane)
    is_three = lane_is_three(lane)
    taps_one = jnp.where(is_one, tile, 0.0)
    taps_three = jnp.where(is_three, tile, 0.0)
    head = (lane % 8 == 4) & (lane < TAP_ROWS)
    u1 = tile[:, TAP_ROWS : TAP_ROWS + 1]
    u2 = u2_ref[...]
    u3 = u3_ref[...]
    for _ in range(2):
        v1 = all_sum(taps_one * u1, axis=0)
        v2 = all_sum(w2t * u2, axis=1)
        mixed = taps_three * u3
        mixed = mixed + pltpu.roll(mixed, LANES - 1, 1) + pltpu.roll(mixed, LANES - 2, 1)
        v3 = jnp.where(head, mixed, 0.0)
        v1 = normed_by(v1, all_sum(v1 * v1))
        v2 = normed_by(v2, all_sum(v2 * v2))
        v3 = normed_by(v3, all_sum(all_sum(v3 * v3, axis=0), axis=1))
        m1 = all_sum(taps_one * v1, axis=1)
        m2 = all_sum(w2t * v2, axis=0)
        spread = v3 + pltpu.roll(v3, 1, 1) + pltpu.roll(v3, 2, 1)
        m3 = all_sum(taps_three * spread, axis=0)
        for shift in (64, 32, 16, 8):
            m3 = m3 + pltpu.roll(m3, shift, 1)
        square1 = all_sum(m1 * m1)
        square2 = all_sum(m2 * m2)
        square3 = all_sum(jnp.where((lane >= 4) & (lane < 7), m3 * m3, 0.0))
        u1 = normed_by(m1, square1)
        u2 = normed_by(m2, square2)
        u3 = jnp.where(is_three, normed_by(m3, square3), 0.0)
    sigma1 = jnp.sqrt(square1)
    sigma2 = jnp.sqrt(square2)
    sigma3 = jnp.sqrt(square3)
    cols_ref[...] = jnp.where(lane == 0, u1, jnp.where(lane == 1, v2, v3)).reshape(cols_ref.shape)
    sigma_row = jnp.where(lane == 0, sigma1, jnp.where(lane == 1, sigma2, sigma3))
    rows_ref[...] = jnp.zeros(rows_ref.shape, F32)
    rows_ref[0:1, :] = u2
    rows_ref[1:2, 0:LANES] = v1
    rows_ref[2:3, 0:LANES] = u3
    rows_ref[3:4, 0:LANES] = sigma_row

    scaled = taps_one * (SHRINK / sigma1) + taps_three * (SHRINK / sigma3)
    w13_s[0:channels] = jnp.where(is_one, scaled, 0.0).astype(BF16)
    w13_s[channels:] = jnp.where(is_three, scaled, 0.0).astype(BF16)
    flipped = scaled.T
    blocks = [pltpu.roll(flipped[(8 - t) * 8 : (9 - t) * 8], 4, 0) for t in range(9)]
    flipped = jnp.concatenate(blocks + [jnp.zeros((8, channels), F32)], axis=0)
    first_rows = iota((TAP_ROWS + 8, 1), 0) % 8 < 4
    wout_s[:, 0:channels] = jnp.where(first_rows, flipped, 0.0).astype(BF16)
    wout_s[:, channels:] = jnp.where(first_rows, 0.0, flipped).astype(BF16)
    w2t_scaled = w2t * (SHRINK / sigma2)
    w2t_s[...] = w2t_scaled.astype(BF16)
    w2_s[...] = w2t_scaled.T.astype(BF16)
    for layer in range(2):
        column = tile[:, TAP_ROWS + 1 + layer : TAP_ROWS + 2 + layer]
        bias_s[layer] = jnp.broadcast_to(column, (channels, LANES))

    shift8 = small_ref[:, 0:1]
    scale8 = small_ref[:, 1:2]
    bias8 = small_ref[:, 2:3]
    extra8 = small_ref[:, 3:4]
    upper = iota((8, 1), 0) >= 4
    probes8 = planes_ref[8:16]
    cot8 = planes_ref[16:24]

    def masks_at(lanes):
        return [planes_ref[32 + i : 33 + i, lanes] for i in range(4)]

    def put_taps(slot, pieces, lanes):
        taps_s[slot, 0 : TAP_ROWS + 8, lanes] = jnp.concatenate(
            pieces + [jnp.zeros((8, lanes.size), F32)], axis=0
        ).astype(BF16)
        taps_s[slot, TAP_ROWS + 8 :, lanes] = jnp.zeros((LANES - TAP_ROWS - 8, lanes.size), BF16)

    whole = pl.ds(0, region)
    h8 = (planes_ref[0:8] + shift8) * scale8
    sig8 = 0.5 + 0.5 * jnp.tanh(0.5 * h8)
    rest8 = 1.0 - sig8
    slope0 = (sig8 + h8 * sig8 * rest8) / 1.1
    curve0 = sig8 * rest8 * (2.0 + h8 * (1.0 - 2.0 * sig8)) / 1.1
    state = jnp.where(upper, cot8, h8 * sig8 / 1.1)
    put_taps(0, col_taps(state, masks_at(whole)), whole)
    state = probes8 * jnp.where(upper, planes_ref[24 + 7 : 24 + 8], slope0)
    put_taps(1, col_taps(state, masks_at(whole)), whole)

    def activation(act, slope_ref, curve_ref, lanes, curve_lanes, in_curve):
        half = 0.5 * jnp.tanh(0.5 * act)
        sig = 0.5 + half
        rest = 0.5 - half
        hidden = act * sig * (1.0 / 1.1)
        slope_ref[:, lanes] = sig * (1.0 / 1.1) + hidden * rest
        sig2 = sig * (2.0 / 1.1)

        @pl.when(in_curve)
        def _():
            curve_ref[:, curve_lanes] = (rest * (sig2 - 2.0 * half * hidden)).astype(BF16)

        return hidden.astype(BF16)

    own_blocks = own // BLOCK

    def start_body(j, carry):
        lanes = pl.ds(pl.multiple_of(j * BLOCK, LANES), BLOCK)
        in_curve = (j >= 1) & (j < own_blocks + 3)
        curve_lanes = pl.ds(pl.multiple_of(jnp.clip(j - 1, 0, own_blocks + 1) * BLOCK, LANES), BLOCK)
        taps = taps_s[0, :, lanes]
        act1 = dot_nn(w13_s[0:channels], taps)
        bias1 = bias_s[0]
        hidden1 = activation(
            act1 + jnp.concatenate([bias1, bias1], axis=1), sl1_s, cv1_s, lanes, curve_lanes, in_curve
        )
        act2 = dot_nn(w2_s[...], hidden1)
        bias2 = bias_s[1]
        hidden2 = activation(
            act2 + jnp.concatenate([bias2, bias2], axis=1), sl2_s, cv2_s, lanes, curve_lanes, in_curve
        )
        q0_s[:, lanes] = dot_nn(wout_s[:, 0:channels], hidden2)[0:TAP_ROWS]

        @pl.when((j >= 2) & (j < own_blocks + 2))
        def _():
            own_lanes = pl.ds(pl.multiple_of((j - 2) * BLOCK, LANES), BLOCK)
            hid1_s[:, own_lanes] = hidden1
            hid2_s[:, own_lanes] = hidden2

        return carry

    lax.fori_loop(0, own_blocks + 4, start_body, 0)

    own_in_slot = pl.ds(LANES, own)

    def series_stage(stage):
        offset = LANES * (stage - 1)
        count = own_blocks + 5 - stage
        tan_slot = min(stage, 3) - 1
        aligned = stage % 2 == 1
        store_from = (HALO - offset) // BLOCK if aligned else (HALO - LANES - offset) // BLOCK
        store_count = own_blocks if aligned else own_blocks + 1

        def body(j, carry):
            start = pl.multiple_of(offset + j * BLOCK, LANES)
            lanes = pl.ds(start, BLOCK)
            both = dot_nn(w13_s[...], taps_s[stage, :, lanes])
            lin1 = both[0:channels]
            gt2 = both[channels:]
            slope1 = sl1_s[:, lanes]
            slope2 = sl2_s[:, lanes]
            tan1 = (slope1 * lin1).astype(BF16)
            g2 = (slope2 * gt2).astype(BF16)
            lin2 = dot_nn(w2_s[...], tan1)
            gt1 = dot_nn(w2t_s[...], g2)
            tan2 = (slope2 * lin2).astype(BF16)
            g1 = (slope1 * gt1).astype(BF16)
            q_s[:, lanes] = dot_nn(wout_s[...], jnp.concatenate([tan2, g1], axis=0))[0:TAP_ROWS]

            @pl.when((j >= store_from) & (j < store_from + store_count))
            def _():
                slot_lanes = pl.ds(pl.multiple_of(start - (HALO - LANES), LANES), BLOCK)
                tan1_s[tan_slot, :, slot_lanes] = tan1
                tan2_s[tan_slot, :, slot_lanes] = tan2
                g1_s[tan_slot, :, slot_lanes] = g1
                g2_s[tan_slot, :, slot_lanes] = g2

            wide_lanes = pl.ds(pl.multiple_of(jnp.maximum(start - BLOCK, 0), LANES), BLOCK)
            if stage <= 2:
                wide_count = own_blocks + 3 - stage

                @pl.when((j >= 1) & (j < 1 + wide_count))
                def _():
                    lin1_s[stage - 1, :, wide_lanes] = lin1.astype(BF16)
                    lin2_s[stage - 1, :, wide_lanes] = lin2.astype(BF16)
                    gt1_s[stage - 1, :, wide_lanes] = gt1.astype(BF16)
                    gt2_s[stage - 1, :, wide_lanes] = gt2.astype(BF16)
            else:
                slot = 4 - stage
                for acc_ref, lin_ref, gt_ref, lin, gt in (
                    (acc1_s, lin1_s, gt1_s, lin1, gt1),
                    (acc2_s, lin2_s, gt2_s, lin2, gt2),
                ):
                    total = lin * gt_ref[slot, :, wide_lanes].astype(F32)
                    total = total + gt * lin_ref[slot, :, wide_lanes].astype(F32)
                    if stage == 4:
                        total = total + acc_ref[:, wide_lanes]
                    acc_ref[:, wide_lanes] = total
            return carry

        lax.fori_loop(0, count, body, 0)

        inside = pl.ds(offset, count * BLOCK)
        result = comb_taps(q_s, inside, masks_at(inside))
        core_from = HALO - offset
        comb_s[stage - 1] = result[:, core_from : core_from + own]
        if stage < NMAX:
            nxt = result[:, LANES : count * BLOCK - LANES]
            lanes = pl.ds(offset + LANES, (count - 1) * BLOCK)
            seed = probes8[:, offset + LANES : offset + LANES + (count - 1) * BLOCK]
            coef = planes_ref[24 + 4 + 3 - stage : 24 + 4 + 4 - stage, lanes]
            following = slope0[:, offset + LANES : offset + LANES + (count - 1) * BLOCK] * nxt
            following = following + jnp.where(upper, seed * coef, 0.0)
            put_taps(stage + 1, col_taps(following, masks_at(lanes)), lanes)

    def own_taps(slot):
        return taps_s[slot, :, pl.ds(HALO, own)]

    def add_weight_grads(slot_pairs, tap_pairs, first):
        total = None
        for left, right in slot_pairs:
            part = dot_nt(left, right)
            total = part if total is None else total + part
        one = None
        three = None
        for left_one, left_three, slot in tap_pairs:
            part_one = dot_nt(left_one, own_taps(slot))
            part_three = dot_nt(left_three, own_taps(slot))
            one = part_one if one is None else one + part_one
            three = part_three if three is None else three + part_three
        tile_part = jnp.where(is_one, one, jnp.where(is_three, three, 0.0))
        w2_part = total.reshape(2 * chips, rows_own, channels)
        tile_part = tile_part.reshape(2 * chips, rows_own, LANES)
        if first:
            w_s[:, :, 0:channels] = w2_part
            w_s[:, :, channels:] = tile_part
        else:
            w_s[:, :, 0:channels] = w_s[:, :, 0:channels] + w2_part
            w_s[:, :, channels:] = w_s[:, :, channels:] + tile_part

    def slot_of(ref, slot):
        return ref[slot, :, own_in_slot]

    series_stage(1)
    series_stage(2)
    series_stage(3)
    add_weight_grads(
        ((slot_of(tan1_s, 1), slot_of(g2_s, 2)), (slot_of(tan1_s, 2), slot_of(g2_s, 1))),
        (
            (slot_of(g1_s, 2), slot_of(tan2_s, 2), 2),
            (slot_of(g1_s, 1), slot_of(tan2_s, 1), 3),
        ),
        True,
    )
    series_stage(4)
    add_weight_grads(
        ((slot_of(tan1_s, 0), slot_of(g2_s, 2)), (slot_of(tan1_s, 2), slot_of(g2_s, 0))),
        (
            (slot_of(g1_s, 2), slot_of(tan2_s, 2), 1),
            (slot_of(g1_s, 0), slot_of(tan2_s, 0), 4),
        ),
        False,
    )

    def final_body(j, carry):
        bias_one, bias_two = carry
        start = pl.multiple_of(HALO - LANES + j * BLOCK, LANES)
        lanes = pl.ds(start, BLOCK)
        wide_lanes = pl.ds(pl.multiple_of(LANES + j * BLOCK, LANES), BLOCK)
        slot_lanes = pl.ds(pl.multiple_of(j * BLOCK, LANES), BLOCK)
        low_lanes = (j > 0).astype(F32)
        high_lanes = (j < own_blocks).astype(F32)
        gs2 = dot_nn(w13_s[channels:], taps_s[0, :, lanes])
        ga2 = cv2_s[:, wide_lanes].astype(F32) * acc2_s[:, wide_lanes] + sl2_s[:, lanes] * gs2
        low2 = ga2.astype(BF16)
        gs1 = dot_nn(w2t_s[...], low2)
        ga1 = cv1_s[:, wide_lanes].astype(F32) * acc1_s[:, wide_lanes] + sl1_s[:, lanes] * gs1
        low1 = ga1.astype(BF16)
        q_s[:, lanes] = q0_s[:, lanes] + dot_nn(wout_s[:, channels:], low1)[0:TAP_ROWS]
        g2_s[0, :, slot_lanes] = low2
        g1_s[0, :, slot_lanes] = low1
        bias_one = bias_one + low_lanes * ga1[:, 0:LANES] + high_lanes * ga1[:, LANES:]
        bias_two = bias_two + low_lanes * ga2[:, 0:LANES] + high_lanes * ga2[:, LANES:]
        return bias_one, bias_two

    zero = jnp.zeros((channels, LANES), F32)
    bias_one, bias_two = lax.fori_loop(0, own_blocks + 1, final_body, (zero, zero))
    add_weight_grads(
        ((hid1_s[...], slot_of(g2_s, 0)),), ((slot_of(g1_s, 0), hid2_s[...], 0),), False
    )

    inside = pl.ds(HALO - LANES, own + BLOCK)
    result = comb_taps(q_s, inside, masks_at(inside))[:, LANES : LANES + own]
    mine = slice(HALO, HALO + own)
    h_own = h8[:, mine]
    cot_own = cot8[:, mine]
    probes_own = probes8[:, mine]
    mixed = comb_s[0] * pltpu.roll(comb_s[2], 4, 0)
    mixed = mixed + comb_s[1] * pltpu.roll(comb_s[1], 4, 0)
    mixed = mixed + comb_s[2] * pltpu.roll(comb_s[0], 4, 0)
    mixed = mixed + comb_s[3] * probes_own
    grad_h = cot_own + slope0[:, mine] * result + curve0[:, mine] * mixed
    grad_in = grad_h * scale8
    density = planes_ref[24:25, mine] * comb_s[0]
    for k in range(1, NMAX):
        density = density + planes_ref[24 + k : 25 + k, mine] * comb_s[k]
    density = density * probes_own
    density = density[0:1] + density[1:2] + density[2:3]
    row8 = iota((8, 1), 0)
    out = jnp.where(row8 < 3, h_own + result + bias8, jnp.where(row8 == 3, density, grad_in))
    og_ref[...] = jnp.where(row8 < 7, out, 0.0)

    sums = (
        all_sum(grad_in, axis=1),
        all_sum(grad_h * h_own, axis=1) + extra8,
        all_sum(cot_own, axis=1),
    )
    small_row = jnp.zeros((1, LANES), F32)
    for a, column in enumerate(sums):
        for i in range(3):
            small_row = jnp.where(lane == TAP_ROWS + 2 + 3 * a + i, column[4 + i : 5 + i], small_row)
    bias_one = all_sum(bias_one, axis=1)
    bias_two = all_sum(bias_two, axis=1)
    extras = jnp.where(lane == TAP_ROWS, bias_one, jnp.where(lane == TAP_ROWS + 1, bias_two, small_row))
    extras = extras.reshape(2 * chips, rows_own, LANES)
    w_s[:, :, channels:] = w_s[:, :, channels:] + extras

    core = jnp.bitwise_and(me, 1)
    chip = jnp.right_shift(me, 1)
    for m in range(chips):
        block = 2 * jnp.bitwise_xor(chip, m)
        keep_ref[m] = w_s[block + core]
        send_ref[m] = w_s[block + 1 - core]


def call_main(me, x0, x1, u2, u3, planes, small, own, channels, chips):
    rows_own = channels // (2 * chips)
    region = own + 2 * HALO
    wide = own + 2 * BLOCK
    slot = own + BLOCK
    width = channels + LANES
    out_shape = (
        jax.ShapeDtypeStruct((chips, rows_own, width), F32),
        jax.ShapeDtypeStruct((chips, rows_own, width), F32),
        jax.ShapeDtypeStruct((2 * chips, rows_own, LANES), F32),
        jax.ShapeDtypeStruct((8, channels), F32),
        jax.ShapeDtypeStruct((8, own), F32),
    )
    vmem = pltpu.VMEM
    scratch = [
        vmem((2 * chips, rows_own, width), F32),
        vmem((2 * channels, LANES), BF16),
        vmem((channels, channels), BF16),
        vmem((channels, channels), BF16),
        vmem((TAP_ROWS + 8, 2 * channels), BF16),
        vmem((2, channels, LANES), F32),
        vmem((NMAX + 1, LANES, region), BF16),
        vmem((channels, region), F32),
        vmem((channels, region), F32),
        vmem((channels, wide), BF16),
        vmem((channels, wide), BF16),
        vmem((2, channels, wide), BF16),
        vmem((2, channels, wide), BF16),
        vmem((2, channels, wide), BF16),
        vmem((2, channels, wide), BF16),
        vmem((channels, wide), F32),
        vmem((channels, wide), F32),
        vmem((3, channels, slot), BF16),
        vmem((3, channels, slot), BF16),
        vmem((3, channels, slot), BF16),
        vmem((3, channels, slot), BF16),
        vmem((channels, own), BF16),
        vmem((channels, own), BF16),
        vmem((TAP_ROWS, region), F32),
        vmem((TAP_ROWS, region), F32),
        vmem((NMAX, 8, own), F32),
    ]
    full = pl.BlockSpec(memory_space=pltpu.VMEM)
    return pl.pallas_call(
        functools.partial(main_kernel, own=own, channels=channels, chips=chips),
        out_shape=out_shape,
        in_specs=[pl.BlockSpec(memory_space=pltpu.SMEM)] + [full] * 6,
        out_specs=[full] * 5,
        scratch_shapes=scratch,
        compiler_params=pltpu.CompilerParams(vmem_limit_bytes=63 * 1024 * 1024),
        name="flow_block",
    )(me, x0, x1, u2, u3, planes, small)


def assemble_kernel(index_ref, kinds_ref, p0_ref, p1_ref, small_ref, z_ref, gin_ref, logdet_ref, dens_s, *, own, chips, frames):
    me = index_ref[0]
    for m in range(chips):
        for b, ref in ((0, p0_ref), (1, p1_ref)):
            shard = jnp.bitwise_xor(me, 2 * m + b)
            lanes = pl.ds(pl.multiple_of(shard * own, LANES), own)
            piece = ref[m]
            z_ref[:, lanes] = piece[0:3]
            gin_ref[:, lanes] = piece[4:7]
            dens_s[:, lanes] = piece[3:4]
    scale_sum = small_ref[0, 0]
    pixel = iota((1, FRAME), 1)
    bottom = (pixel // (WIDTH * 32)) % 2
    right = (pixel // 32) % 2
    lane = iota((1, 4), 1)
    for f in range(frames):
        line = dens_s[:, f * FRAME : (f + 1) * FRAME]
        quads = jnp.zeros((1, 4), F32)
        total = jnp.zeros((1, 1), F32)
        for slot in range(4):
            picked = jnp.where(bottom * 2 + right == slot, line, 0.0)
            picked = jnp.sum(picked, axis=1, keepdims=True)
            quads = jnp.where(lane == slot, picked, quads)
            total = total + picked
        split = kinds_ref[f] == 2
        whole = jnp.where(lane == 0, total + 4096.0 * scale_sum, 0.0)
        logdet_ref[f : f + 1, :] = jnp.where(split, quads + 1024.0 * scale_sum, whole)


def norm_kernel(index_ref, a_ref, b_ref, pack_ref, cols_ref, rows_ref, grad_ref, out_ref, *, channels):
    grad = a_ref[...].astype(F32) + b_ref[...].astype(F32)
    grad_ref[...] = grad
    lane = iota((1, LANES), 1)
    is_one = lane_is_one(lane)
    is_three = lane_is_three(lane)
    tile = grad[:, channels:]
    weights = pack_ref[:, channels:]
    cols = cols_ref[...]
    u1 = cols[:, 0:1]
    v2 = cols[:, 1:2]
    spread = jnp.where((lane % 8 == 4) & (lane < TAP_ROWS), cols, 0.0)
    spread = spread + pltpu.roll(spread, 1, 1) + pltpu.roll(spread, 2, 1)
    outer_one = u1 * rows_ref[1:2, 0:LANES]
    outer_three = spread * rows_ref[2:3, 0:LANES]
    outer_two = v2 * rows_ref[0:1, :]
    grad_two = grad[:, 0:channels]
    weight_two = pack_ref[:, 0:channels]

    def total(values):
        return jnp.sum(jnp.sum(values, axis=0, keepdims=True), axis=1, keepdims=True)

    bias = (lane == TAP_ROWS) | (lane == TAP_ROWS + 1)
    parts = (
        total(jnp.where(is_one, tile * tile, 0.0)),
        total(grad_two * grad_two),
        total(jnp.where(is_three, tile * tile, 0.0)),
        total(jnp.where(is_one, tile * weights, 0.0)),
        total(grad_two * weight_two),
        total(jnp.where(is_three, tile * weights, 0.0)),
        total(jnp.where(is_one, tile * outer_one, 0.0)),
        total(grad_two * outer_two),
        total(jnp.where(is_three, tile * outer_three, 0.0)),
        total(jnp.where(is_one, outer_one * outer_one, 0.0)),
        total(outer_two * outer_two),
        total(jnp.where(is_three, outer_three * outer_three, 0.0)),
        total(jnp.where(bias, tile * tile, 0.0)),
    )
    row = jnp.zeros((1, LANES), F32)
    for index, part in enumerate(parts):
        row = jnp.where(lane == index, part, row)
    small = (lane >= TAP_ROWS + 2) & (lane < TAP_ROWS + 11) & (index_ref[0] == 0)
    row = jnp.where(small, tile[0:1], row)
    out_ref[...] = jnp.broadcast_to(row, out_ref.shape)


def moment_step(grad, moment, second):
    new_moment = BETA_ONE * moment + (1.0 - BETA_ONE) * grad
    new_second = BETA_TWO * second + (1.0 - BETA_TWO) * grad * grad
    return (new_moment, new_second)


def adam_step(param, grad, moment, second):
    new_moment, new_second = moment_step(grad, moment, second)
    fix_one = 1.0 - BETA_ONE**STEP
    fix_two = 1.0 - BETA_TWO**STEP
    update = new_moment / fix_one / (jnp.sqrt(new_second / fix_two) + ADAM_EPS) + DECAY * param
    return (param - LR_RATE * update, new_moment, new_second)


def update_kernel(
    totals_ref, grad_ref, cols_ref, rows_ref,
    w1_ref, m1_ref, s1_ref, w2_ref, m2_ref, s2_ref, w3_ref, m3_ref, s3_ref,
    mb_ref, sb_ref, small_ref, msmall_ref, ssmall_ref,
    norm_out, nw1, nm1, ns1, nw2, nm2, ns2, nw3, nm3, ns3, cb, nmb, nsb, nsm, nmsm, nssm, lw1, lw2, lw3,
    u1_out, v1_out, u2_out, v2_out, u3_out, v3_out, *, channels,
):
    lane = iota((1, LANES), 1)
    lines = [totals_ref[m : m + 1] for m in range(totals_ref.shape[0])]
    while len(lines) > 1:
        lines = [lines[m] + lines[m + 1] for m in range(0, len(lines), 2)]
    row = lines[0]

    def pick(index):
        return jnp.sum(jnp.where(lane == index, row, 0.0), axis=1, keepdims=True)

    sigmas = rows_ref[3:4, 0:LANES]
    small_row = jnp.where((lane >= TAP_ROWS + 2) & (lane < TAP_ROWS + 11), row, 0.0)
    square = pick(12) + jnp.sum(small_row * small_row, axis=1, keepdims=True)
    scales = []
    for j in range(3):
        sigma = sigmas[:, j : j + 1]
        ratio = SHRINK / sigma
        factor = pick(3 + j) / sigma
        fixed = pick(j) - 2.0 * factor * pick(6 + j) + factor * factor * pick(9 + j)
        square = square + ratio * ratio * jnp.maximum(fixed, 0.0)
        scales.append((ratio, factor))
    norm = jnp.sqrt(square)
    norm_out[...] = norm
    clip = jnp.minimum(1.0, CLIP_LIMIT / (norm + 1e-06))

    cols = cols_ref[...]
    grad = grad_ref[...]
    tile = grad[:, channels:]
    is_one = lane_is_one(lane)
    is_three = lane_is_three(lane)
    spread = jnp.where((lane % 8 == 4) & (lane < TAP_ROWS), cols, 0.0)
    spread = spread + pltpu.roll(spread, 1, 1) + pltpu.roll(spread, 2, 1)
    outer_one = cols[:, 0:1] * rows_ref[1:2, 0:LANES]
    outer_three = spread * rows_ref[2:3, 0:LANES]
    outer_two = cols[:, 1:2] * rows_ref[0:1, :]
    fixed_one = jnp.where(is_one, scales[0][0] * (tile - scales[0][1] * outer_one) * clip, 0.0)
    fixed_two = scales[1][0] * (grad[:, 0:channels] - scales[1][1] * outer_two) * clip
    fixed_three = jnp.where(is_three, scales[2][0] * (tile - scales[2][1] * outer_three) * clip, 0.0)
    grad_one = dot_nt(fixed_one, spread_one(), HIGH)
    grad_two = fixed_two.T
    grad_three = dot_nt(spread_three(), fixed_three, HIGH)

    for grad_j, w_ref, m_ref, s_ref, nw, nm, ns, lw in (
        (grad_one, w1_ref, m1_ref, s1_ref, nw1, nm1, ns1, lw1),
        (grad_two, w2_ref, m2_ref, s2_ref, nw2, nm2, ns2, lw2),
        (grad_three, w3_ref, m3_ref, s3_ref, nw3, nm3, ns3, lw3),
    ):
        new, moment, second = adam_step(w_ref[...], grad_j, m_ref[...], s_ref[...])
        nw[...] = new
        nm[...] = moment
        ns[...] = second
        lw[...] = new.astype(BF16)

    bias = (tile * clip).T[TAP_ROWS : TAP_ROWS + 2, :]
    cb[...] = bias
    moment, second = moment_step(bias, mb_ref[...], sb_ref[...])
    nmb[...] = moment
    nsb[...] = second

    small_row = small_row * clip
    lane3 = iota((1, 3), 1)
    rows = []
    for a in range(3):
        line = jnp.zeros((1, 3), F32)
        for i in range(3):
            at = TAP_ROWS + 2 + 3 * a + i
            line = jnp.where(lane3 == i, small_row[:, at : at + 1], line)
        rows.append(line)
    small_grad = jnp.concatenate(rows, axis=0)
    new, moment, second = adam_step(small_ref[...], small_grad, msmall_ref[...], ssmall_ref[...])
    nsm[...] = new
    nmsm[...] = moment
    nssm[...] = second

    flipped = cols.T
    u1_out[...] = flipped[0:1]
    v2_out[...] = flipped[1:2]
    tap = iota((9, LANES), 0)
    select = (iota((9, LANES), 1) == (8 - tap) * 8 + 4).astype(F32)
    v3_out[...] = dot_nn(select, flipped, HIGH)
    v1_out[...] = dot_nt(rows_ref[1:2, 0:LANES], spread_one(), HIGH)
    u2_out[...] = rows_ref[0:1, :]
    u3_out[...] = rows_ref[2:3, 4:7]


def window_planes(images, frame_kinds, series_len, probes, cot_z, cot_logdet, first, region):
    frames = frame_kinds.shape[0]
    pixels = images.shape[1]
    position = lax.iota(jnp.int32, pixels)
    kind = jnp.broadcast_to(frame_kinds[:, None], (frames, FRAME)).reshape(pixels)
    limit = jnp.where(kind == 1, 64, 32)
    row = (position // WIDTH) % limit
    col = position % limit

    def spread(values):
        quads = jnp.broadcast_to(values.reshape(-1, frames, 2, 1, 2, 1), (values.shape[0], frames, 2, 32, 2, 32))
        single = values[:, :, 0].reshape(-1, frames, 1, 1, 1, 1)
        picked = jnp.where(frame_kinds.reshape(1, frames, 1, 1, 1, 1) == 2, quads, single)
        return picked.reshape(values.shape[0], pixels)

    coefs = []
    for k in range(NMAX):
        term = (-1.0) ** k / (k + 1)
        coefs.append(jnp.where(series_len >= k + 1, term, 0.0).astype(F32))
    coefs = jnp.stack(coefs)
    coefs = spread(jnp.concatenate([coefs, coefs * cot_logdet[None]], axis=0))
    masks = jnp.stack([row > 0, row < limit - 1, col > 0, col < limit - 1]).astype(F32)
    blank1 = jnp.zeros((1, pixels), F32)
    blank4 = jnp.zeros((4, pixels), F32)
    planes = jnp.concatenate(
        [images, blank1, images, blank1, probes, blank1, probes, blank1, blank4, cot_z, blank1, coefs, masks, blank4],
        axis=0,
    )
    planes = jnp.pad(planes, ((0, 0), (HALO, HALO)))
    return lax.dynamic_slice_in_dim(planes, first, region, 1)


def local(
    images, frame_kinds, series_len, probes, cot_z, cot_logdet, weight1, weight2, weight3, biases,
    small_params, power_u1, power_u2, power_u3, moment_w1, second_w1, moment_w2, second_w2,
    moment_w3, second_w3, moment_bias, second_bias, moment_small, second_small,
):
    shards = lax.axis_size("chan")
    replicas = lax.axis_size("dp")
    chips = shards // 2
    me = lax.axis_index("chan")
    channels = weight2.shape[0]
    rows_own = weight1.shape[0]
    pixels = images.shape[1]
    frames = frame_kinds.shape[0]
    own = pixels // shards
    width = channels + LANES
    full = pl.BlockSpec(memory_space=pltpu.VMEM)
    smem = pl.BlockSpec(memory_space=pltpu.SMEM)
    index = me.reshape(1).astype(jnp.int32)

    def swap(values, axis, size, bits):
        return lax.ppermute(values, axis, [(j, j ^ bits) for j in range(size)])

    def gather_shards(values):
        pieces = [values] + [swap(values, "chan", shards, 2 * m) for m in range(1, chips)]
        first = jnp.stack(pieces)
        return first, swap(first, "chan", shards, 1)

    pack = pl.pallas_call(
        pack_kernel,
        out_shape=jax.ShapeDtypeStruct((rows_own, width), F32),
        in_specs=[full] * 5,
        out_specs=full,
        name="pack_weights",
    )(weight1, weight2, weight3, biases, power_u1.reshape(1, rows_own))
    x0, x1 = gather_shards(pack)

    u3_row = jnp.tile(jnp.concatenate([jnp.zeros((4,), F32), power_u3, jnp.zeros((1,), F32)]), LANES // 8)
    planes = window_planes(
        images, frame_kinds, series_len, probes, cot_z, cot_logdet, me * own, own + 2 * HALO
    )
    slots = lax.broadcasted_iota(jnp.int32, (frames, 4), 1)
    counts = jnp.where(frame_kinds[:, None] == 2, 1024.0, jnp.where(slots == 0, 4096.0, 0.0))
    extra = jnp.where(me == 0, jnp.sum(counts * cot_logdet), 0.0)
    columns = jnp.stack(
        [small_params[0], jnp.exp(small_params[1]), small_params[2], jnp.broadcast_to(extra, (3,))], axis=1
    )
    small = jnp.zeros((8, LANES), F32).at[0:3, 0:4].set(columns).at[4:7, 0:4].set(columns)

    keep, send, cols, rows, og = call_main(
        index, x0, x1, power_u2.reshape(1, channels), u3_row.reshape(1, LANES), planes, small, own, channels, chips
    )

    got = swap(send, "chan", shards, 1)
    summed = keep + got
    low = summed.astype(BF16)
    total = summed[0]
    for m in range(1, chips):
        total = total + swap(low[m], "chan", shards, 2 * m).astype(F32)
    half = total.astype(BF16)
    bits = 1
    while 2 * bits < replicas:
        half = (half.astype(F32) + swap(half, "dp", replicas, bits).astype(F32)).astype(BF16)
        bits *= 2
    other = swap(half, "dp", replicas, bits) if replicas > 1 else jnp.zeros_like(half)

    p0, p1 = gather_shards(og)
    z_out, grad_input, logdet = pl.pallas_call(
        functools.partial(assemble_kernel, own=own, chips=chips, frames=frames),
        out_shape=(
            jax.ShapeDtypeStruct((3, pixels), F32),
            jax.ShapeDtypeStruct((3, pixels), F32),
            jax.ShapeDtypeStruct((frames, 4), F32),
        ),
        in_specs=[smem, smem, full, full, smem],
        out_specs=[full] * 3,
        scratch_shapes=[pltpu.VMEM((1, pixels), F32)],
        name="assemble_outputs",
    )(index, frame_kinds, p0, p1, jnp.sum(small_params[1]).reshape(1, 1))

    cols_own = lax.dynamic_index_in_dim(cols, me, 0, False)
    grad, parts = pl.pallas_call(
        functools.partial(norm_kernel, channels=channels),
        out_shape=(
            jax.ShapeDtypeStruct((rows_own, width), F32),
            jax.ShapeDtypeStruct((8, LANES), F32),
        ),
        in_specs=[smem] + [full] * 5,
        out_specs=[full] * 2,
        name="norm_parts",
    )(index, half, other, pack, cols_own, rows)
    pair = parts + swap(parts, "chan", shards, 1)
    totals = [pair[0:1]] + [swap(pair, "chan", shards, 2 * m)[0:1] for m in range(1, chips)]
    totals = jnp.concatenate(totals, axis=0)

    def like(value, dtype=F32):
        return jax.ShapeDtypeStruct(value.shape, dtype)

    out_shape = (
        [jax.ShapeDtypeStruct((1, 1), F32)]
        + [like(weight1)] * 3
        + [like(weight2)] * 3
        + [like(weight3)] * 3
        + [like(biases)] * 3
        + [like(small_params)] * 3
        + [like(weight1, BF16), like(weight2, BF16), like(weight3, BF16)]
        + [jax.ShapeDtypeStruct((1, rows_own), F32), jax.ShapeDtypeStruct((1, 27), F32)]
        + [jax.ShapeDtypeStruct((1, channels), F32), jax.ShapeDtypeStruct((1, rows_own), F32)]
        + [jax.ShapeDtypeStruct((1, 3), F32), jax.ShapeDtypeStruct((9, rows_own), F32)]
    )
    done = pl.pallas_call(
        functools.partial(update_kernel, channels=channels),
        out_shape=out_shape,
        in_specs=[full] * 18,
        out_specs=[full] * len(out_shape),
        name="adam_update",
    )(
        totals, grad, cols_own, rows,
        weight1, moment_w1, second_w1, weight2, moment_w2, second_w2, weight3, moment_w3, second_w3,
        moment_bias, second_bias, small_params, moment_small, second_small,
    )
    norm, updates, vectors = done[0], done[1:19], done[19:]
    return (
        z_out,
        logdet,
        grad_input,
        norm.reshape(()),
        *updates,
        vectors[0].reshape(rows_own),
        vectors[1].reshape(27),
        vectors[2].reshape(channels),
        vectors[3].reshape(rows_own),
        vectors[4].reshape(3),
        vectors[5],
    )


def solution(mesh):
    chan_rows = P("chan", None)
    chan_cols = P(None, "chan")
    return jax.shard_map(
        local,
        mesh=mesh,
        in_specs=(
            P(None, "dp"), P("dp"), P("dp", None), P(None, "dp"), P(None, "dp"), P("dp", None),
            chan_rows, chan_cols, chan_cols, chan_cols, P(), P("chan"), P(), P(),
            chan_rows, chan_rows, chan_cols, chan_cols, chan_cols, chan_cols, chan_cols, chan_cols, P(), P(),
        ),
        out_specs=(
            P(None, "dp"), P("dp", None), P(None, "dp"), P(),
            chan_rows, chan_rows, chan_rows, chan_cols, chan_cols, chan_cols, chan_cols, chan_cols, chan_cols,
            chan_cols, chan_cols, chan_cols, P(), P(), P(), chan_rows, chan_cols, chan_cols,
            P("chan"), P(), P(), P("chan"), P(), chan_cols,
        ),
        check_vma=False,
    )
```

```python
import functools

import jax
import jax.numpy as jnp
from jax import lax
from jax.experimental import pallas as pl
from jax.experimental.pallas import tpu as pltpu
from jax.sharding import PartitionSpec as P

NMAX = 4
STEP = 7
SHRINK = 0.98
LR_RATE = 0.05
BETA_ONE = 0.5
BETA_TWO = 0.55
ADAM_EPS = 1e-08
DECAY = 0.01
CLIP_LIMIT = 1.0

WIDTH = 64
FRAME = 4096
BLOCK = 256
HALO = 2 * NMAX * WIDTH
LANES = 128
TAP_ROWS = 72
F32 = jnp.float32
BF16 = jnp.bfloat16
HIGH = lax.Precision.HIGHEST


def iota(shape, dim):
    return lax.broadcasted_iota(jnp.int32, shape, dim)


def dot_nn(left, right, precision=None):
    return lax.dot_general(
        left, right, (((1,), (0,)), ((), ())), precision=precision, preferred_element_type=F32
    )


def dot_nt(left, right, precision=None):
    return lax.dot_general(
        left, right, (((1,), (1,)), ((), ())), precision=precision, preferred_element_type=F32
    )


def dot_tn(left, right, precision=None):
    return lax.dot_general(
        left, right, (((0,), (0,)), ((), ())), precision=precision, preferred_element_type=F32
    )


def spread_one():
    row = iota((27, LANES), 0)
    return (iota((27, LANES), 1) == (row % 9) * 8 + row // 9).astype(F32)


def spread_three():
    row = iota((27, LANES), 0)
    return (iota((27, LANES), 1) == (8 - row % 9) * 8 + 4 + row // 9).astype(F32)


def lane_is_one(lane):
    return (lane % 8 < 3) & (lane < TAP_ROWS)


def lane_is_three(lane):
    return (lane % 8 >= 4) & (lane % 8 < 7) & (lane < TAP_ROWS)


def pack_kernel(w1_ref, w2_ref, w3_ref, bias_ref, u1_ref, out_ref):
    channels = w2_ref.shape[1]
    out_ref[:, 0:channels] = w2_ref[...]
    tile = dot_tn(w1_ref[...], spread_one(), HIGH) + dot_tn(w3_ref[...], spread_three(), HIGH)
    lane = iota((1, LANES), 1)
    for index, row in enumerate((u1_ref[...], bias_ref[0:1, :], bias_ref[1:2, :])):
        column = jnp.broadcast_to(row, (8, row.shape[1])).T[:, 0:1]
        tile = jnp.where(lane == TAP_ROWS + index, column, tile)
    out_ref[:, channels:] = tile


def col_taps(state, masks):
    size = state.shape[1]
    row_up, row_down, col_left, col_right = masks
    left = col_left * pltpu.roll(state, 1, 1)
    right = col_right * pltpu.roll(state, size - 1, 1)
    pieces = []
    for shift_y in (-1, 0, 1):
        for plane in (left, state, right):
            if shift_y == -1:
                plane = row_up * pltpu.roll(plane, WIDTH, 1)
            if shift_y == 1:
                plane = row_down * pltpu.roll(plane, size - WIDTH, 1)
            pieces.append(plane)
    return pieces


def comb_taps(q_ref, lanes, masks):
    size = lanes.size
    row_up, row_down, col_left, col_right = masks
    result = None
    for shift_y in (-1, 0, 1):
        base = 24 * (shift_y + 1)
        line = (
            col_left * pltpu.roll(q_ref[base : base + 8, lanes], 1, 1)
            + q_ref[base + 8 : base + 16, lanes]
            + col_right * pltpu.roll(q_ref[base + 16 : base + 24, lanes], size - 1, 1)
        )
        if shift_y == -1:
            line = row_up * pltpu.roll(line, WIDTH, 1)
        if shift_y == 1:
            line = row_down * pltpu.roll(line, size - WIDTH, 1)
        result = line if result is None else result + line
    return result


def normed_by(values, square):
    return values / jnp.sqrt(square + 1e-12)


def main_kernel(
    index_ref, u3_ref, x0_ref, x1_ref, u2_ref, planes_ref, small_ref,
    keep_ref, send_ref, cols_ref, rows_ref, og_ref,
    w_s, w13_s, w2_s, w2t_s, wout_s, bias_s, taps_s, sl1_s, sl2_s, cv1_s, cv2_s,
    lin1_s, lin2_s, gt1_s, gt2_s, acc1_s, acc2_s, tan1_s, tan2_s, g1_s, g2_s, hid1_s, hid2_s,
    q_s, q0_s, comb_s, *, own, channels, chips,
):
    me = index_ref[0]
    rows_own = channels // (2 * chips)
    region = own + 2 * HALO
    all_sum = functools.partial(jnp.sum, keepdims=True)

    for m in range(chips):
        for b, ref in ((0, x0_ref), (1, x1_ref)):
            w_s[jnp.bitwise_xor(me, 2 * m + b)] = ref[m]
    tile = w_s[:, :, channels:].reshape(channels, LANES)
    w2t = w_s[:, :, 0:channels].reshape(channels, channels)
    lane = iota((1, LANES), 1)
    is_one = lane_is_one(lane)
    is_three = lane_is_three(lane)
    taps_one = jnp.where(is_one, tile, 0.0)
    taps_three = jnp.where(is_three, tile, 0.0)
    head = (lane % 8 == 4) & (lane < TAP_ROWS)
    u1 = tile[:, TAP_ROWS : TAP_ROWS + 1]
    u2 = u2_ref[...]
    u3 = jnp.zeros((1, LANES), F32)
    for o in range(3):
        u3 = jnp.where(is_three & (lane % 8 == 4 + o), u3_ref[o], u3)
    for _ in range(2):
        v1 = all_sum(taps_one * u1, axis=0)
        v2 = all_sum(w2t * u2, axis=1)
        mixed = taps_three * u3
        mixed = mixed + pltpu.roll(mixed, LANES - 1, 1) + pltpu.roll(mixed, LANES - 2, 1)
        v3 = jnp.where(head, mixed, 0.0)
        v1 = normed_by(v1, all_sum(v1 * v1))
        v2 = normed_by(v2, all_sum(v2 * v2))
        v3 = normed_by(v3, all_sum(all_sum(v3 * v3, axis=0), axis=1))
        m1 = all_sum(taps_one * v1, axis=1)
        m2 = all_sum(w2t * v2, axis=0)
        spread = v3 + pltpu.roll(v3, 1, 1) + pltpu.roll(v3, 2, 1)
        m3 = all_sum(taps_three * spread, axis=0)
        for shift in (64, 32, 16, 8):
            m3 = m3 + pltpu.roll(m3, shift, 1)
        square1 = all_sum(m1 * m1)
        square2 = all_sum(m2 * m2)
        square3 = all_sum(jnp.where((lane >= 4) & (lane < 7), m3 * m3, 0.0))
        u1 = normed_by(m1, square1)
        u2 = normed_by(m2, square2)
        u3 = jnp.where(is_three, normed_by(m3, square3), 0.0)
    sigma1 = jnp.sqrt(square1)
    sigma2 = jnp.sqrt(square2)
    sigma3 = jnp.sqrt(square3)
    cols_ref[...] = jnp.where(lane == 0, u1, jnp.where(lane == 1, v2, v3)).reshape(cols_ref.shape)
    sigma_row = jnp.where(lane == 0, sigma1, jnp.where(lane == 1, sigma2, sigma3))
    rows_ref[...] = jnp.zeros(rows_ref.shape, F32)
    rows_ref[0:1, :] = u2
    rows_ref[1:2, 0:LANES] = v1
    rows_ref[2:3, 0:LANES] = u3
    rows_ref[3:4, 0:LANES] = sigma_row

    scaled = taps_one * (SHRINK / sigma1) + taps_three * (SHRINK / sigma3)
    w13_s[0:channels] = jnp.where(is_one, scaled, 0.0).astype(BF16)
    w13_s[channels:] = jnp.where(is_three, scaled, 0.0).astype(BF16)
    flipped = scaled.T
    blocks = [pltpu.roll(flipped[(8 - t) * 8 : (9 - t) * 8], 4, 0) for t in range(9)]
    flipped = jnp.concatenate(blocks + [jnp.zeros((8, channels), F32)], axis=0)
    first_rows = iota((TAP_ROWS + 8, 1), 0) % 8 < 4
    wout_s[:, 0:channels] = jnp.where(first_rows, flipped, 0.0).astype(BF16)
    wout_s[:, channels:] = jnp.where(first_rows, 0.0, flipped).astype(BF16)
    w2t_scaled = w2t * (SHRINK / sigma2)
    w2t_s[...] = w2t_scaled.astype(BF16)
    w2_s[...] = w2t_scaled.T.astype(BF16)
    for layer in range(2):
        column = tile[:, TAP_ROWS + 1 + layer : TAP_ROWS + 2 + layer]
        bias_s[layer] = jnp.broadcast_to(column, (channels, LANES))

    shift8 = small_ref[:, 0:1]
    scale8 = small_ref[:, 1:2]
    bias8 = small_ref[:, 2:3]
    extra8 = small_ref[:, 3:4]
    upper = iota((8, 1), 0) >= 4
    probes8 = planes_ref[8:16]
    cot8 = planes_ref[16:24]

    def masks_at(lanes):
        return [planes_ref[32 + i : 33 + i, lanes] for i in range(4)]

    def put_taps(slot, pieces, lanes):
        taps_s[slot, 0 : TAP_ROWS + 8, lanes] = jnp.concatenate(
            pieces + [jnp.zeros((8, lanes.size), F32)], axis=0
        ).astype(BF16)
        taps_s[slot, TAP_ROWS + 8 :, lanes] = jnp.zeros((LANES - TAP_ROWS - 8, lanes.size), BF16)

    whole = pl.ds(0, region)
    h8 = (planes_ref[0:8] + shift8) * scale8
    sig8 = 0.5 + 0.5 * jnp.tanh(0.5 * h8)
    rest8 = 1.0 - sig8
    slope0 = (sig8 + h8 * sig8 * rest8) / 1.1
    curve0 = sig8 * rest8 * (2.0 + h8 * (1.0 - 2.0 * sig8)) / 1.1
    state = jnp.where(upper, cot8, h8 * sig8 / 1.1)
    put_taps(0, col_taps(state, masks_at(whole)), whole)
    state = probes8 * jnp.where(upper, planes_ref[24 + 7 : 24 + 8], slope0)
    put_taps(1, col_taps(state, masks_at(whole)), whole)

    def activation(act, slope_ref, curve_ref, lanes, curve_lanes, in_curve):
        half = 0.5 * jnp.tanh(0.5 * act)
        sig = 0.5 + half
        rest = 0.5 - half
        hidden = act * sig * (1.0 / 1.1)
        slope_ref[:, lanes] = sig * (1.0 / 1.1) + hidden * rest
        sig2 = sig * (2.0 / 1.1)

        @pl.when(in_curve)
        def _():
            curve_ref[:, curve_lanes] = (rest * (sig2 - 2.0 * half * hidden)).astype(BF16)

        return hidden.astype(BF16)

    own_blocks = own // BLOCK

    def start_body(j, carry):
        lanes = pl.ds(pl.multiple_of(j * BLOCK, LANES), BLOCK)
        in_curve = (j >= 1) & (j < own_blocks + 3)
        curve_lanes = pl.ds(pl.multiple_of(jnp.clip(j - 1, 0, own_blocks + 1) * BLOCK, LANES), BLOCK)
        taps = taps_s[0, :, lanes]
        act1 = dot_nn(w13_s[0:channels], taps)
        bias1 = bias_s[0]
        hidden1 = activation(
            act1 + jnp.concatenate([bias1, bias1], axis=1), sl1_s, cv1_s, lanes, curve_lanes, in_curve
        )
        act2 = dot_nn(w2_s[...], hidden1)
        bias2 = bias_s[1]
        hidden2 = activation(
            act2 + jnp.concatenate([bias2, bias2], axis=1), sl2_s, cv2_s, lanes, curve_lanes, in_curve
        )
        q0_s[:, lanes] = dot_nn(wout_s[:, 0:channels], hidden2)[0:TAP_ROWS]

        @pl.when((j >= 2) & (j < own_blocks + 2))
        def _():
            own_lanes = pl.ds(pl.multiple_of((j - 2) * BLOCK, LANES), BLOCK)
            hid1_s[:, own_lanes] = hidden1
            hid2_s[:, own_lanes] = hidden2

        return carry

    lax.fori_loop(0, own_blocks + 4, start_body, 0)

    own_in_slot = pl.ds(LANES, own)

    def series_stage(stage):
        offset = LANES * (stage - 1)
        count = own_blocks + 5 - stage
        tan_slot = min(stage, 3) - 1
        aligned = stage % 2 == 1
        store_from = (HALO - offset) // BLOCK if aligned else (HALO - LANES - offset) // BLOCK
        store_count = own_blocks if aligned else own_blocks + 1

        def body(j, carry):
            start = pl.multiple_of(offset + j * BLOCK, LANES)
            lanes = pl.ds(start, BLOCK)
            both = dot_nn(w13_s[...], taps_s[stage, :, lanes])
            lin1 = both[0:channels]
            gt2 = both[channels:]
            slope1 = sl1_s[:, lanes]
            slope2 = sl2_s[:, lanes]
            tan1 = (slope1 * lin1).astype(BF16)
            g2 = (slope2 * gt2).astype(BF16)
            lin2 = dot_nn(w2_s[...], tan1)
            gt1 = dot_nn(w2t_s[...], g2)
            tan2 = (slope2 * lin2).astype(BF16)
            g1 = (slope1 * gt1).astype(BF16)
            q_s[:, lanes] = dot_nn(wout_s[...], jnp.concatenate([tan2, g1], axis=0))[0:TAP_ROWS]

            @pl.when((j >= store_from) & (j < store_from + store_count))
            def _():
                slot_lanes = pl.ds(pl.multiple_of(start - (HALO - LANES), LANES), BLOCK)
                tan1_s[tan_slot, :, slot_lanes] = tan1
                tan2_s[tan_slot, :, slot_lanes] = tan2
                g1_s[tan_slot, :, slot_lanes] = g1
                g2_s[tan_slot, :, slot_lanes] = g2

            wide_lanes = pl.ds(pl.multiple_of(jnp.maximum(start - BLOCK, 0), LANES), BLOCK)
            if stage <= 2:
                wide_count = own_blocks + 3 - stage

                @pl.when((j >= 1) & (j < 1 + wide_count))
                def _():
                    lin1_s[stage - 1, :, wide_lanes] = lin1.astype(BF16)
                    lin2_s[stage - 1, :, wide_lanes] = lin2.astype(BF16)
                    gt1_s[stage - 1, :, wide_lanes] = gt1.astype(BF16)
                    gt2_s[stage - 1, :, wide_lanes] = gt2.astype(BF16)
            else:
                slot = 4 - stage
                for acc_ref, lin_ref, gt_ref, lin, gt in (
                    (acc1_s, lin1_s, gt1_s, lin1, gt1),
                    (acc2_s, lin2_s, gt2_s, lin2, gt2),
                ):
                    total = lin * gt_ref[slot, :, wide_lanes].astype(F32)
                    total = total + gt * lin_ref[slot, :, wide_lanes].astype(F32)
                    if stage == 4:
                        total = total + acc_ref[:, wide_lanes]
                    acc_ref[:, wide_lanes] = total
            return carry

        lax.fori_loop(0, count, body, 0)

        inside = pl.ds(offset, count * BLOCK)
        result = comb_taps(q_s, inside, masks_at(inside))
        core_from = HALO - offset
        comb_s[stage - 1] = result[:, core_from : core_from + own]
        if stage < NMAX:
            nxt = result[:, LANES : count * BLOCK - LANES]
            lanes = pl.ds(offset + LANES, (count - 1) * BLOCK)
            seed = probes8[:, offset + LANES : offset + LANES + (count - 1) * BLOCK]
            coef = planes_ref[24 + 4 + 3 - stage : 24 + 4 + 4 - stage, lanes]
            following = slope0[:, offset + LANES : offset + LANES + (count - 1) * BLOCK] * nxt
            following = following + jnp.where(upper, seed * coef, 0.0)
            put_taps(stage + 1, col_taps(following, masks_at(lanes)), lanes)

    def own_taps(slot):
        return taps_s[slot, :, pl.ds(HALO, own)]

    def add_weight_grads(slot_pairs, tap_pairs, first):
        total = None
        for left, right in slot_pairs:
            part = dot_nt(left, right)
            total = part if total is None else total + part
        one = None
        three = None
        for left_one, left_three, slot in tap_pairs:
            part_one = dot_nt(left_one, own_taps(slot))
            part_three = dot_nt(left_three, own_taps(slot))
            one = part_one if one is None else one + part_one
            three = part_three if three is None else three + part_three
        tile_part = jnp.where(is_one, one, jnp.where(is_three, three, 0.0))
        w2_part = total.reshape(2 * chips, rows_own, channels)
        tile_part = tile_part.reshape(2 * chips, rows_own, LANES)
        if first:
            w_s[:, :, 0:channels] = w2_part
            w_s[:, :, channels:] = tile_part
        else:
            w_s[:, :, 0:channels] = w_s[:, :, 0:channels] + w2_part
            w_s[:, :, channels:] = w_s[:, :, channels:] + tile_part

    def slot_of(ref, slot):
        return ref[slot, :, own_in_slot]

    series_stage(1)
    series_stage(2)
    series_stage(3)
    add_weight_grads(
        ((slot_of(tan1_s, 1), slot_of(g2_s, 2)), (slot_of(tan1_s, 2), slot_of(g2_s, 1))),
        (
            (slot_of(g1_s, 2), slot_of(tan2_s, 2), 2),
            (slot_of(g1_s, 1), slot_of(tan2_s, 1), 3),
        ),
        True,
    )
    series_stage(4)
    add_weight_grads(
        ((slot_of(tan1_s, 0), slot_of(g2_s, 2)), (slot_of(tan1_s, 2), slot_of(g2_s, 0))),
        (
            (slot_of(g1_s, 2), slot_of(tan2_s, 2), 1),
            (slot_of(g1_s, 0), slot_of(tan2_s, 0), 4),
        ),
        False,
    )

    def final_body(j, carry):
        bias_one, bias_two = carry
        start = pl.multiple_of(HALO - LANES + j * BLOCK, LANES)
        lanes = pl.ds(start, BLOCK)
        wide_lanes = pl.ds(pl.multiple_of(LANES + j * BLOCK, LANES), BLOCK)
        slot_lanes = pl.ds(pl.multiple_of(j * BLOCK, LANES), BLOCK)
        low_lanes = (j > 0).astype(F32)
        high_lanes = (j < own_blocks).astype(F32)
        gs2 = dot_nn(w13_s[channels:], taps_s[0, :, lanes])
        ga2 = cv2_s[:, wide_lanes].astype(F32) * acc2_s[:, wide_lanes] + sl2_s[:, lanes] * gs2
        low2 = ga2.astype(BF16)
        gs1 = dot_nn(w2t_s[...], low2)
        ga1 = cv1_s[:, wide_lanes].astype(F32) * acc1_s[:, wide_lanes] + sl1_s[:, lanes] * gs1
        low1 = ga1.astype(BF16)
        q_s[:, lanes] = q0_s[:, lanes] + dot_nn(wout_s[:, channels:], low1)[0:TAP_ROWS]
        g2_s[0, :, slot_lanes] = low2
        g1_s[0, :, slot_lanes] = low1
        bias_one = bias_one + low_lanes * ga1[:, 0:LANES] + high_lanes * ga1[:, LANES:]
        bias_two = bias_two + low_lanes * ga2[:, 0:LANES] + high_lanes * ga2[:, LANES:]
        return bias_one, bias_two

    zero = jnp.zeros((channels, LANES), F32)
    bias_one, bias_two = lax.fori_loop(0, own_blocks + 1, final_body, (zero, zero))
    add_weight_grads(
        ((hid1_s[...], slot_of(g2_s, 0)),), ((slot_of(g1_s, 0), hid2_s[...], 0),), False
    )

    inside = pl.ds(HALO - LANES, own + BLOCK)
    result = comb_taps(q_s, inside, masks_at(inside))[:, LANES : LANES + own]
    mine = slice(HALO, HALO + own)
    h_own = h8[:, mine]
    cot_own = cot8[:, mine]
    probes_own = probes8[:, mine]
    mixed = comb_s[0] * pltpu.roll(comb_s[2], 4, 0)
    mixed = mixed + comb_s[1] * pltpu.roll(comb_s[1], 4, 0)
    mixed = mixed + comb_s[2] * pltpu.roll(comb_s[0], 4, 0)
    mixed = mixed + comb_s[3] * probes_own
    grad_h = cot_own + slope0[:, mine] * result + curve0[:, mine] * mixed
    grad_in = grad_h * scale8
    density = planes_ref[24:25, mine] * comb_s[0]
    for k in range(1, NMAX):
        density = density + planes_ref[24 + k : 25 + k, mine] * comb_s[k]
    density = density * probes_own
    density = density[0:1] + density[1:2] + density[2:3]
    row8 = iota((8, 1), 0)
    out = jnp.where(row8 < 3, h_own + result + bias8, jnp.where(row8 == 3, density, grad_in))
    og_ref[...] = jnp.where(row8 < 7, out, 0.0)

    sums = (
        all_sum(grad_in, axis=1),
        all_sum(grad_h * h_own, axis=1) + extra8,
        all_sum(cot_own, axis=1),
    )
    small_row = jnp.zeros((1, LANES), F32)
    for a, column in enumerate(sums):
        for i in range(3):
            small_row = jnp.where(lane == TAP_ROWS + 2 + 3 * a + i, column[4 + i : 5 + i], small_row)
    bias_one = all_sum(bias_one, axis=1)
    bias_two = all_sum(bias_two, axis=1)
    extras = jnp.where(lane == TAP_ROWS, bias_one, jnp.where(lane == TAP_ROWS + 1, bias_two, small_row))
    extras = extras.reshape(2 * chips, rows_own, LANES)
    w_s[:, :, channels:] = w_s[:, :, channels:] + extras

    core = jnp.bitwise_and(me, 1)
    chip = jnp.right_shift(me, 1)
    for m in range(chips):
        block = 2 * jnp.bitwise_xor(chip, m)
        keep_ref[m] = w_s[block + core]
        send_ref[m] = w_s[block + 1 - core]


def call_main(me, u3, x0, x1, u2, planes, small, own, channels, chips):
    rows_own = channels // (2 * chips)
    region = own + 2 * HALO
    wide = own + 2 * BLOCK
    slot = own + BLOCK
    width = channels + LANES
    out_shape = (
        jax.ShapeDtypeStruct((chips, rows_own, width), F32),
        jax.ShapeDtypeStruct((chips, rows_own, width), F32),
        jax.ShapeDtypeStruct((2 * chips, rows_own, LANES), F32),
        jax.ShapeDtypeStruct((8, channels), F32),
        jax.ShapeDtypeStruct((8, own), F32),
    )
    vmem = pltpu.VMEM
    scratch = [
        vmem((2 * chips, rows_own, width), F32),
        vmem((2 * channels, LANES), BF16),
        vmem((channels, channels), BF16),
        vmem((channels, channels), BF16),
        vmem((TAP_ROWS + 8, 2 * channels), BF16),
        vmem((2, channels, LANES), F32),
        vmem((NMAX + 1, LANES, region), BF16),
        vmem((channels, region), F32),
        vmem((channels, region), F32),
        vmem((channels, wide), BF16),
        vmem((channels, wide), BF16),
        vmem((2, channels, wide), BF16),
        vmem((2, channels, wide), BF16),
        vmem((2, channels, wide), BF16),
        vmem((2, channels, wide), BF16),
        vmem((channels, wide), F32),
        vmem((channels, wide), F32),
        vmem((3, channels, slot), BF16),
        vmem((3, channels, slot), BF16),
        vmem((3, channels, slot), BF16),
        vmem((3, channels, slot), BF16),
        vmem((channels, own), BF16),
        vmem((channels, own), BF16),
        vmem((TAP_ROWS, region), F32),
        vmem((TAP_ROWS, region), F32),
        vmem((NMAX, 8, own), F32),
    ]
    full = pl.BlockSpec(memory_space=pltpu.VMEM)
    return pl.pallas_call(
        functools.partial(main_kernel, own=own, channels=channels, chips=chips),
        out_shape=out_shape,
        in_specs=[pl.BlockSpec(memory_space=pltpu.SMEM)] * 2 + [full] * 5,
        out_specs=[full] * 5,
        scratch_shapes=scratch,
        compiler_params=pltpu.CompilerParams(vmem_limit_bytes=63 * 1024 * 1024),
        name="flow_block",
    )(me, u3, x0, x1, u2, planes, small)


def assemble_kernel(index_ref, kinds_ref, p0_ref, p1_ref, small_ref, z_ref, gin_ref, logdet_ref, dens_s, *, own, chips, frames):
    me = index_ref[0]
    for m in range(chips):
        for b, ref in ((0, p0_ref), (1, p1_ref)):
            shard = jnp.bitwise_xor(me, 2 * m + b)
            lanes = pl.ds(pl.multiple_of(shard * own, LANES), own)
            piece = ref[m]
            z_ref[:, lanes] = piece[0:3]
            gin_ref[:, lanes] = piece[4:7]
            dens_s[:, lanes] = piece[3:4]
    scale_sum = small_ref[1, 0] + small_ref[1, 1] + small_ref[1, 2]
    pixel = iota((1, FRAME), 1)
    bottom = (pixel // (WIDTH * 32)) % 2
    right = (pixel // 32) % 2
    lane = iota((1, 4), 1)
    for f in range(frames):
        line = dens_s[:, f * FRAME : (f + 1) * FRAME]
        quads = jnp.zeros((1, 4), F32)
        total = jnp.zeros((1, 1), F32)
        for slot in range(4):
            picked = jnp.where(bottom * 2 + right == slot, line, 0.0)
            picked = jnp.sum(picked, axis=1, keepdims=True)
            quads = jnp.where(lane == slot, picked, quads)
            total = total + picked
        split = kinds_ref[f] == 2
        whole = jnp.where(lane == 0, total + 4096.0 * scale_sum, 0.0)
        logdet_ref[f : f + 1, :] = jnp.where(split, quads + 1024.0 * scale_sum, whole)


def norm_kernel(index_ref, a_ref, b_ref, pack_ref, cols_ref, rows_ref, grad_ref, out_ref, *, channels):
    grad = a_ref[...].astype(F32) + b_ref[...].astype(F32)
    grad_ref[...] = grad
    lane = iota((1, LANES), 1)
    is_one = lane_is_one(lane)
    is_three = lane_is_three(lane)
    tile = grad[:, channels:]
    weights = pack_ref[:, channels:]
    cols = cols_ref[...]
    u1 = cols[:, 0:1]
    v2 = cols[:, 1:2]
    spread = jnp.where((lane % 8 == 4) & (lane < TAP_ROWS), cols, 0.0)
    spread = spread + pltpu.roll(spread, 1, 1) + pltpu.roll(spread, 2, 1)
    outer_one = u1 * rows_ref[1:2, 0:LANES]
    outer_three = spread * rows_ref[2:3, 0:LANES]
    outer_two = v2 * rows_ref[0:1, :]
    grad_two = grad[:, 0:channels]
    weight_two = pack_ref[:, 0:channels]

    def total(values):
        return jnp.sum(jnp.sum(values, axis=0, keepdims=True), axis=1, keepdims=True)

    bias = (lane == TAP_ROWS) | (lane == TAP_ROWS + 1)
    parts = (
        total(jnp.where(is_one, tile * tile, 0.0)),
        total(grad_two * grad_two),
        total(jnp.where(is_three, tile * tile, 0.0)),
        total(jnp.where(is_one, tile * weights, 0.0)),
        total(grad_two * weight_two),
        total(jnp.where(is_three, tile * weights, 0.0)),
        total(jnp.where(is_one, tile * outer_one, 0.0)),
        total(grad_two * outer_two),
        total(jnp.where(is_three, tile * outer_three, 0.0)),
        total(jnp.where(is_one, outer_one * outer_one, 0.0)),
        total(outer_two * outer_two),
        total(jnp.where(is_three, outer_three * outer_three, 0.0)),
        total(jnp.where(bias, tile * tile, 0.0)),
    )
    row = jnp.zeros((1, LANES), F32)
    for index, part in enumerate(parts):
        row = jnp.where(lane == index, part, row)
    small = (lane >= TAP_ROWS + 2) & (lane < TAP_ROWS + 11) & (index_ref[0] == 0)
    row = jnp.where(small, tile[0:1], row)
    out_ref[...] = jnp.broadcast_to(row, out_ref.shape)


def moment_step(grad, moment, second):
    new_moment = BETA_ONE * moment + (1.0 - BETA_ONE) * grad
    new_second = BETA_TWO * second + (1.0 - BETA_TWO) * grad * grad
    return (new_moment, new_second)


def adam_step(param, grad, moment, second):
    new_moment, new_second = moment_step(grad, moment, second)
    fix_one = 1.0 - BETA_ONE**STEP
    fix_two = 1.0 - BETA_TWO**STEP
    update = new_moment / fix_one / (jnp.sqrt(new_second / fix_two) + ADAM_EPS) + DECAY * param
    return (param - LR_RATE * update, new_moment, new_second)


def update_kernel(
    totals_ref, grad_ref, cols_ref, rows_ref,
    w1_ref, m1_ref, s1_ref, w2_ref, m2_ref, s2_ref, w3_ref, m3_ref, s3_ref,
    mb_ref, sb_ref, small_ref, msmall_ref, ssmall_ref,
    norm_out, nw1, nm1, ns1, nw2, nm2, ns2, nw3, nm3, ns3, cb, nmb, nsb, nsm, nmsm, nssm, lw1, lw2, lw3,
    u1_out, v1_out, u2_out, v2_out, u3_out, v3_out, *, channels,
):
    lane = iota((1, LANES), 1)
    lines = [totals_ref[m : m + 1] for m in range(totals_ref.shape[0])]
    while len(lines) > 1:
        lines = [lines[m] + lines[m + 1] for m in range(0, len(lines), 2)]
    row = lines[0]

    def pick(index):
        return jnp.sum(jnp.where(lane == index, row, 0.0), axis=1, keepdims=True)

    sigmas = rows_ref[3:4, 0:LANES]
    small_row = jnp.where((lane >= TAP_ROWS + 2) & (lane < TAP_ROWS + 11), row, 0.0)
    square = pick(12) + jnp.sum(small_row * small_row, axis=1, keepdims=True)
    scales = []
    for j in range(3):
        sigma = sigmas[:, j : j + 1]
        ratio = SHRINK / sigma
        factor = pick(3 + j) / sigma
        fixed = pick(j) - 2.0 * factor * pick(6 + j) + factor * factor * pick(9 + j)
        square = square + ratio * ratio * jnp.maximum(fixed, 0.0)
        scales.append((ratio, factor))
    norm = jnp.sqrt(square)
    norm_out[...] = norm
    clip = jnp.minimum(1.0, CLIP_LIMIT / (norm + 1e-06))

    cols = cols_ref[...]
    grad = grad_ref[...]
    tile = grad[:, channels:]
    is_one = lane_is_one(lane)
    is_three = lane_is_three(lane)
    spread = jnp.where((lane % 8 == 4) & (lane < TAP_ROWS), cols, 0.0)
    spread = spread + pltpu.roll(spread, 1, 1) + pltpu.roll(spread, 2, 1)
    outer_one = cols[:, 0:1] * rows_ref[1:2, 0:LANES]
    outer_three = spread * rows_ref[2:3, 0:LANES]
    outer_two = cols[:, 1:2] * rows_ref[0:1, :]
    fixed_one = jnp.where(is_one, scales[0][0] * (tile - scales[0][1] * outer_one) * clip, 0.0)
    fixed_two = scales[1][0] * (grad[:, 0:channels] - scales[1][1] * outer_two) * clip
    fixed_three = jnp.where(is_three, scales[2][0] * (tile - scales[2][1] * outer_three) * clip, 0.0)
    grad_one = dot_nt(spread_one(), fixed_one, HIGH)
    grad_two = fixed_two
    grad_three = dot_nt(spread_three(), fixed_three, HIGH)

    for grad_j, w_ref, m_ref, s_ref, nw, nm, ns, lw in (
        (grad_one, w1_ref, m1_ref, s1_ref, nw1, nm1, ns1, lw1),
        (grad_two, w2_ref, m2_ref, s2_ref, nw2, nm2, ns2, lw2),
        (grad_three, w3_ref, m3_ref, s3_ref, nw3, nm3, ns3, lw3),
    ):
        new, moment, second = adam_step(w_ref[...], grad_j, m_ref[...], s_ref[...])
        nw[...] = new
        nm[...] = moment
        ns[...] = second
        lw[...] = new.astype(BF16)

    bias = (tile * clip).T[TAP_ROWS : TAP_ROWS + 2, :]
    cb[...] = bias
    moment, second = moment_step(bias, mb_ref[...], sb_ref[...])
    nmb[...] = moment
    nsb[...] = second

    small_row = small_row * clip
    lane3 = iota((1, 3), 1)
    rows = []
    for a in range(3):
        line = jnp.zeros((1, 3), F32)
        for i in range(3):
            at = TAP_ROWS + 2 + 3 * a + i
            line = jnp.where(lane3 == i, small_row[:, at : at + 1], line)
        rows.append(line)
    small_grad = jnp.concatenate(rows, axis=0)
    new, moment, second = adam_step(small_ref[...], small_grad, msmall_ref[...], ssmall_ref[...])
    nsm[...] = new
    nmsm[...] = moment
    nssm[...] = second

    flipped = cols.T
    u1_out[...] = flipped[0:1]
    v2_out[...] = flipped[1:2]
    tap = iota((9, LANES), 0)
    select = (iota((9, LANES), 1) == (8 - tap) * 8 + 4).astype(F32)
    v3_out[...] = dot_nn(select, flipped, HIGH)
    v1_out[...] = dot_nt(rows_ref[1:2, 0:LANES], spread_one(), HIGH)
    u2_out[...] = rows_ref[0:1, :]
    u3_out[...] = rows_ref[2:3, 4:7]


def prepare_kernel(
    index_ref, kinds_ref, len_ref, cot_ref, params_ref, images_ref, probes_ref, cot_z_ref,
    planes_ref, small_ref, *, own, frames,
):
    region = planes_ref.shape[1]
    pixels = images_ref.shape[1]
    me = index_ref[0]
    first = me * own - HALO
    planes_ref[...] = jnp.zeros(planes_ref.shape, F32)
    for chunk in range(region // LANES):
        start = first + chunk * LANES
        source = pl.ds(pl.multiple_of(jnp.clip(start, 0, pixels - LANES), LANES), LANES)
        lanes = pl.ds(chunk * LANES, LANES)
        inside = (start >= 0) & (start < pixels)
        for row, ref in ((0, images_ref), (4, images_ref), (8, probes_ref), (12, probes_ref), (20, cot_z_ref)):
            planes_ref[row : row + 3, lanes] = jnp.where(inside, ref[:, source], 0.0)

    position = first + iota((1, region), 1)
    frame = jnp.right_shift(position, 12)
    pixel = jnp.bitwise_and(position, FRAME - 1)
    row = jnp.right_shift(pixel, 6)
    col = jnp.bitwise_and(pixel, WIDTH - 1)
    half = WIDTH // 2
    quad = 2 * jnp.right_shift(row, 5) + jnp.right_shift(col, 5)
    split = jnp.zeros((1, region), jnp.int32)
    for f in range(frames):
        split = jnp.where(frame == f, jnp.where(kinds_ref[f] == 2, 1, 0), split)
    slot = 4 * frame + jnp.where(split == 1, quad, 0)
    length = jnp.zeros((1, region), jnp.int32)
    weight = jnp.zeros((1, region), F32)
    for f in range(frames):
        for q in range(4):
            here = slot == 4 * f + q
            length = jnp.where(here, len_ref[f, q], length)
            weight = jnp.where(here, cot_ref[f, q], weight)
    for k in range(NMAX):
        coef = jnp.where(length >= k + 1, (-1.0) ** k / (k + 1), 0.0)
        planes_ref[24 + k : 25 + k] = coef
        planes_ref[24 + NMAX + k : 25 + NMAX + k] = coef * weight
    for index, line in enumerate((row, col)):
        low = (line == 0) | ((split == 1) & (line == half))
        high = (line == WIDTH - 1) | ((split == 1) & (line == half - 1))
        planes_ref[32 + 2 * index : 33 + 2 * index] = jnp.where(low, 0.0, 1.0)
        planes_ref[33 + 2 * index : 34 + 2 * index] = jnp.where(high, 0.0, 1.0)

    extra = jnp.float32(0.0)
    for f in range(frames):
        whole = 4096.0 * cot_ref[f, 0]
        quads = 1024.0 * (cot_ref[f, 0] + cot_ref[f, 1] + cot_ref[f, 2] + cot_ref[f, 3])
        extra = extra + jnp.where(kinds_ref[f] == 2, quads, whole)
    extra = jnp.where(me == 0, extra, 0.0)
    row8 = iota((8, LANES), 0)
    lane = iota((8, LANES), 1)
    values = []
    for a in range(3):
        value = jnp.zeros((8, LANES), F32)
        for i in range(3):
            value = jnp.where(row8 % 4 == i, params_ref[a, i], value)
        values.append(value)
    result = jnp.where(lane == 0, values[0], jnp.where(lane == 1, jnp.exp(values[1]), values[2]))
    small_ref[...] = jnp.where(row8 % 4 == 3, 0.0, jnp.where(lane == 3, extra, result))


def local(
    images, frame_kinds, series_len, probes, cot_z, cot_logdet, weight1, weight2, weight3, biases,
    small_params, power_u1, power_u2, power_u3, moment_w1, second_w1, moment_w2, second_w2,
    moment_w3, second_w3, moment_bias, second_bias, moment_small, second_small,
):
    shards = lax.axis_size("chan")
    replicas = lax.axis_size("dp")
    chips = shards // 2
    me = lax.axis_index("chan")
    channels = weight2.shape[0]
    rows_own = weight1.shape[0]
    pixels = images.shape[1]
    frames = frame_kinds.shape[0]
    own = pixels // shards
    width = channels + LANES
    full = pl.BlockSpec(memory_space=pltpu.VMEM)
    smem = pl.BlockSpec(memory_space=pltpu.SMEM)
    index = me.reshape(1).astype(jnp.int32)

    def swap(values, axis, size, bits):
        return lax.ppermute(values, axis, [(j, j ^ bits) for j in range(size)])

    def gather_shards(values):
        pieces = [values] + [swap(values, "chan", shards, 2 * m) for m in range(1, chips)]
        first = jnp.stack(pieces)
        return first, swap(first, "chan", shards, 1)

    pack = pl.pallas_call(
        pack_kernel,
        out_shape=jax.ShapeDtypeStruct((rows_own, width), F32),
        in_specs=[full] * 5,
        out_specs=full,
        name="pack_weights",
    )(weight1.T, weight2.T, weight3, biases, power_u1.reshape(1, rows_own))
    x0, x1 = gather_shards(pack)

    planes, small = pl.pallas_call(
        functools.partial(prepare_kernel, own=own, frames=frames),
        out_shape=(
            jax.ShapeDtypeStruct((40, own + 2 * HALO), F32),
            jax.ShapeDtypeStruct((8, LANES), F32),
        ),
        in_specs=[smem] * 5 + [full] * 3,
        out_specs=[full] * 2,
        name="prepare_planes",
    )(index, frame_kinds, series_len, cot_logdet, small_params, images, probes, cot_z)

    keep, send, cols, rows, og = call_main(
        index, power_u3, x0, x1, power_u2.reshape(1, channels), planes, small, own, channels, chips
    )

    got = swap(send, "chan", shards, 1)
    summed = keep + got
    low = summed.astype(BF16)
    total = summed[0]
    for m in range(1, chips):
        total = total + swap(low[m], "chan", shards, 2 * m).astype(F32)
    og, half = lax.optimization_barrier((og, total.astype(BF16)))
    bits = 1
    while 2 * bits < replicas:
        half = (half.astype(F32) + swap(half, "dp", replicas, bits).astype(F32)).astype(BF16)
        bits *= 2
    other = swap(half, "dp", replicas, bits) if replicas > 1 else jnp.zeros_like(half)

    p0, p1 = gather_shards(og)
    z_out, grad_input, logdet = pl.pallas_call(
        functools.partial(assemble_kernel, own=own, chips=chips, frames=frames),
        out_shape=(
            jax.ShapeDtypeStruct((3, pixels), F32),
            jax.ShapeDtypeStruct((3, pixels), F32),
            jax.ShapeDtypeStruct((frames, 4), F32),
        ),
        in_specs=[smem, smem, full, full, smem],
        out_specs=[full] * 3,
        scratch_shapes=[pltpu.VMEM((1, pixels), F32)],
        name="assemble_outputs",
    )(index, frame_kinds, p0, p1, small_params)

    cols_own = lax.dynamic_index_in_dim(cols, me, 0, False)
    grad, parts = pl.pallas_call(
        functools.partial(norm_kernel, channels=channels),
        out_shape=(
            jax.ShapeDtypeStruct((rows_own, width), F32),
            jax.ShapeDtypeStruct((8, LANES), F32),
        ),
        in_specs=[smem] + [full] * 5,
        out_specs=[full] * 2,
        name="norm_parts",
    )(index, half, other, pack, cols_own, rows)
    pair = parts + swap(parts, "chan", shards, 1)
    totals = [pair[0:1]] + [swap(pair, "chan", shards, 2 * m)[0:1] for m in range(1, chips)]
    totals = jnp.concatenate(totals, axis=0)

    def like(value, dtype=F32):
        return jax.ShapeDtypeStruct(value.shape, dtype)

    out_shape = (
        [jax.ShapeDtypeStruct((1, 1), F32)]
        + [like(weight1.T)] * 3
        + [like(weight2.T)] * 3
        + [like(weight3)] * 3
        + [like(biases)] * 3
        + [like(small_params)] * 3
        + [like(weight1.T, BF16), like(weight2.T, BF16), like(weight3, BF16)]
        + [jax.ShapeDtypeStruct((1, rows_own), F32), jax.ShapeDtypeStruct((1, 27), F32)]
        + [jax.ShapeDtypeStruct((1, channels), F32), jax.ShapeDtypeStruct((1, rows_own), F32)]
        + [jax.ShapeDtypeStruct((1, 3), F32), jax.ShapeDtypeStruct((9, rows_own), F32)]
    )
    done = pl.pallas_call(
        functools.partial(update_kernel, channels=channels),
        out_shape=out_shape,
        in_specs=[full] * 18,
        out_specs=[full] * len(out_shape),
        name="adam_update",
    )(
        totals, grad, cols_own, rows,
        weight1.T, moment_w1.T, second_w1.T, weight2.T, moment_w2.T, second_w2.T,
        weight3, moment_w3, second_w3, moment_bias, second_bias, small_params, moment_small, second_small,
    )
    norm, updates, vectors = done[0], list(done[1:19]), done[19:]
    for slot in (0, 1, 2, 3, 4, 5, 15, 16):
        updates[slot] = updates[slot].T
    return (
        z_out,
        logdet,
        grad_input,
        norm.reshape(()),
        *updates,
        vectors[0].reshape(rows_own),
        vectors[1].reshape(27),
        vectors[2].reshape(channels),
        vectors[3].reshape(rows_own),
        vectors[4].reshape(3),
        vectors[5],
    )


def solution(mesh):
    chan_rows = P("chan", None)
    chan_cols = P(None, "chan")
    return jax.shard_map(
        local,
        mesh=mesh,
        in_specs=(
            P(None, "dp"), P("dp"), P("dp", None), P(None, "dp"), P(None, "dp"), P("dp", None),
            chan_rows, chan_cols, chan_cols, chan_cols, P(), P("chan"), P(), P(),
            chan_rows, chan_rows, chan_cols, chan_cols, chan_cols, chan_cols, chan_cols, chan_cols, P(), P(),
        ),
        out_specs=(
            P(None, "dp"), P("dp", None), P(None, "dp"), P(),
            chan_rows, chan_rows, chan_rows, chan_cols, chan_cols, chan_cols, chan_cols, chan_cols, chan_cols,
            chan_cols, chan_cols, chan_cols, P(), P(), P(), chan_rows, chan_cols, chan_cols,
            P("chan"), P(), P(), P("chan"), P(), chan_cols,
        ),
        check_vma=False,
    )
```

```python
import functools

import jax
import jax.numpy as jnp
from jax import lax
from jax.experimental import pallas as pl
from jax.experimental.pallas import tpu as pltpu
from jax.sharding import PartitionSpec as P

NMAX = 4
STEP = 7
SHRINK = 0.98
LR_RATE = 0.05
BETA_ONE = 0.5
BETA_TWO = 0.55
ADAM_EPS = 1e-08
DECAY = 0.01
CLIP_LIMIT = 1.0

WIDTH = 64
FRAME = 4096
BLOCK = 256
HALO = 2 * NMAX * WIDTH
LANES = 128
TAP_ROWS = 72
F32 = jnp.float32
BF16 = jnp.bfloat16
HIGH = lax.Precision.HIGHEST


def iota(shape, dim):
    return lax.broadcasted_iota(jnp.int32, shape, dim)


def dot_nn(left, right, precision=None):
    return lax.dot_general(
        left, right, (((1,), (0,)), ((), ())), precision=precision, preferred_element_type=F32
    )


def dot_nt(left, right, precision=None):
    return lax.dot_general(
        left, right, (((1,), (1,)), ((), ())), precision=precision, preferred_element_type=F32
    )


def dot_tn(left, right, precision=None):
    return lax.dot_general(
        left, right, (((0,), (0,)), ((), ())), precision=precision, preferred_element_type=F32
    )


def spread_one():
    row = iota((27, LANES), 0)
    return (iota((27, LANES), 1) == (row % 9) * 8 + row // 9).astype(F32)


def spread_three():
    row = iota((27, LANES), 0)
    return (iota((27, LANES), 1) == (8 - row % 9) * 8 + 4 + row // 9).astype(F32)


def lane_is_one(lane):
    return (lane % 8 < 3) & (lane < TAP_ROWS)


def lane_is_three(lane):
    return (lane % 8 >= 4) & (lane % 8 < 7) & (lane < TAP_ROWS)


def pack_kernel(w1_ref, w2_ref, w3_ref, bias_ref, u1_ref, out_ref):
    channels = w2_ref.shape[1]
    out_ref[:, 0:channels] = w2_ref[...]
    tile = dot_tn(w1_ref[...], spread_one(), HIGH) + dot_tn(w3_ref[...], spread_three(), HIGH)
    lane = iota((1, LANES), 1)
    for index, row in enumerate((u1_ref[...], bias_ref[0:1, :], bias_ref[1:2, :])):
        column = jnp.broadcast_to(row, (8, row.shape[1])).T[:, 0:1]
        tile = jnp.where(lane == TAP_ROWS + index, column, tile)
    out_ref[:, channels:] = tile


def col_taps(state, masks):
    size = state.shape[1]
    row_up, row_down, col_left, col_right = masks
    left = col_left * pltpu.roll(state, 1, 1)
    right = col_right * pltpu.roll(state, size - 1, 1)
    pieces = []
    for shift_y in (-1, 0, 1):
        for plane in (left, state, right):
            if shift_y == -1:
                plane = row_up * pltpu.roll(plane, WIDTH, 1)
            if shift_y == 1:
                plane = row_down * pltpu.roll(plane, size - WIDTH, 1)
            pieces.append(plane)
    return pieces


def comb_taps(q_ref, lanes, masks):
    size = lanes.size
    row_up, row_down, col_left, col_right = masks
    result = None
    for shift_y in (-1, 0, 1):
        base = 24 * (shift_y + 1)
        line = (
            col_left * pltpu.roll(q_ref[base : base + 8, lanes], 1, 1)
            + q_ref[base + 8 : base + 16, lanes]
            + col_right * pltpu.roll(q_ref[base + 16 : base + 24, lanes], size - 1, 1)
        )
        if shift_y == -1:
            line = row_up * pltpu.roll(line, WIDTH, 1)
        if shift_y == 1:
            line = row_down * pltpu.roll(line, size - WIDTH, 1)
        result = line if result is None else result + line
    return result


def normed_by(values, square):
    return values / jnp.sqrt(square + 1e-12)


def main_kernel(
    index_ref, u3_ref, x0_ref, x1_ref, u2_ref, planes_ref, small_ref,
    keep_ref, send_ref, cols_ref, rows_ref, og_ref,
    w_s, w13_s, w2_s, w2t_s, wout_s, bias_s, taps_s, sl1_s, sl2_s, cv1_s, cv2_s,
    lin1_s, lin2_s, gt1_s, gt2_s, acc1_s, acc2_s, tan1_s, tan2_s, g1_s, g2_s, hid1_s, hid2_s,
    q_s, q0_s, comb_s, *, own, channels, chips,
):
    me = index_ref[0]
    rows_own = channels // (2 * chips)
    region = own + 2 * HALO
    all_sum = functools.partial(jnp.sum, keepdims=True)

    for m in range(chips):
        for b, ref in ((0, x0_ref), (1, x1_ref)):
            w_s[jnp.bitwise_xor(me, 2 * m + b)] = ref[m]
    tile = w_s[:, :, channels:].reshape(channels, LANES)
    w2t = w_s[:, :, 0:channels].reshape(channels, channels)
    lane = iota((1, LANES), 1)
    is_one = lane_is_one(lane)
    is_three = lane_is_three(lane)
    taps_one = jnp.where(is_one, tile, 0.0)
    taps_three = jnp.where(is_three, tile, 0.0)
    head = (lane % 8 == 4) & (lane < TAP_ROWS)
    u1 = tile[:, TAP_ROWS : TAP_ROWS + 1]
    u2 = u2_ref[...]
    u3 = jnp.zeros((1, LANES), F32)
    for o in range(3):
        u3 = jnp.where(is_three & (lane % 8 == 4 + o), u3_ref[o], u3)
    for _ in range(2):
        v1 = all_sum(taps_one * u1, axis=0)
        v2 = all_sum(w2t * u2, axis=1)
        mixed = taps_three * u3
        mixed = mixed + pltpu.roll(mixed, LANES - 1, 1) + pltpu.roll(mixed, LANES - 2, 1)
        v3 = jnp.where(head, mixed, 0.0)
        v1 = normed_by(v1, all_sum(v1 * v1))
        v2 = normed_by(v2, all_sum(v2 * v2))
        v3 = normed_by(v3, all_sum(all_sum(v3 * v3, axis=0), axis=1))
        m1 = all_sum(taps_one * v1, axis=1)
        m2 = all_sum(w2t * v2, axis=0)
        spread = v3 + pltpu.roll(v3, 1, 1) + pltpu.roll(v3, 2, 1)
        m3 = all_sum(taps_three * spread, axis=0)
        for shift in (64, 32, 16, 8):
            m3 = m3 + pltpu.roll(m3, shift, 1)
        square1 = all_sum(m1 * m1)
        square2 = all_sum(m2 * m2)
        square3 = all_sum(jnp.where((lane >= 4) & (lane < 7), m3 * m3, 0.0))
        u1 = normed_by(m1, square1)
        u2 = normed_by(m2, square2)
        u3 = jnp.where(is_three, normed_by(m3, square3), 0.0)
    sigma1 = jnp.sqrt(square1)
    sigma2 = jnp.sqrt(square2)
    sigma3 = jnp.sqrt(square3)
    cols_ref[...] = jnp.where(lane == 0, u1, jnp.where(lane == 1, v2, v3)).reshape(cols_ref.shape)
    sigma_row = jnp.where(lane == 0, sigma1, jnp.where(lane == 1, sigma2, sigma3))
    rows_ref[...] = jnp.zeros(rows_ref.shape, F32)
    rows_ref[0:1, :] = u2
    rows_ref[1:2, 0:LANES] = v1
    rows_ref[2:3, 0:LANES] = u3
    rows_ref[3:4, 0:LANES] = sigma_row

    scaled = taps_one * (SHRINK / sigma1) + taps_three * (SHRINK / sigma3)
    w13_s[0:channels] = jnp.where(is_one, scaled, 0.0).astype(BF16)
    w13_s[channels:] = jnp.where(is_three, scaled, 0.0).astype(BF16)
    flipped = scaled.T
    blocks = [pltpu.roll(flipped[(8 - t) * 8 : (9 - t) * 8], 4, 0) for t in range(9)]
    flipped = jnp.concatenate(blocks + [jnp.zeros((8, channels), F32)], axis=0)
    first_rows = iota((TAP_ROWS + 8, 1), 0) % 8 < 4
    wout_s[:, 0:channels] = jnp.where(first_rows, flipped, 0.0).astype(BF16)
    wout_s[:, channels:] = jnp.where(first_rows, 0.0, flipped).astype(BF16)
    w2t_scaled = w2t * (SHRINK / sigma2)
    w2t_s[...] = w2t_scaled.astype(BF16)
    w2_s[...] = w2t_scaled.T.astype(BF16)
    for layer in range(2):
        column = tile[:, TAP_ROWS + 1 + layer : TAP_ROWS + 2 + layer]
        bias_s[layer] = jnp.broadcast_to(column, (channels, LANES))

    shift8 = small_ref[:, 0:1]
    scale8 = small_ref[:, 1:2]
    bias8 = small_ref[:, 2:3]
    extra8 = small_ref[:, 3:4]
    upper = iota((8, 1), 0) >= 4
    probes8 = planes_ref[8:16]
    cot8 = planes_ref[16:24]

    def masks_at(lanes):
        return [planes_ref[32 + i : 33 + i, lanes] for i in range(4)]

    def put_taps(slot, pieces, lanes):
        full = jnp.concatenate(pieces + [jnp.zeros((8, lanes.size), F32)], axis=0).astype(BF16)
        for c in range(lanes.size // LANES):
            chunk = lanes.start // LANES + c
            taps_s[slot, chunk, 0 : TAP_ROWS + 8] = full[:, c * LANES : (c + 1) * LANES]
            taps_s[slot, chunk, TAP_ROWS + 8 :] = jnp.zeros((LANES - TAP_ROWS - 8, LANES), BF16)

    whole = pl.ds(0, region)
    h8 = (planes_ref[0:8] + shift8) * scale8
    sig8 = 0.5 + 0.5 * jnp.tanh(0.5 * h8)
    rest8 = 1.0 - sig8
    slope0 = (sig8 + h8 * sig8 * rest8) / 1.1
    curve0 = sig8 * rest8 * (2.0 + h8 * (1.0 - 2.0 * sig8)) / 1.1
    state = jnp.where(upper, cot8, h8 * sig8 / 1.1)
    put_taps(0, col_taps(state, masks_at(whole)), whole)
    state = probes8 * jnp.where(upper, planes_ref[24 + 7 : 24 + 8], slope0)
    put_taps(1, col_taps(state, masks_at(whole)), whole)

    own_blocks = own // BLOCK
    ring = own + BLOCK

    def over_blocks(count, body, carry=0):
        pairs = count // 2
        if pairs:
            carry = lax.fori_loop(0, pairs, lambda j, kept: body(2 * j * BLOCK, 2 * BLOCK, kept), carry)
        if count % 2:
            carry = body((count - 1) * BLOCK, BLOCK, carry)
        return carry

    def halves(start, size, base, width):
        places = []
        for h in range(size // LANES):
            chunk = start // LANES + h - base // LANES
            chunks = width // LANES
            places.append(jnp.where((chunk >= 0) & (chunk < chunks), chunk, chunks))
        return places

    def put(ref, places, value):
        for h, place in enumerate(places):
            ref[place] = value[:, h * LANES : (h + 1) * LANES]

    def join(ref, first, count):
        return jnp.concatenate([ref[first + i] for i in range(count)], axis=1)

    def activation(act, slope_ref, curve_ref, lanes, ring_places):
        tanh = jnp.tanh(0.5 * act)
        half = 0.5 * tanh
        rest = 0.5 - half
        sig = (1.0 / 1.1) * (0.5 + half)
        hidden = act * sig
        slope_ref[:, lanes] = sig + hidden * rest
        put(curve_ref, ring_places, (rest * ((sig + sig) - tanh * hidden)).astype(BF16))
        return hidden.astype(BF16)

    def start_body(at, size, carry):
        start = pl.multiple_of(at, LANES)
        lanes = pl.ds(start, size)
        count = size // LANES
        ring_places = halves(start, size, HALO - LANES, ring)
        own_places = halves(start, size, HALO, own)
        act1 = dot_nn(w13_s[0:channels], join(taps_s.at[0], start // LANES, count))
        bias1 = bias_s[0]
        hidden1 = activation(
            act1 + jnp.concatenate([bias1] * count, axis=1), sl1_s, cv1_s, lanes, ring_places
        )
        put(hid1_s, own_places, hidden1)
        act2 = dot_nn(w2_s[...], hidden1)
        bias2 = bias_s[1]
        hidden2 = activation(
            act2 + jnp.concatenate([bias2] * count, axis=1), sl2_s, cv2_s, lanes, ring_places
        )
        put(hid2_s, own_places, hidden2)
        q0_s[:, lanes] = dot_nn(wout_s[:, 0:channels], hidden2)[0:TAP_ROWS]
        return carry

    over_blocks(own_blocks + 4, start_body)


    def series_stage(stage):
        offset = LANES * (stage - 1)
        count = own_blocks + 5 - stage
        tan_slot = min(stage, 3) - 1

        def body(at, size, carry):
            start = pl.multiple_of(offset + at, LANES)
            lanes = pl.ds(start, size)
            ring_places = halves(start, size, HALO - LANES, ring)
            own_places = halves(start, size, HALO, own)

            def pair_up(acc_ref, mine_ref, other_ref, value, slot):
                for h, place in enumerate(ring_places):
                    part = value[:, h * LANES : (h + 1) * LANES]
                    if stage <= 2:
                        mine_ref[stage - 1, place] = part.astype(BF16)
                    else:
                        acc_ref[place] += part * other_ref[slot, place].astype(F32)

            slot = 4 - stage
            taps = join(taps_s.at[stage], start // LANES, size // LANES)
            lin1 = dot_nn(w13_s[0:channels], taps)
            tan1 = (sl1_s[:, lanes] * lin1).astype(BF16)
            put(tan1_s.at[tan_slot], own_places, tan1)
            pair_up(acc1_s, lin1_s, gt1_s, lin1, slot)
            gt2 = dot_nn(w13_s[channels:], taps)
            g2 = (sl2_s[:, lanes] * gt2).astype(BF16)
            put(g2_s.at[tan_slot], own_places, g2)
            pair_up(acc2_s, gt2_s, lin2_s, gt2, slot)
            lin2 = dot_nn(w2_s[...], tan1)
            tan2 = (sl2_s[:, lanes] * lin2).astype(BF16)
            put(tan2_s.at[tan_slot], own_places, tan2)
            pair_up(acc2_s, lin2_s, gt2_s, lin2, slot)
            gt1 = dot_nn(w2t_s[...], g2)
            g1 = (sl1_s[:, lanes] * gt1).astype(BF16)
            put(g1_s.at[tan_slot], own_places, g1)
            pair_up(acc1_s, gt1_s, lin1_s, gt1, slot)
            q_fwd = dot_nn(wout_s[:, 0:channels], tan2)[0:TAP_ROWS]
            q_s[:, lanes] = q_fwd + dot_nn(wout_s[:, channels:], g1)[0:TAP_ROWS]
            return carry

        over_blocks(count, body)

        inside = pl.ds(offset, count * BLOCK)
        result = comb_taps(q_s, inside, masks_at(inside))
        core_from = HALO - offset
        comb_s[stage - 1] = result[:, core_from : core_from + own]
        if stage < NMAX:
            nxt = result[:, LANES : count * BLOCK - LANES]
            lanes = pl.ds(offset + LANES, (count - 1) * BLOCK)
            seed = probes8[:, offset + LANES : offset + LANES + (count - 1) * BLOCK]
            coef = planes_ref[24 + 4 + 3 - stage : 24 + 4 + 4 - stage, lanes]
            following = slope0[:, offset + LANES : offset + LANES + (count - 1) * BLOCK] * nxt
            following = following + jnp.where(upper, seed * coef, 0.0)
            put_taps(stage + 1, col_taps(following, masks_at(lanes)), lanes)

    def own_taps(slot):
        return join(taps_s.at[slot], HALO // LANES, own // LANES)

    def add_weight_grads(slot_pairs, tap_pairs, first):
        total = None
        for left, right in slot_pairs:
            part = dot_nt(left, right)
            total = part if total is None else total + part
        one = None
        three = None
        for left_one, left_three, slot in tap_pairs:
            part_one = dot_nt(left_one, own_taps(slot))
            part_three = dot_nt(left_three, own_taps(slot))
            one = part_one if one is None else one + part_one
            three = part_three if three is None else three + part_three
        tile_part = jnp.where(is_one, one, jnp.where(is_three, three, 0.0))
        w2_part = total.reshape(2 * chips, rows_own, channels)
        tile_part = tile_part.reshape(2 * chips, rows_own, LANES)
        if first:
            w_s[:, :, 0:channels] = w2_part
            w_s[:, :, channels:] = tile_part
        else:
            w_s[:, :, 0:channels] = w_s[:, :, 0:channels] + w2_part
            w_s[:, :, channels:] = w_s[:, :, channels:] + tile_part

    def slot_of(ref, slot):
        return join(ref.at[slot], 0, own // LANES)

    acc1_s[...] = jnp.zeros(acc1_s.shape, F32)
    acc2_s[...] = jnp.zeros(acc2_s.shape, F32)
    series_stage(1)
    series_stage(2)
    series_stage(3)
    add_weight_grads(
        ((slot_of(tan1_s, 1), slot_of(g2_s, 2)), (slot_of(tan1_s, 2), slot_of(g2_s, 1))),
        (
            (slot_of(g1_s, 2), slot_of(tan2_s, 2), 2),
            (slot_of(g1_s, 1), slot_of(tan2_s, 1), 3),
        ),
        True,
    )
    series_stage(4)
    add_weight_grads(
        ((slot_of(tan1_s, 0), slot_of(g2_s, 2)), (slot_of(tan1_s, 2), slot_of(g2_s, 0))),
        (
            (slot_of(g1_s, 2), slot_of(tan2_s, 2), 1),
            (slot_of(g1_s, 0), slot_of(tan2_s, 0), 4),
        ),
        False,
    )

    def final_body(at, size, carry):
        bias_one, bias_two = carry
        start = pl.multiple_of(HALO - LANES + at, LANES)
        lanes = pl.ds(start, size)
        count = size // LANES
        ring_from = at // LANES
        own_places = halves(start, size, HALO, own)
        gs2 = dot_nn(w13_s[channels:], join(taps_s.at[0], start // LANES, count))
        ga2 = join(cv2_s, ring_from, count).astype(F32) * join(acc2_s, ring_from, count) + sl2_s[:, lanes] * gs2
        low2 = ga2.astype(BF16)
        gs1 = dot_nn(w2t_s[...], low2)
        ga1 = join(cv1_s, ring_from, count).astype(F32) * join(acc1_s, ring_from, count) + sl1_s[:, lanes] * gs1
        low1 = ga1.astype(BF16)
        q_s[:, lanes] = q0_s[:, lanes] + dot_nn(wout_s[:, channels:], low1)[0:TAP_ROWS]
        put(g2_s.at[0], own_places, low2)
        put(g1_s.at[0], own_places, low1)
        for c in range(count):
            here = jnp.where(own_places[c] < own // LANES, 1.0, 0.0)
            bias_one = bias_one + here * ga1[:, c * LANES : (c + 1) * LANES]
            bias_two = bias_two + here * ga2[:, c * LANES : (c + 1) * LANES]
        return bias_one, bias_two

    zero = jnp.zeros((channels, LANES), F32)
    bias_one, bias_two = over_blocks(own_blocks + 1, final_body, (zero, zero))
    add_weight_grads(
        ((join(hid1_s, 0, own // LANES), slot_of(g2_s, 0)),), ((slot_of(g1_s, 0), join(hid2_s, 0, own // LANES), 0),), False
    )

    inside = pl.ds(HALO - LANES, own + BLOCK)
    result = comb_taps(q_s, inside, masks_at(inside))[:, LANES : LANES + own]
    mine = slice(HALO, HALO + own)
    h_own = h8[:, mine]
    cot_own = cot8[:, mine]
    probes_own = probes8[:, mine]
    mixed = comb_s[0] * pltpu.roll(comb_s[2], 4, 0)
    mixed = mixed + comb_s[1] * pltpu.roll(comb_s[1], 4, 0)
    mixed = mixed + comb_s[2] * pltpu.roll(comb_s[0], 4, 0)
    mixed = mixed + comb_s[3] * probes_own
    grad_h = cot_own + slope0[:, mine] * result + curve0[:, mine] * mixed
    grad_in = grad_h * scale8
    density = planes_ref[24:25, mine] * comb_s[0]
    for k in range(1, NMAX):
        density = density + planes_ref[24 + k : 25 + k, mine] * comb_s[k]
    density = density * probes_own
    density = density[0:1] + density[1:2] + density[2:3]
    row8 = iota((8, 1), 0)
    out = jnp.where(row8 < 3, h_own + result + bias8, jnp.where(row8 == 3, density, grad_in))
    og_ref[...] = jnp.where(row8 < 7, out, 0.0)

    sums = (
        all_sum(grad_in, axis=1),
        all_sum(grad_h * h_own, axis=1) + extra8,
        all_sum(cot_own, axis=1),
    )
    small_row = jnp.zeros((1, LANES), F32)
    for a, column in enumerate(sums):
        for i in range(3):
            small_row = jnp.where(lane == TAP_ROWS + 2 + 3 * a + i, column[4 + i : 5 + i], small_row)
    bias_one = all_sum(bias_one, axis=1)
    bias_two = all_sum(bias_two, axis=1)
    extras = jnp.where(lane == TAP_ROWS, bias_one, jnp.where(lane == TAP_ROWS + 1, bias_two, small_row))
    extras = extras.reshape(2 * chips, rows_own, LANES)
    w_s[:, :, channels:] = w_s[:, :, channels:] + extras

    core = jnp.bitwise_and(me, 1)
    chip = jnp.right_shift(me, 1)
    for m in range(chips):
        block = 2 * jnp.bitwise_xor(chip, m)
        keep_ref[m] = w_s[block + core]
        send_ref[m] = w_s[block + 1 - core]


def call_main(me, u3, x0, x1, u2, planes, small, own, channels, chips):
    rows_own = channels // (2 * chips)
    region = own + 2 * HALO
    wide = (own + BLOCK) // LANES + 1
    slot = own // LANES + 1
    width = channels + LANES
    out_shape = (
        jax.ShapeDtypeStruct((chips, rows_own, width), F32),
        jax.ShapeDtypeStruct((chips, rows_own, width), F32),
        jax.ShapeDtypeStruct((2 * chips, rows_own, LANES), F32),
        jax.ShapeDtypeStruct((8, channels), F32),
        jax.ShapeDtypeStruct((8, own), F32),
    )
    vmem = pltpu.VMEM
    scratch = [
        vmem((2 * chips, rows_own, width), F32),
        vmem((2 * channels, LANES), BF16),
        vmem((channels, channels), BF16),
        vmem((channels, channels), BF16),
        vmem((TAP_ROWS + 8, 2 * channels), BF16),
        vmem((2, channels, LANES), F32),
        vmem((NMAX + 1, region // LANES, LANES, LANES), BF16),
        vmem((channels, region), F32),
        vmem((channels, region), F32),
        vmem((wide, channels, LANES), BF16),
        vmem((wide, channels, LANES), BF16),
        vmem((2, wide, channels, LANES), BF16),
        vmem((2, wide, channels, LANES), BF16),
        vmem((2, wide, channels, LANES), BF16),
        vmem((2, wide, channels, LANES), BF16),
        vmem((wide, channels, LANES), F32),
        vmem((wide, channels, LANES), F32),
        vmem((3, slot, channels, LANES), BF16),
        vmem((3, slot, channels, LANES), BF16),
        vmem((3, slot, channels, LANES), BF16),
        vmem((3, slot, channels, LANES), BF16),
        vmem((slot, channels, LANES), BF16),
        vmem((slot, channels, LANES), BF16),
        vmem((TAP_ROWS, region), F32),
        vmem((TAP_ROWS, region), F32),
        vmem((NMAX, 8, own), F32),
    ]
    full = pl.BlockSpec(memory_space=pltpu.VMEM)
    return pl.pallas_call(
        functools.partial(main_kernel, own=own, channels=channels, chips=chips),
        out_shape=out_shape,
        in_specs=[pl.BlockSpec(memory_space=pltpu.SMEM)] * 2 + [full] * 5,
        out_specs=[full] * 5,
        scratch_shapes=scratch,
        compiler_params=pltpu.CompilerParams(vmem_limit_bytes=63 * 1024 * 1024),
        name="flow_block",
    )(me, u3, x0, x1, u2, planes, small)


def assemble_kernel(index_ref, kinds_ref, p0_ref, p1_ref, small_ref, z_ref, gin_ref, logdet_ref, dens_s, *, own, chips, frames):
    me = index_ref[0]
    for m in range(chips):
        for b, ref in ((0, p0_ref), (1, p1_ref)):
            shard = jnp.bitwise_xor(me, 2 * m + b)
            lanes = pl.ds(pl.multiple_of(shard * own, LANES), own)
            piece = ref[m]
            z_ref[:, lanes] = piece[0:3]
            gin_ref[:, lanes] = piece[4:7]
            dens_s[:, lanes] = piece[3:4]
    scale_sum = small_ref[1, 0] + small_ref[1, 1] + small_ref[1, 2]
    pixel = iota((1, FRAME), 1)
    bottom = (pixel // (WIDTH * 32)) % 2
    right = (pixel // 32) % 2
    lane = iota((1, 4), 1)
    for f in range(frames):
        line = dens_s[:, f * FRAME : (f + 1) * FRAME]
        quads = jnp.zeros((1, 4), F32)
        total = jnp.zeros((1, 1), F32)
        for slot in range(4):
            picked = jnp.where(bottom * 2 + right == slot, line, 0.0)
            picked = jnp.sum(picked, axis=1, keepdims=True)
            quads = jnp.where(lane == slot, picked, quads)
            total = total + picked
        split = kinds_ref[f] == 2
        whole = jnp.where(lane == 0, total + 4096.0 * scale_sum, 0.0)
        logdet_ref[f : f + 1, :] = jnp.where(split, quads + 1024.0 * scale_sum, whole)


def norm_kernel(index_ref, a_ref, b_ref, pack_ref, cols_ref, rows_ref, grad_ref, out_ref, *, channels):
    grad = a_ref[...].astype(F32) + b_ref[...].astype(F32)
    grad_ref[...] = grad
    lane = iota((1, LANES), 1)
    is_one = lane_is_one(lane)
    is_three = lane_is_three(lane)
    tile = grad[:, channels:]
    weights = pack_ref[:, channels:]
    cols = cols_ref[...]
    u1 = cols[:, 0:1]
    v2 = cols[:, 1:2]
    spread = jnp.where((lane % 8 == 4) & (lane < TAP_ROWS), cols, 0.0)
    spread = spread + pltpu.roll(spread, 1, 1) + pltpu.roll(spread, 2, 1)
    outer_one = u1 * rows_ref[1:2, 0:LANES]
    outer_three = spread * rows_ref[2:3, 0:LANES]
    outer_two = v2 * rows_ref[0:1, :]
    grad_two = grad[:, 0:channels]
    weight_two = pack_ref[:, 0:channels]

    def total(values):
        return jnp.sum(jnp.sum(values, axis=0, keepdims=True), axis=1, keepdims=True)

    bias = (lane == TAP_ROWS) | (lane == TAP_ROWS + 1)
    parts = (
        total(jnp.where(is_one, tile * tile, 0.0)),
        total(grad_two * grad_two),
        total(jnp.where(is_three, tile * tile, 0.0)),
        total(jnp.where(is_one, tile * weights, 0.0)),
        total(grad_two * weight_two),
        total(jnp.where(is_three, tile * weights, 0.0)),
        total(jnp.where(is_one, tile * outer_one, 0.0)),
        total(grad_two * outer_two),
        total(jnp.where(is_three, tile * outer_three, 0.0)),
        total(jnp.where(is_one, outer_one * outer_one, 0.0)),
        total(outer_two * outer_two),
        total(jnp.where(is_three, outer_three * outer_three, 0.0)),
        total(jnp.where(bias, tile * tile, 0.0)),
    )
    row = jnp.zeros((1, LANES), F32)
    for index, part in enumerate(parts):
        row = jnp.where(lane == index, part, row)
    small = (lane >= TAP_ROWS + 2) & (lane < TAP_ROWS + 11) & (index_ref[0] == 0)
    row = jnp.where(small, tile[0:1], row)
    out_ref[...] = jnp.broadcast_to(row, out_ref.shape)


def moment_step(grad, moment, second):
    new_moment = BETA_ONE * moment + (1.0 - BETA_ONE) * grad
    new_second = BETA_TWO * second + (1.0 - BETA_TWO) * grad * grad
    return (new_moment, new_second)


def adam_step(param, grad, moment, second):
    new_moment, new_second = moment_step(grad, moment, second)
    fix_one = 1.0 - BETA_ONE**STEP
    fix_two = 1.0 - BETA_TWO**STEP
    update = new_moment / fix_one / (jnp.sqrt(new_second / fix_two) + ADAM_EPS) + DECAY * param
    return (param - LR_RATE * update, new_moment, new_second)


def update_kernel(
    totals_ref, grad_ref, cols_ref, rows_ref,
    w1_ref, m1_ref, s1_ref, w2_ref, m2_ref, s2_ref, w3_ref, m3_ref, s3_ref,
    mb_ref, sb_ref, small_ref, msmall_ref, ssmall_ref,
    norm_out, nw1, nm1, ns1, nw2, nm2, ns2, nw3, nm3, ns3, cb, nmb, nsb, nsm, nmsm, nssm, lw1, lw2, lw3,
    u1_out, v1_out, u2_out, v2_out, u3_out, v3_out, *, channels,
):
    lane = iota((1, LANES), 1)
    lines = [totals_ref[m : m + 1] for m in range(totals_ref.shape[0])]
    while len(lines) > 1:
        lines = [lines[m] + lines[m + 1] for m in range(0, len(lines), 2)]
    row = lines[0]

    def pick(index):
        return jnp.sum(jnp.where(lane == index, row, 0.0), axis=1, keepdims=True)

    sigmas = rows_ref[3:4, 0:LANES]
    small_row = jnp.where((lane >= TAP_ROWS + 2) & (lane < TAP_ROWS + 11), row, 0.0)
    square = pick(12) + jnp.sum(small_row * small_row, axis=1, keepdims=True)
    scales = []
    for j in range(3):
        sigma = sigmas[:, j : j + 1]
        ratio = SHRINK / sigma
        factor = pick(3 + j) / sigma
        fixed = pick(j) - 2.0 * factor * pick(6 + j) + factor * factor * pick(9 + j)
        square = square + ratio * ratio * jnp.maximum(fixed, 0.0)
        scales.append((ratio, factor))
    norm = jnp.sqrt(square)
    norm_out[...] = norm
    clip = jnp.minimum(1.0, CLIP_LIMIT / (norm + 1e-06))

    cols = cols_ref[...]
    grad = grad_ref[...]
    tile = grad[:, channels:]
    is_one = lane_is_one(lane)
    is_three = lane_is_three(lane)
    spread = jnp.where((lane % 8 == 4) & (lane < TAP_ROWS), cols, 0.0)
    spread = spread + pltpu.roll(spread, 1, 1) + pltpu.roll(spread, 2, 1)
    outer_one = cols[:, 0:1] * rows_ref[1:2, 0:LANES]
    outer_three = spread * rows_ref[2:3, 0:LANES]
    outer_two = cols[:, 1:2] * rows_ref[0:1, :]
    fixed_one = jnp.where(is_one, scales[0][0] * (tile - scales[0][1] * outer_one) * clip, 0.0)
    fixed_two = scales[1][0] * (grad[:, 0:channels] - scales[1][1] * outer_two) * clip
    fixed_three = jnp.where(is_three, scales[2][0] * (tile - scales[2][1] * outer_three) * clip, 0.0)
    grad_one = dot_nt(spread_one(), fixed_one, HIGH)
    grad_two = fixed_two
    grad_three = dot_nt(spread_three(), fixed_three, HIGH)

    for grad_j, w_ref, m_ref, s_ref, nw, nm, ns, lw in (
        (grad_one, w1_ref, m1_ref, s1_ref, nw1, nm1, ns1, lw1),
        (grad_two, w2_ref, m2_ref, s2_ref, nw2, nm2, ns2, lw2),
        (grad_three, w3_ref, m3_ref, s3_ref, nw3, nm3, ns3, lw3),
    ):
        new, moment, second = adam_step(w_ref[...], grad_j, m_ref[...], s_ref[...])
        nw[...] = new
        nm[...] = moment
        ns[...] = second
        lw[...] = new.astype(BF16)

    bias = (tile * clip).T[TAP_ROWS : TAP_ROWS + 2, :]
    cb[...] = bias
    moment, second = moment_step(bias, mb_ref[...], sb_ref[...])
    nmb[...] = moment
    nsb[...] = second

    small_row = small_row * clip
    lane3 = iota((1, 3), 1)
    rows = []
    for a in range(3):
        line = jnp.zeros((1, 3), F32)
        for i in range(3):
            at = TAP_ROWS + 2 + 3 * a + i
            line = jnp.where(lane3 == i, small_row[:, at : at + 1], line)
        rows.append(line)
    small_grad = jnp.concatenate(rows, axis=0)
    new, moment, second = adam_step(small_ref[...], small_grad, msmall_ref[...], ssmall_ref[...])
    nsm[...] = new
    nmsm[...] = moment
    nssm[...] = second

    flipped = cols.T
    u1_out[...] = flipped[0:1]
    v2_out[...] = flipped[1:2]
    tap = iota((9, LANES), 0)
    select = (iota((9, LANES), 1) == (8 - tap) * 8 + 4).astype(F32)
    v3_out[...] = dot_nn(select, flipped, HIGH)
    v1_out[...] = dot_nt(rows_ref[1:2, 0:LANES], spread_one(), HIGH)
    u2_out[...] = rows_ref[0:1, :]
    u3_out[...] = rows_ref[2:3, 4:7]


def prepare_kernel(
    index_ref, kinds_ref, len_ref, cot_ref, params_ref, images_ref, probes_ref, cot_z_ref,
    planes_ref, small_ref, *, own, frames,
):
    region = planes_ref.shape[1]
    pixels = images_ref.shape[1]
    me = index_ref[0]
    first = me * own - HALO
    planes_ref[...] = jnp.zeros(planes_ref.shape, F32)
    for chunk in range(region // LANES):
        start = first + chunk * LANES
        source = pl.ds(pl.multiple_of(jnp.clip(start, 0, pixels - LANES), LANES), LANES)
        lanes = pl.ds(chunk * LANES, LANES)
        inside = (start >= 0) & (start < pixels)
        for row, ref in ((0, images_ref), (4, images_ref), (8, probes_ref), (12, probes_ref), (20, cot_z_ref)):
            planes_ref[row : row + 3, lanes] = jnp.where(inside, ref[:, source], 0.0)

    position = first + iota((1, region), 1)
    frame = jnp.right_shift(position, 12)
    pixel = jnp.bitwise_and(position, FRAME - 1)
    row = jnp.right_shift(pixel, 6)
    col = jnp.bitwise_and(pixel, WIDTH - 1)
    half = WIDTH // 2
    quad = 2 * jnp.right_shift(row, 5) + jnp.right_shift(col, 5)
    split = jnp.zeros((1, region), jnp.int32)
    for f in range(frames):
        split = jnp.where(frame == f, jnp.where(kinds_ref[f] == 2, 1, 0), split)
    slot = 4 * frame + jnp.where(split == 1, quad, 0)
    length = jnp.zeros((1, region), jnp.int32)
    weight = jnp.zeros((1, region), F32)
    for f in range(frames):
        for q in range(4):
            here = slot == 4 * f + q
            length = jnp.where(here, len_ref[f, q], length)
            weight = jnp.where(here, cot_ref[f, q], weight)
    for k in range(NMAX):
        coef = jnp.where(length >= k + 1, (-1.0) ** k / (k + 1), 0.0)
        planes_ref[24 + k : 25 + k] = coef
        planes_ref[24 + NMAX + k : 25 + NMAX + k] = coef * weight
    for index, line in enumerate((row, col)):
        low = (line == 0) | ((split == 1) & (line == half))
        high = (line == WIDTH - 1) | ((split == 1) & (line == half - 1))
        planes_ref[32 + 2 * index : 33 + 2 * index] = jnp.where(low, 0.0, 1.0)
        planes_ref[33 + 2 * index : 34 + 2 * index] = jnp.where(high, 0.0, 1.0)

    extra = jnp.float32(0.0)
    for f in range(frames):
        whole = 4096.0 * cot_ref[f, 0]
        quads = 1024.0 * (cot_ref[f, 0] + cot_ref[f, 1] + cot_ref[f, 2] + cot_ref[f, 3])
        extra = extra + jnp.where(kinds_ref[f] == 2, quads, whole)
    extra = jnp.where(me == 0, extra, 0.0)
    row8 = iota((8, LANES), 0)
    lane = iota((8, LANES), 1)
    values = []
    for a in range(3):
        value = jnp.zeros((8, LANES), F32)
        for i in range(3):
            value = jnp.where(row8 % 4 == i, params_ref[a, i], value)
        values.append(value)
    result = jnp.where(lane == 0, values[0], jnp.where(lane == 1, jnp.exp(values[1]), values[2]))
    small_ref[...] = jnp.where(row8 % 4 == 3, 0.0, jnp.where(lane == 3, extra, result))


def local(
    images, frame_kinds, series_len, probes, cot_z, cot_logdet, weight1, weight2, weight3, biases,
    small_params, power_u1, power_u2, power_u3, moment_w1, second_w1, moment_w2, second_w2,
    moment_w3, second_w3, moment_bias, second_bias, moment_small, second_small,
):
    shards = lax.axis_size("chan")
    replicas = lax.axis_size("dp")
    chips = shards // 2
    me = lax.axis_index("chan")
    channels = weight2.shape[0]
    rows_own = weight1.shape[0]
    pixels = images.shape[1]
    frames = frame_kinds.shape[0]
    own = pixels // shards
    width = channels + LANES
    full = pl.BlockSpec(memory_space=pltpu.VMEM)
    smem = pl.BlockSpec(memory_space=pltpu.SMEM)
    index = me.reshape(1).astype(jnp.int32)

    def swap(values, axis, size, bits):
        return lax.ppermute(values, axis, [(j, j ^ bits) for j in range(size)])

    def gather_shards(values):
        pieces = [values] + [swap(values, "chan", shards, 2 * m) for m in range(1, chips)]
        first = jnp.stack(pieces)
        return first, swap(first, "chan", shards, 1)

    pack = pl.pallas_call(
        pack_kernel,
        out_shape=jax.ShapeDtypeStruct((rows_own, width), F32),
        in_specs=[full] * 5,
        out_specs=full,
        name="pack_weights",
    )(weight1.T, weight2.T, weight3, biases, power_u1.reshape(1, rows_own))
    x0, x1 = gather_shards(pack)

    planes, small = pl.pallas_call(
        functools.partial(prepare_kernel, own=own, frames=frames),
        out_shape=(
            jax.ShapeDtypeStruct((40, own + 2 * HALO), F32),
            jax.ShapeDtypeStruct((8, LANES), F32),
        ),
        in_specs=[smem] * 5 + [full] * 3,
        out_specs=[full] * 2,
        name="prepare_planes",
    )(index, frame_kinds, series_len, cot_logdet, small_params, images, probes, cot_z)

    keep, send, cols, rows, og = call_main(
        index, power_u3, x0, x1, power_u2.reshape(1, channels), planes, small, own, channels, chips
    )

    got = swap(send, "chan", shards, 1)
    summed = keep + got
    low = summed.astype(BF16)
    total = summed[0]
    for m in range(1, chips):
        total = total + swap(low[m], "chan", shards, 2 * m).astype(F32)
    og, half = lax.optimization_barrier((og, total.astype(BF16)))
    bits = 1
    while 2 * bits < replicas:
        half = (half.astype(F32) + swap(half, "dp", replicas, bits).astype(F32)).astype(BF16)
        bits *= 2
    other = swap(half, "dp", replicas, bits) if replicas > 1 else jnp.zeros_like(half)

    p0, p1 = gather_shards(og)
    z_out, grad_input, logdet = pl.pallas_call(
        functools.partial(assemble_kernel, own=own, chips=chips, frames=frames),
        out_shape=(
            jax.ShapeDtypeStruct((3, pixels), F32),
            jax.ShapeDtypeStruct((3, pixels), F32),
            jax.ShapeDtypeStruct((frames, 4), F32),
        ),
        in_specs=[smem, smem, full, full, smem],
        out_specs=[full] * 3,
        scratch_shapes=[pltpu.VMEM((1, pixels), F32)],
        name="assemble_outputs",
    )(index, frame_kinds, p0, p1, small_params)

    cols_own = lax.dynamic_index_in_dim(cols, me, 0, False)
    grad, parts = pl.pallas_call(
        functools.partial(norm_kernel, channels=channels),
        out_shape=(
            jax.ShapeDtypeStruct((rows_own, width), F32),
            jax.ShapeDtypeStruct((8, LANES), F32),
        ),
        in_specs=[smem] + [full] * 5,
        out_specs=[full] * 2,
        name="norm_parts",
    )(index, half, other, pack, cols_own, rows)
    pair = parts + swap(parts, "chan", shards, 1)
    totals = [pair[0:1]] + [swap(pair, "chan", shards, 2 * m)[0:1] for m in range(1, chips)]
    totals = jnp.concatenate(totals, axis=0)

    def like(value, dtype=F32):
        return jax.ShapeDtypeStruct(value.shape, dtype)

    out_shape = (
        [jax.ShapeDtypeStruct((1, 1), F32)]
        + [like(weight1.T)] * 3
        + [like(weight2.T)] * 3
        + [like(weight3)] * 3
        + [like(biases)] * 3
        + [like(small_params)] * 3
        + [like(weight1.T, BF16), like(weight2.T, BF16), like(weight3, BF16)]
        + [jax.ShapeDtypeStruct((1, rows_own), F32), jax.ShapeDtypeStruct((1, 27), F32)]
        + [jax.ShapeDtypeStruct((1, channels), F32), jax.ShapeDtypeStruct((1, rows_own), F32)]
        + [jax.ShapeDtypeStruct((1, 3), F32), jax.ShapeDtypeStruct((9, rows_own), F32)]
    )
    done = pl.pallas_call(
        functools.partial(update_kernel, channels=channels),
        out_shape=out_shape,
        in_specs=[full] * 18,
        out_specs=[full] * len(out_shape),
        name="adam_update",
    )(
        totals, grad, cols_own, rows,
        weight1.T, moment_w1.T, second_w1.T, weight2.T, moment_w2.T, second_w2.T,
        weight3, moment_w3, second_w3, moment_bias, second_bias, small_params, moment_small, second_small,
    )
    norm, updates, vectors = done[0], list(done[1:19]), done[19:]
    for slot in (0, 1, 2, 3, 4, 5, 15, 16):
        updates[slot] = updates[slot].T
    return (
        z_out,
        logdet,
        grad_input,
        norm.reshape(()),
        *updates,
        vectors[0].reshape(rows_own),
        vectors[1].reshape(27),
        vectors[2].reshape(channels),
        vectors[3].reshape(rows_own),
        vectors[4].reshape(3),
        vectors[5],
    )


def solution(mesh):
    chan_rows = P("chan", None)
    chan_cols = P(None, "chan")
    return jax.shard_map(
        local,
        mesh=mesh,
        in_specs=(
            P(None, "dp"), P("dp"), P("dp", None), P(None, "dp"), P(None, "dp"), P("dp", None),
            chan_rows, chan_cols, chan_cols, chan_cols, P(), P("chan"), P(), P(),
            chan_rows, chan_rows, chan_cols, chan_cols, chan_cols, chan_cols, chan_cols, chan_cols, P(), P(),
        ),
        out_specs=(
            P(None, "dp"), P("dp", None), P(None, "dp"), P(),
            chan_rows, chan_rows, chan_rows, chan_cols, chan_cols, chan_cols, chan_cols, chan_cols, chan_cols,
            chan_cols, chan_cols, chan_cols, P(), P(), P(), chan_rows, chan_cols, chan_cols,
            P("chan"), P(), P(), P("chan"), P(), chan_cols,
        ),
        check_vma=False,
    )
```

```python
import functools

import jax
import jax.numpy as jnp
from jax import lax
from jax.experimental import pallas as pl
from jax.experimental.pallas import tpu as pltpu
from jax.sharding import PartitionSpec as P

NMAX = 4
STEP = 7
SHRINK = 0.98
LR_RATE = 0.05
BETA_ONE = 0.5
BETA_TWO = 0.55
ADAM_EPS = 1e-08
DECAY = 0.01
CLIP_LIMIT = 1.0

WIDTH = 64
FRAME = 4096
BLOCK = 256
HALO = 2 * NMAX * WIDTH
LANES = 128
TAP_ROWS = 72
F32 = jnp.float32
BF16 = jnp.bfloat16
HIGH = lax.Precision.HIGHEST


def iota(shape, dim):
    return lax.broadcasted_iota(jnp.int32, shape, dim)


def dot_nn(left, right, precision=None):
    return lax.dot_general(
        left, right, (((1,), (0,)), ((), ())), precision=precision, preferred_element_type=F32
    )


def dot_nt(left, right, precision=None):
    return lax.dot_general(
        left, right, (((1,), (1,)), ((), ())), precision=precision, preferred_element_type=F32
    )


def dot_tn(left, right, precision=None):
    return lax.dot_general(
        left, right, (((0,), (0,)), ((), ())), precision=precision, preferred_element_type=F32
    )


def spread_one():
    row = iota((27, LANES), 0)
    return (iota((27, LANES), 1) == (row % 9) * 8 + row // 9).astype(F32)


def spread_three():
    row = iota((27, LANES), 0)
    return (iota((27, LANES), 1) == (8 - row % 9) * 8 + 4 + row // 9).astype(F32)


def lane_is_one(lane):
    return (lane % 8 < 3) & (lane < TAP_ROWS)


def lane_is_three(lane):
    return (lane % 8 >= 4) & (lane % 8 < 7) & (lane < TAP_ROWS)


def pack_kernel(w1_ref, w2_ref, w3_ref, bias_ref, u1_ref, out_ref):
    channels = w2_ref.shape[1]
    out_ref[:, 0:channels] = w2_ref[...]
    tile = dot_tn(w1_ref[...], spread_one(), HIGH) + dot_tn(w3_ref[...], spread_three(), HIGH)
    lane = iota((1, LANES), 1)
    for index, row in enumerate((u1_ref[...], bias_ref[0:1, :], bias_ref[1:2, :])):
        column = jnp.broadcast_to(row, (8, row.shape[1])).T[:, 0:1]
        tile = jnp.where(lane == TAP_ROWS + index, column, tile)
    out_ref[:, channels:] = tile


def col_taps(state, masks):
    size = state.shape[1]
    row_up, row_down, col_left, col_right = masks
    left = col_left * pltpu.roll(state, 1, 1)
    right = col_right * pltpu.roll(state, size - 1, 1)
    pieces = []
    for shift_y in (-1, 0, 1):
        for plane in (left, state, right):
            if shift_y == -1:
                plane = row_up * pltpu.roll(plane, WIDTH, 1)
            if shift_y == 1:
                plane = row_down * pltpu.roll(plane, size - WIDTH, 1)
            pieces.append(plane)
    return pieces


def comb_taps(q_ref, lanes, masks):
    size = lanes.size
    row_up, row_down, col_left, col_right = masks
    result = None
    for shift_y in (-1, 0, 1):
        base = 24 * (shift_y + 1)
        line = (
            col_left * pltpu.roll(q_ref[base : base + 8, lanes], 1, 1)
            + q_ref[base + 8 : base + 16, lanes]
            + col_right * pltpu.roll(q_ref[base + 16 : base + 24, lanes], size - 1, 1)
        )
        if shift_y == -1:
            line = row_up * pltpu.roll(line, WIDTH, 1)
        if shift_y == 1:
            line = row_down * pltpu.roll(line, size - WIDTH, 1)
        result = line if result is None else result + line
    return result


def normed_by(values, square):
    return values / jnp.sqrt(square + 1e-12)


def visits(blocks):
    pairs = blocks // 2
    listed = [(2 * (blocks - 1), 2)] if blocks % 2 else []
    return listed + [(4 * j, 4) for j in [pairs - 1] + list(range(pairs - 1)) if pairs]


def margins(uses, valid):
    for extra in range(64):
        for before in range(extra + 1):
            size = extra + valid
            wrong = size < 4
            for first, blocks in uses:
                held = {}
                for at, n in visits(blocks):
                    place = min(max(first + at + before, 0), size - n)
                    for h in range(n):
                        held[place + h] = first + at + h
                wrong = wrong or any(held.get(before + c, c) != c for c in range(valid))
            if not wrong:
                return before, extra - before
    raise ValueError("no margins")


def buffer_plan(own):
    chunks = own // LANES
    blocks = own // BLOCK
    ring = chunks + 2
    return {
        "early": margins([(-4, blocks + 4)], chunks),
        "second": margins([(-3, blocks + 3)], chunks),
        "late": margins([(-2, blocks + 2), (-1, blocks + 1)], chunks),
        "kept": margins([(-2, blocks + 3), (0, blocks + 1), (-1, blocks + 2)], ring),
    }


def main_kernel(index_ref, u3_ref, u2_ref, planes_ref, small_ref, *refs, own, channels, chips):
    packs = refs[: 2 * chips]
    keep_ref, send_ref, og_ref, cols_ref, rows_ref = refs[2 * chips : 2 * chips + 5]
    (
        w_s, w13_s, w2_s, w2t_s, wout_s, bias_s, taps_s, sl1_s, sl2_s, cv1_s, cv2_s,
        lin1a_s, lin2a_s, gt1a_s, gt2a_s, lin1b_s, lin2b_s, gt1b_s, gt2b_s,
        part1_s, part2_s, mid1_s, mid2_s, tan1a_s, tan2a_s, g1a_s, g2a_s, tan1b_s, tan2b_s, g1b_s, g2b_s,
        tan1c_s, tan2c_s, g1c_s, g2c_s, hid1_s, hid2_s,
        q_s, q0_s, comb_s, tile_s, cols_s,
    ) = refs[2 * chips + 5 :]
    me = index_ref[0]
    rows_own = channels // (2 * chips)
    region = own + 2 * HALO
    all_sum = functools.partial(jnp.sum, keepdims=True)

    for shard, ref in enumerate(packs):
        w_s[jnp.bitwise_xor(me, shard)] = ref[...]
    tile = w_s[:, :, channels:].reshape(channels, LANES)
    w2t = w_s[:, :, 0:channels].reshape(channels, channels)
    lane = iota((1, LANES), 1)
    is_one = lane_is_one(lane)
    is_three = lane_is_three(lane)
    taps_one = jnp.where(is_one, tile, 0.0)
    taps_three = jnp.where(is_three, tile, 0.0)
    head = (lane % 8 == 4) & (lane < TAP_ROWS)
    u1 = tile[:, TAP_ROWS : TAP_ROWS + 1]
    u2 = u2_ref[...]
    u3 = jnp.zeros((1, LANES), F32)
    for o in range(3):
        u3 = jnp.where(is_three & (lane % 8 == 4 + o), u3_ref[o], u3)
    for _ in range(2):
        v1 = all_sum(taps_one * u1, axis=0)
        v2 = all_sum(w2t * u2, axis=1)
        mixed = taps_three * u3
        mixed = mixed + pltpu.roll(mixed, LANES - 1, 1) + pltpu.roll(mixed, LANES - 2, 1)
        v3 = jnp.where(head, mixed, 0.0)
        v1 = normed_by(v1, all_sum(v1 * v1))
        v2 = normed_by(v2, all_sum(v2 * v2))
        v3 = normed_by(v3, all_sum(all_sum(v3 * v3, axis=0), axis=1))
        m1 = all_sum(taps_one * v1, axis=1)
        m2 = all_sum(w2t * v2, axis=0)
        spread = v3 + pltpu.roll(v3, 1, 1) + pltpu.roll(v3, 2, 1)
        m3 = all_sum(taps_three * spread, axis=0)
        for shift in (64, 32, 16, 8):
            m3 = m3 + pltpu.roll(m3, shift, 1)
        square1 = all_sum(m1 * m1)
        square2 = all_sum(m2 * m2)
        square3 = all_sum(jnp.where((lane >= 4) & (lane < 7), m3 * m3, 0.0))
        u1 = normed_by(m1, square1)
        u2 = normed_by(m2, square2)
        u3 = jnp.where(is_three, normed_by(m3, square3), 0.0)
    sigma1 = jnp.sqrt(square1)
    sigma2 = jnp.sqrt(square2)
    sigma3 = jnp.sqrt(square3)
    cols_s[...] = jnp.where(lane == 0, u1, jnp.where(lane == 1, v2, v3)).reshape(cols_s.shape)
    cols_ref[...] = cols_s[me]
    sigma_row = jnp.where(lane == 0, sigma1, jnp.where(lane == 1, sigma2, sigma3))
    rows_ref[...] = jnp.zeros(rows_ref.shape, F32)
    rows_ref[0:1, :] = u2
    rows_ref[1:2, 0:LANES] = v1
    rows_ref[2:3, 0:LANES] = u3
    rows_ref[3:4, 0:LANES] = sigma_row

    scaled = taps_one * (SHRINK / sigma1) + taps_three * (SHRINK / sigma3)
    halved = jnp.where(is_one, 0.5 * scaled, 0.0)
    rest1 = 0.5 * tile[:, TAP_ROWS + 1 : TAP_ROWS + 2]
    for i in range(3):
        part = rest1.astype(BF16).astype(F32)
        halved = jnp.where(lane == TAP_ROWS + i, part, halved)
        rest1 = rest1 - part
    w13_s[0:channels] = halved.astype(BF16)
    w13_s[channels:] = jnp.where(is_three, 0.5 * scaled, 0.0).astype(BF16)
    flipped = scaled.T
    blocks = [pltpu.roll(flipped[(8 - t) * 8 : (9 - t) * 8], 4, 0) for t in range(9)]
    flipped = jnp.concatenate(blocks + [jnp.zeros((8, channels), F32)], axis=0)
    first_rows = iota((TAP_ROWS + 8, 1), 0) % 8 < 4
    wout_s[:, 0:channels] = jnp.where(first_rows, flipped, 0.0).astype(BF16)
    wout_s[:, channels:] = jnp.where(first_rows, 0.0, flipped).astype(BF16)
    w2t_scaled = w2t * (0.5 * SHRINK / sigma2)
    w2t_s[...] = w2t_scaled.astype(BF16)
    w2_s[...] = w2t_scaled.T.astype(BF16)
    bias_s[...] = jnp.broadcast_to(0.5 * tile[:, TAP_ROWS + 2 : TAP_ROWS + 3], (channels, LANES))

    shift8 = small_ref[:, 0:1]
    scale8 = small_ref[:, 1:2]
    bias8 = small_ref[:, 2:3]
    extra8 = small_ref[:, 3:4]
    upper = iota((8, 1), 0) >= 4
    probes8 = planes_ref[8:16]
    cot8 = planes_ref[16:24]

    def masks_at(lanes):
        return [planes_ref[32 + i : 33 + i, lanes] for i in range(4)]

    def put_taps(slot, pieces, lanes):
        ones = jnp.where(iota((8, lanes.size), 0) < 3, 1.0 if slot == 0 else 0.0, 0.0)
        full = jnp.concatenate(pieces + [ones], axis=0).astype(BF16)
        for c in range(lanes.size // LANES):
            chunk = lanes.start // LANES + c
            taps_s[slot, chunk] = full[:, c * LANES : (c + 1) * LANES]

    whole = pl.ds(0, region)
    h8 = (planes_ref[0:8] + shift8) * scale8
    sig8 = 0.5 + 0.5 * jnp.tanh(0.5 * h8)
    rest8 = 1.0 - sig8
    slope0 = (sig8 + h8 * sig8 * rest8) / 1.1
    curve0 = sig8 * rest8 * (2.0 + h8 * (1.0 - 2.0 * sig8)) / 1.1
    state = jnp.where(upper, cot8, h8 * sig8 / 1.1)
    put_taps(0, col_taps(state, masks_at(whole)), whole)
    state = probes8 * jnp.where(upper, planes_ref[24 + 7 : 24 + 8], slope0)
    put_taps(1, col_taps(state, masks_at(whole)), whole)

    own_blocks = own // BLOCK
    ring = own + BLOCK
    plan = buffer_plan(own)
    own_before = [plan[name][0] for name in ("early", "second", "late")]
    kept_before = plan["kept"][0]
    tan_s = (
        (tan1a_s, tan2a_s, g1a_s, g2a_s),
        (tan1b_s, tan2b_s, g1b_s, g2b_s),
        (tan1c_s, tan2c_s, g1c_s, g2c_s),
    )
    kept_s = ((lin1a_s, lin2a_s, gt1a_s, gt2a_s), (lin1b_s, lin2b_s, gt1b_s, gt2b_s))

    def over_blocks(count, body, carry=0):
        pairs = count // 2
        if count % 2:
            carry = body((count - 1) * BLOCK, BLOCK, carry)

        def turn(j, kept):
            return body(jnp.where(j == 0, pairs - 1, j - 1) * (2 * BLOCK), 2 * BLOCK, kept)

        return lax.fori_loop(0, pairs, turn, carry)

    def halves(start, size, base, width):
        places = []
        for h in range(size // LANES):
            chunk = start // LANES + h - base // LANES
            chunks = width // LANES
            places.append(jnp.where((chunk >= 0) & (chunk < chunks), chunk, chunks))
        return places

    def run_of(ref, start, size, base, before):
        first = start // LANES - base // LANES + before
        first = jnp.clip(first, 0, ref.shape[0] - size // LANES)
        return [first + h for h in range(size // LANES)]

    def put(ref, places, value):
        for h, place in enumerate(places):
            ref[place] = value[:, h * LANES : (h + 1) * LANES]

    def join(ref, first, count):
        return jnp.concatenate([ref[first + i] for i in range(count)], axis=1)

    def activation(half_act, slope_ref, curve_ref, lanes, ring_places):
        tanh = jnp.tanh(half_act)
        sig = (1.0 / 1.1) + (1.0 / 1.1) * tanh
        hidden = half_act * sig
        bent = tanh * hidden
        slope_ref[:, lanes] = (sig + hidden) - bent
        put(curve_ref, ring_places, ((1.0 - tanh) * (sig - bent)).astype(BF16))
        return hidden.astype(BF16)

    def start_body(at, size, carry):
        start = pl.multiple_of(at, LANES)
        lanes = pl.ds(start, size)
        count = size // LANES
        ring_places = halves(start, size, HALO - LANES, ring)
        own_places = run_of(hid1_s, start, size, HALO, own_before[0])
        act1 = dot_nn(w13_s[0:channels, 0 : TAP_ROWS + 8], join(taps_s.at[0], start // LANES, count))
        hidden1 = activation(act1, sl1_s, cv1_s, lanes, ring_places)
        put(hid1_s, own_places, hidden1)
        act2 = dot_nn(w2_s[...], hidden1)
        bias2 = bias_s[...]
        hidden2 = activation(
            act2 + jnp.concatenate([bias2] * count, axis=1), sl2_s, cv2_s, lanes, ring_places
        )
        put(hid2_s, own_places, hidden2)
        q0_s[:, lanes] = dot_nn(wout_s[:, 0:channels], hidden2)[0:TAP_ROWS]
        return carry

    over_blocks(own_blocks + 4, start_body)


    def series_stage(stage):
        offset = LANES * (stage - 1)
        count = own_blocks + 5 - stage
        tan_slot = min(stage, 3) - 1
        tan_refs = tan_s[tan_slot]

        def body(at, size, carry):
            start = pl.multiple_of(offset + at, LANES)
            lanes = pl.ds(start, size)
            own_places = run_of(tan_refs[0], start, size, HALO, own_before[tan_slot])
            if stage == 1:
                ring_places = halves(start, size, HALO - LANES, ring)
            else:
                ring_places = run_of(mid1_s, start, size, HALO - LANES, kept_before)
            shift = -kept_before if stage == 4 else 0

            def pair_up(value, save_to, partner, add_from, mix_to):
                for h, place in enumerate(ring_places):
                    part = value[:, h * LANES : (h + 1) * LANES]
                    if save_to is not None:
                        save_to[place] = part.astype(BF16)
                        continue
                    part = (part.astype(BF16) * partner[place + shift]).astype(F32)
                    if add_from is not None:
                        part = part + add_from[place].astype(F32)
                    mix_to[place] = part.astype(BF16)

            if stage <= 2:
                lin1_to, lin2_to, gt1_to, gt2_to = kept_s[stage - 1]
                moves = ((lin1_to,), (gt2_to,), (lin2_to,), (gt1_to,))
                moves = [(place, None, None, None) for (place,) in moves]
            else:
                lin1_of, lin2_of, gt1_of, gt2_of = kept_s[4 - stage]
                sum1, sum2 = (None, None) if stage == 3 else (mid1_s, mid2_s)
                end1, end2 = (mid1_s, mid2_s) if stage == 3 else (lin1b_s, lin2b_s)
                moves = (
                    (None, gt1_of, sum1, part1_s),
                    (None, lin2_of, sum2, part2_s),
                    (None, gt2_of, part2_s, end2),
                    (None, lin1_of, part1_s, end1),
                )
            taps = join(taps_s.at[stage], start // LANES, size // LANES)
            lin1 = dot_nn(w13_s[0:channels, 0 : TAP_ROWS + 8], taps)
            tan1 = (sl1_s[:, lanes] * lin1).astype(BF16)
            put(tan_refs[0], own_places, tan1)
            pair_up(lin1, *moves[0])
            gt2 = dot_nn(w13_s[channels:, 0 : TAP_ROWS + 8], taps)
            g2 = (sl2_s[:, lanes] * gt2).astype(BF16)
            put(tan_refs[3], own_places, g2)
            pair_up(gt2, *moves[1])
            lin2 = dot_nn(w2_s[...], tan1)
            tan2 = (sl2_s[:, lanes] * lin2).astype(BF16)
            put(tan_refs[1], own_places, tan2)
            pair_up(lin2, *moves[2])
            gt1 = dot_nn(w2t_s[...], g2)
            g1 = (sl1_s[:, lanes] * gt1).astype(BF16)
            put(tan_refs[2], own_places, g1)
            pair_up(gt1, *moves[3])
            q_fwd = dot_nn(wout_s[:, 0:channels], tan2)[0:TAP_ROWS]
            q_s[:, lanes] = q_fwd + dot_nn(wout_s[:, channels:], g1)[0:TAP_ROWS]
            return carry

        over_blocks(count, body)

        inside = pl.ds(offset, count * BLOCK)
        result = comb_taps(q_s, inside, masks_at(inside))
        core_from = HALO - offset
        comb_s[stage - 1] = result[:, core_from : core_from + own]
        if stage < NMAX:
            nxt = result[:, LANES : count * BLOCK - LANES]
            lanes = pl.ds(offset + LANES, (count - 1) * BLOCK)
            seed = probes8[:, offset + LANES : offset + LANES + (count - 1) * BLOCK]
            coef = planes_ref[24 + 4 + 3 - stage : 24 + 4 + 4 - stage, lanes]
            following = slope0[:, offset + LANES : offset + LANES + (count - 1) * BLOCK] * nxt
            following = following + jnp.where(upper, seed * coef, 0.0)
            put_taps(stage + 1, col_taps(following, masks_at(lanes)), lanes)

    def own_taps(slot):
        return join(taps_s.at[slot], HALO // LANES, own // LANES)

    def add_weight_grads(slot_pairs, tap_pairs, first):
        total = None
        for left, right in slot_pairs:
            part = dot_nt(left, right)
            total = part if total is None else total + part
        one = None
        three = None
        for left_one, left_three, slot in tap_pairs:
            taps = own_taps(slot)
            part_one = dot_nt(taps, left_one)
            part_three = dot_nt(taps, left_three)
            one = part_one if one is None else one + part_one
            three = part_three if three is None else three + part_three
        w2_part = total.reshape(2 * chips, rows_own, channels)
        tile_part = jnp.where(first_rows, one, three)
        if first:
            w_s[:, :, 0:channels] = w2_part
            tile_s[...] = tile_part
        else:
            w_s[:, :, 0:channels] = w_s[:, :, 0:channels] + w2_part
            tile_s[...] = tile_s[...] + tile_part

    def slot_of(kind, slot):
        return join(tan_s[slot][kind], own_before[slot], own // LANES)

    series_stage(1)
    series_stage(2)
    series_stage(3)
    add_weight_grads(
        ((slot_of(0, 1), slot_of(3, 2)), (slot_of(0, 2), slot_of(3, 1))),
        (
            (slot_of(2, 2), slot_of(1, 2), 2),
            (slot_of(2, 1), slot_of(1, 1), 3),
        ),
        True,
    )
    series_stage(4)
    add_weight_grads(
        ((slot_of(0, 0), slot_of(3, 2)), (slot_of(0, 2), slot_of(3, 0))),
        (
            (slot_of(2, 2), slot_of(1, 2), 1),
            (slot_of(2, 0), slot_of(1, 0), 4),
        ),
        False,
    )

    def final_body(at, size, carry):
        bias_one, bias_two = carry
        start = pl.multiple_of(HALO - LANES + at, LANES)
        lanes = pl.ds(start, size)
        count = size // LANES
        ring_from = at // LANES
        own_places = run_of(g1c_s, start, size, HALO, own_before[2])
        gs2 = dot_nn(w13_s[channels:, 0 : TAP_ROWS + 8], join(taps_s.at[0], start // LANES, count))
        acc2 = join(cv2_s, ring_from, count).astype(F32) * join(lin2b_s, ring_from + kept_before, count).astype(F32)
        ga2 = (acc2 + acc2) + sl2_s[:, lanes] * gs2
        low2 = ga2.astype(BF16)
        gs1 = dot_nn(w2t_s[...], low2)
        acc1 = join(cv1_s, ring_from, count).astype(F32) * join(lin1b_s, ring_from + kept_before, count).astype(F32)
        ga1 = (acc1 + acc1) + sl1_s[:, lanes] * gs1
        low1 = ga1.astype(BF16)
        q_s[:, lanes] = q0_s[:, lanes] + dot_nn(wout_s[:, channels:], low1)[0:TAP_ROWS]
        put(g2c_s, own_places, low2)
        put(g1c_s, own_places, low1)
        for c in range(count):
            chunk = (start - HALO) // LANES + c
            here = jnp.where((chunk >= 0) & (chunk < own // LANES), 1.0, 0.0)
            bias_one = bias_one + here * ga1[:, c * LANES : (c + 1) * LANES]
            bias_two = bias_two + here * ga2[:, c * LANES : (c + 1) * LANES]
        return bias_one, bias_two

    zero = jnp.zeros((channels, LANES), F32)
    bias_one, bias_two = over_blocks(own_blocks + 1, final_body, (zero, zero))
    add_weight_grads(
        ((join(hid1_s, own_before[0], own // LANES), slot_of(3, 2)),), ((slot_of(2, 2), join(hid2_s, own_before[0], own // LANES), 0),), False
    )

    inside = pl.ds(HALO - LANES, own + BLOCK)
    result = comb_taps(q_s, inside, masks_at(inside))[:, LANES : LANES + own]
    mine = slice(HALO, HALO + own)
    h_own = h8[:, mine]
    cot_own = cot8[:, mine]
    probes_own = probes8[:, mine]
    mixed = comb_s[0] * pltpu.roll(comb_s[2], 4, 0)
    mixed = mixed + comb_s[1] * pltpu.roll(comb_s[1], 4, 0)
    mixed = mixed + comb_s[2] * pltpu.roll(comb_s[0], 4, 0)
    mixed = mixed + comb_s[3] * probes_own
    grad_h = cot_own + slope0[:, mine] * result + curve0[:, mine] * mixed
    grad_in = grad_h * scale8
    density = planes_ref[24:25, mine] * comb_s[0]
    for k in range(1, NMAX):
        density = density + planes_ref[24 + k : 25 + k, mine] * comb_s[k]
    density = density * probes_own
    density = density[0:1] + density[1:2] + density[2:3]
    row8 = iota((8, 1), 0)
    high = density.astype(BF16).astype(F32)
    out = jnp.where(row8 < 3, h_own + result + bias8, jnp.where(row8 == 3, high, grad_in))
    out = jnp.where(row8 == 7, density - high, out)
    if own < channels:
        out = jnp.concatenate([out, jnp.zeros((8, channels - own), F32)], axis=1)
    lines = [out[:, c * channels : (c + 1) * channels] for c in range(out.shape[1] // channels)]
    if len(lines) == 1:
        lines.append(jnp.zeros((8, channels), F32))
    out = jnp.concatenate(lines, axis=0).astype(BF16)
    og_ref[...] = jnp.zeros(og_ref.shape, BF16)
    og_ref[:, 0:channels] = out
    send_ref[chips * rows_own :, 0:channels] = out
    send_ref[chips * rows_own :, channels:] = jnp.zeros((out.shape[0], LANES), BF16)

    sums = (
        all_sum(grad_in, axis=1),
        all_sum(grad_h * h_own, axis=1) + extra8,
        all_sum(cot_own, axis=1),
    )
    small_row = jnp.zeros((1, LANES), F32)
    for a, column in enumerate(sums):
        for i in range(3):
            small_row = jnp.where(lane == TAP_ROWS + 2 + 3 * a + i, column[4 + i : 5 + i], small_row)
    bias_one = all_sum(bias_one, axis=1)
    bias_two = all_sum(bias_two, axis=1)
    extras = jnp.where(lane == TAP_ROWS, bias_one, jnp.where(lane == TAP_ROWS + 1, bias_two, small_row))
    blank = jnp.zeros((LANES - TAP_ROWS - 8, channels), F32)
    flat = jnp.concatenate([tile_s[...], blank], axis=0).T
    extras = jnp.where(lane < TAP_ROWS, flat, extras)
    w_s[:, :, channels:] = extras.reshape(2 * chips, rows_own, LANES)

    core = jnp.bitwise_and(me, 1)
    chip = jnp.right_shift(me, 1)
    for m in range(chips):
        block = 2 * jnp.bitwise_xor(chip, m)
        keep_ref[m] = w_s[block + core]
        send_ref[m * rows_own : (m + 1) * rows_own] = w_s[block + 1 - core].astype(BF16)


def output_rows(own, channels):
    return max(8 * (own // channels), 16)


def call_main(me, u3, u2, planes, small, packs, own, channels, chips):
    rows_own = channels // (2 * chips)
    region = own + 2 * HALO
    wide = (own + BLOCK) // LANES + 1
    width = channels + LANES
    out_shape = (
        jax.ShapeDtypeStruct((chips, rows_own, width), F32),
        jax.ShapeDtypeStruct((chips * rows_own + output_rows(own, channels), width), BF16),
        jax.ShapeDtypeStruct((output_rows(own, channels), width), BF16),
        jax.ShapeDtypeStruct((rows_own, LANES), F32),
        jax.ShapeDtypeStruct((8, channels), F32),
    )
    vmem = pltpu.VMEM
    plan = buffer_plan(own)

    def buffer(name, lanes):
        return vmem((lanes // LANES + sum(plan[name]), channels, LANES), BF16)

    scratch = [
        vmem((2 * chips, rows_own, width), F32),
        vmem((2 * channels, LANES), BF16),
        vmem((channels, channels), BF16),
        vmem((channels, channels), BF16),
        vmem((TAP_ROWS + 8, 2 * channels), BF16),
        vmem((channels, LANES), F32),
        vmem((NMAX + 1, region // LANES, TAP_ROWS + 8, LANES), BF16),
        vmem((channels, region), F32),
        vmem((channels, region), F32),
        *[vmem((wide, channels, LANES), BF16)] * 6,
        *[buffer("kept", own + BLOCK)] * 8,
        *[buffer("early", own)] * 4,
        *[buffer("second", own)] * 4,
        *[buffer("late", own)] * 4,
        *[buffer("early", own)] * 2,
        vmem((TAP_ROWS, region), F32),
        vmem((TAP_ROWS, region), F32),
        vmem((NMAX, 8, own), F32),
        vmem((TAP_ROWS + 8, channels), F32),
        vmem((2 * chips, rows_own, LANES), F32),
    ]
    full = pl.BlockSpec(memory_space=pltpu.VMEM)
    return pl.pallas_call(
        functools.partial(main_kernel, own=own, channels=channels, chips=chips),
        out_shape=out_shape,
        in_specs=[pl.BlockSpec(memory_space=pltpu.SMEM)] * 2 + [full] * (3 + 2 * chips),
        out_specs=[full] * 5,
        scratch_shapes=scratch,
        compiler_params=pltpu.CompilerParams(vmem_limit_bytes=63 * 1024 * 1024),
        name="flow_block",
    )(me, u3, u2, planes, small, *packs)


def assemble_kernel(index_ref, kinds_ref, small_ref, *refs, own, channels, chips, frames):
    pieces = refs[: chips + 1]
    z_ref, gin_ref, logdet_ref, dens_s = refs[chips + 1 :]
    me = index_ref[0]
    lines = max(own // channels, 1)
    size = min(own, channels)
    rows = output_rows(own, channels)
    for m in range(chips):
        for b in range(2):
            shard = jnp.bitwise_xor(me, 2 * m + b)
            if m == 0:
                block = pieces[b][...]
            else:
                message = pieces[m + 1]
                first = message.shape[0] - (2 - b) * rows
                block = message[first : first + rows]
            block = block.astype(F32)
            for c in range(lines):
                lanes = pl.ds(pl.multiple_of(shard * own + c * size, LANES), size)
                piece = block[8 * c : 8 * c + 8, 0:size]
                z_ref[:, lanes] = piece[0:3]
                gin_ref[:, lanes] = piece[4:7]
                dens_s[:, lanes] = piece[3:4] + piece[7:8]
    scale_sum = small_ref[1, 0] + small_ref[1, 1] + small_ref[1, 2]
    pixel = iota((1, FRAME), 1)
    bottom = (pixel // (WIDTH * 32)) % 2
    right = (pixel // 32) % 2
    lane = iota((1, 4), 1)
    for f in range(frames):
        line = dens_s[:, f * FRAME : (f + 1) * FRAME]
        quads = jnp.zeros((1, 4), F32)
        total = jnp.zeros((1, 1), F32)
        for slot in range(4):
            picked = jnp.where(bottom * 2 + right == slot, line, 0.0)
            picked = jnp.sum(picked, axis=1, keepdims=True)
            quads = jnp.where(lane == slot, picked, quads)
            total = total + picked
        split = kinds_ref[f] == 2
        whole = jnp.where(lane == 0, total + 4096.0 * scale_sum, 0.0)
        logdet_ref[f : f + 1, :] = jnp.where(split, quads + 1024.0 * scale_sum, whole)


def norm_kernel(index_ref, a_ref, b_ref, pack_ref, cols_ref, rows_ref, grad_ref, out_ref, *, channels):
    grad = a_ref[...].astype(F32) + b_ref[...].astype(F32)
    grad_ref[...] = grad
    lane = iota((1, LANES), 1)
    is_one = lane_is_one(lane)
    is_three = lane_is_three(lane)
    tile = grad[:, channels:]
    weights = pack_ref[:, channels:]
    cols = cols_ref[...]
    u1 = cols[:, 0:1]
    v2 = cols[:, 1:2]
    spread = jnp.where((lane % 8 == 4) & (lane < TAP_ROWS), cols, 0.0)
    spread = spread + pltpu.roll(spread, 1, 1) + pltpu.roll(spread, 2, 1)
    outer_one = u1 * rows_ref[1:2, 0:LANES]
    outer_three = spread * rows_ref[2:3, 0:LANES]
    outer_two = v2 * rows_ref[0:1, :]
    grad_two = grad[:, 0:channels]
    weight_two = pack_ref[:, 0:channels]

    def total(values):
        return jnp.sum(jnp.sum(values, axis=0, keepdims=True), axis=1, keepdims=True)

    bias = (lane == TAP_ROWS) | (lane == TAP_ROWS + 1)
    parts = (
        total(jnp.where(is_one, tile * tile, 0.0)),
        total(grad_two * grad_two),
        total(jnp.where(is_three, tile * tile, 0.0)),
        total(jnp.where(is_one, tile * weights, 0.0)),
        total(grad_two * weight_two),
        total(jnp.where(is_three, tile * weights, 0.0)),
        total(jnp.where(is_one, tile * outer_one, 0.0)),
        total(grad_two * outer_two),
        total(jnp.where(is_three, tile * outer_three, 0.0)),
        total(jnp.where(is_one, outer_one * outer_one, 0.0)),
        total(outer_two * outer_two),
        total(jnp.where(is_three, outer_three * outer_three, 0.0)),
        total(jnp.where(bias, tile * tile, 0.0)),
    )
    row = jnp.zeros((1, LANES), F32)
    for index, part in enumerate(parts):
        row = jnp.where(lane == index, part, row)
    small = (lane >= TAP_ROWS + 2) & (lane < TAP_ROWS + 11) & (index_ref[0] == 0)
    row = jnp.where(small, tile[0:1], row)
    out_ref[...] = jnp.broadcast_to(row, out_ref.shape)


def moment_step(grad, moment, second):
    new_moment = BETA_ONE * moment + (1.0 - BETA_ONE) * grad
    new_second = BETA_TWO * second + (1.0 - BETA_TWO) * grad * grad
    return (new_moment, new_second)


def adam_step(param, grad, moment, second):
    new_moment, new_second = moment_step(grad, moment, second)
    fix_one = 1.0 - BETA_ONE**STEP
    fix_two = 1.0 - BETA_TWO**STEP
    update = new_moment / fix_one / (jnp.sqrt(new_second / fix_two) + ADAM_EPS) + DECAY * param
    return (param - LR_RATE * update, new_moment, new_second)


def arrange_kernel(
    grad_ref, cols_ref, rows_ref,
    g1_out, o1_out, o2_out, g3_out, o3_out, bias_out, u1_out, v1_out, u2_out, v2_out, u3_out, v3_out, *, channels,
):
    lane = iota((1, LANES), 1)
    cols = cols_ref[...]
    tile = grad_ref[:, channels:]
    is_one = lane_is_one(lane)
    is_three = lane_is_three(lane)
    spread = jnp.where((lane % 8 == 4) & (lane < TAP_ROWS), cols, 0.0)
    spread = spread + pltpu.roll(spread, 1, 1) + pltpu.roll(spread, 2, 1)
    outer_one = jnp.where(is_one, cols[:, 0:1] * rows_ref[1:2, 0:LANES], 0.0)
    outer_three = jnp.where(is_three, spread * rows_ref[2:3, 0:LANES], 0.0)
    o2_out[...] = cols[:, 1:2] * rows_ref[0:1, :]
    g1_out[...] = dot_nt(spread_one(), jnp.where(is_one, tile, 0.0), HIGH)
    o1_out[...] = dot_nt(spread_one(), outer_one, HIGH)
    g3_out[...] = dot_nt(spread_three(), jnp.where(is_three, tile, 0.0), HIGH)
    o3_out[...] = dot_nt(spread_three(), outer_three, HIGH)
    bias_out[...] = tile.T[TAP_ROWS : TAP_ROWS + 2, :]
    flipped = cols.T
    u1_out[...] = flipped[0:1]
    v2_out[...] = flipped[1:2]
    tap = iota((9, LANES), 0)
    select = (iota((9, LANES), 1) == (8 - tap) * 8 + 4).astype(F32)
    v3_out[...] = dot_nn(select, flipped, HIGH)
    v1_out[...] = dot_nt(rows_ref[1:2, 0:LANES], spread_one(), HIGH)
    u2_out[...] = rows_ref[0:1, :]
    u3_out[...] = rows_ref[2:3, 4:7]


def update_kernel(
    totals_ref, rows_ref, grad_ref, g1_ref, o1_ref, o2_ref, g3_ref, o3_ref, bias_ref,
    w1_ref, m1_ref, s1_ref, w2_ref, m2_ref, s2_ref, w3_ref, m3_ref, s3_ref,
    mb_ref, sb_ref, small_ref, msmall_ref, ssmall_ref,
    norm_out, nw1, nm1, ns1, nw2, nm2, ns2, nw3, nm3, ns3, cb, nmb, nsb, nsm, nmsm, nssm, lw1, lw2, lw3, *, channels,
):
    lane = iota((1, LANES), 1)
    lines = [totals_ref[m : m + 1] for m in range(totals_ref.shape[0])]
    while len(lines) > 1:
        lines = [lines[m] + lines[m + 1] for m in range(0, len(lines), 2)]
    row = lines[0]

    def pick(index):
        return row[:, index : index + 1]

    small_row = jnp.where((lane >= TAP_ROWS + 2) & (lane < TAP_ROWS + 11), row, 0.0)
    square = pick(12) + jnp.sum(small_row * small_row, axis=1, keepdims=True)
    scales = []
    for j in range(3):
        sigma = rows_ref[3:4, j : j + 1]
        ratio = SHRINK / sigma
        factor = pick(3 + j) / sigma
        fixed = pick(j) - 2.0 * factor * pick(6 + j) + factor * factor * pick(9 + j)
        square = square + ratio * ratio * jnp.maximum(fixed, 0.0)
        scales.append((ratio, factor))
    norm = jnp.sqrt(square)
    norm_out[...] = norm
    clip = jnp.minimum(1.0, CLIP_LIMIT / (norm + 1e-06))

    for index, grad, outer, w_ref, m_ref, s_ref, nw, nm, ns, lw in (
        (0, g1_ref[...], o1_ref, w1_ref, m1_ref, s1_ref, nw1, nm1, ns1, lw1),
        (1, grad_ref[:, 0:channels], o2_ref, w2_ref, m2_ref, s2_ref, nw2, nm2, ns2, lw2),
        (2, g3_ref[...], o3_ref, w3_ref, m3_ref, s3_ref, nw3, nm3, ns3, lw3),
    ):
        ratio, factor = scales[index]
        fixed = (clip * ratio) * (grad - factor * outer[...])
        new, moment, second = adam_step(w_ref[...], fixed, m_ref[...], s_ref[...])
        nw[...] = new
        nm[...] = moment
        ns[...] = second
        lw[...] = new.astype(BF16)

    bias = bias_ref[...] * clip
    cb[...] = bias
    moment, second = moment_step(bias, mb_ref[...], sb_ref[...])
    nmb[...] = moment
    nsb[...] = second

    small_row = small_row * clip
    lane3 = iota((1, 3), 1)
    rows = []
    for a in range(3):
        line = jnp.zeros((1, 3), F32)
        for i in range(3):
            at = TAP_ROWS + 2 + 3 * a + i
            line = jnp.where(lane3 == i, small_row[:, at : at + 1], line)
        rows.append(line)
    small_grad = jnp.concatenate(rows, axis=0)
    new, moment, second = adam_step(small_ref[...], small_grad, msmall_ref[...], ssmall_ref[...])
    nsm[...] = new
    nmsm[...] = moment
    nssm[...] = second


def prepare_kernel(
    index_ref, kinds_ref, len_ref, cot_ref, params_ref, images_ref, probes_ref, cot_z_ref,
    planes_ref, small_ref, *, own, frames,
):
    region = planes_ref.shape[1]
    pixels = images_ref.shape[1]
    me = index_ref[0]
    first = me * own - HALO
    planes_ref[...] = jnp.zeros(planes_ref.shape, F32)
    for chunk in range(region // LANES):
        start = first + chunk * LANES
        source = pl.ds(pl.multiple_of(jnp.clip(start, 0, pixels - LANES), LANES), LANES)
        lanes = pl.ds(chunk * LANES, LANES)
        inside = (start >= 0) & (start < pixels)
        for row, ref in ((0, images_ref), (4, images_ref), (8, probes_ref), (12, probes_ref), (20, cot_z_ref)):
            planes_ref[row : row + 3, lanes] = jnp.where(inside, ref[:, source], 0.0)

    position = first + iota((1, region), 1)
    frame = jnp.right_shift(position, 12)
    pixel = jnp.bitwise_and(position, FRAME - 1)
    row = jnp.right_shift(pixel, 6)
    col = jnp.bitwise_and(pixel, WIDTH - 1)
    half = WIDTH // 2
    quad = 2 * jnp.right_shift(row, 5) + jnp.right_shift(col, 5)
    split = jnp.zeros((1, region), jnp.int32)
    for f in range(frames):
        split = jnp.where(frame == f, jnp.where(kinds_ref[f] == 2, 1, 0), split)
    slot = 4 * frame + jnp.where(split == 1, quad, 0)
    length = jnp.zeros((1, region), jnp.int32)
    weight = jnp.zeros((1, region), F32)
    for f in range(frames):
        for q in range(4):
            here = slot == 4 * f + q
            length = jnp.where(here, len_ref[f, q], length)
            weight = jnp.where(here, cot_ref[f, q], weight)
    for k in range(NMAX):
        coef = jnp.where(length >= k + 1, (-1.0) ** k / (k + 1), 0.0)
        planes_ref[24 + k : 25 + k] = coef
        planes_ref[24 + NMAX + k : 25 + NMAX + k] = coef * weight
    for index, line in enumerate((row, col)):
        low = (line == 0) | ((split == 1) & (line == half))
        high = (line == WIDTH - 1) | ((split == 1) & (line == half - 1))
        planes_ref[32 + 2 * index : 33 + 2 * index] = jnp.where(low, 0.0, 1.0)
        planes_ref[33 + 2 * index : 34 + 2 * index] = jnp.where(high, 0.0, 1.0)

    extra = jnp.float32(0.0)
    for f in range(frames):
        whole = 4096.0 * cot_ref[f, 0]
        quads = 1024.0 * (cot_ref[f, 0] + cot_ref[f, 1] + cot_ref[f, 2] + cot_ref[f, 3])
        extra = extra + jnp.where(kinds_ref[f] == 2, quads, whole)
    extra = jnp.where(me == 0, extra, 0.0)
    row8 = iota((8, LANES), 0)
    lane = iota((8, LANES), 1)
    values = []
    for a in range(3):
        value = jnp.zeros((8, LANES), F32)
        for i in range(3):
            value = jnp.where(row8 % 4 == i, params_ref[a, i], value)
        values.append(value)
    result = jnp.where(lane == 0, values[0], jnp.where(lane == 1, jnp.exp(values[1]), values[2]))
    small_ref[...] = jnp.where(row8 % 4 == 3, 0.0, jnp.where(lane == 3, extra, result))


def local(
    images, frame_kinds, series_len, probes, cot_z, cot_logdet, weight1, weight2, weight3, biases,
    small_params, power_u1, power_u2, power_u3, moment_w1, second_w1, moment_w2, second_w2,
    moment_w3, second_w3, moment_bias, second_bias, moment_small, second_small,
):
    shards = lax.axis_size("chan")
    replicas = lax.axis_size("dp")
    chips = shards // 2
    me = lax.axis_index("chan")
    channels = weight2.shape[0]
    rows_own = weight1.shape[0]
    pixels = images.shape[1]
    frames = frame_kinds.shape[0]
    own = pixels // shards
    width = channels + LANES
    full = pl.BlockSpec(memory_space=pltpu.VMEM)
    smem = pl.BlockSpec(memory_space=pltpu.SMEM)
    index = me.reshape(1).astype(jnp.int32)

    def swap(values, axis, size, bits):
        return lax.ppermute(values, axis, [(j, j ^ bits) for j in range(size)])

    pack = pl.pallas_call(
        pack_kernel,
        out_shape=jax.ShapeDtypeStruct((rows_own, width), F32),
        in_specs=[full] * 5,
        out_specs=full,
        name="pack_weights",
    )(weight1.T, weight2.T, weight3, biases, power_u1.reshape(1, rows_own))
    near = [pack] + [swap(pack, "chan", shards, 2 * m) for m in range(1, chips)]
    planes, small = pl.pallas_call(
        functools.partial(prepare_kernel, own=own, frames=frames),
        out_shape=(
            jax.ShapeDtypeStruct((40, own + 2 * HALO), F32),
            jax.ShapeDtypeStruct((8, LANES), F32),
        ),
        in_specs=[smem] * 5 + [full] * 3,
        out_specs=[full] * 2,
        name="prepare_planes",
    )(index, frame_kinds, series_len, cot_logdet, small_params, images, probes, cot_z)

    near[-1], planes = lax.optimization_barrier((near[-1], planes))
    packs = []
    for values in near:
        packs += [values, swap(values, "chan", shards, 1)]

    keep, send, og, cols_own, rows = call_main(
        index, power_u3, power_u2.reshape(1, channels), planes, small, packs, own, channels, chips
    )

    got = swap(send, "chan", shards, 1)
    og_other = got[chips * rows_own :]
    summed = keep + got[: chips * rows_own].reshape(keep.shape).astype(F32)
    total = summed[0]
    pieces = [og, og_other]
    for m in range(1, chips):
        message = jnp.concatenate([summed[m].astype(BF16), og, og_other], axis=0)
        message = swap(message, "chan", shards, 2 * m)
        total = total + message[:rows_own].astype(F32)
        pieces.append(message)
    half = total.astype(BF16)
    assembled = pl.pallas_call(
        functools.partial(assemble_kernel, own=own, channels=channels, chips=chips, frames=frames),
        out_shape=(
            jax.ShapeDtypeStruct((3, pixels), F32),
            jax.ShapeDtypeStruct((3, pixels), F32),
            jax.ShapeDtypeStruct((frames, 4), F32),
        ),
        in_specs=[smem] * 3 + [full] * (chips + 1),
        out_specs=[full] * 3,
        scratch_shapes=[pltpu.VMEM((1, pixels), F32)],
        name="assemble_outputs",
    )(index, frame_kinds, small_params, *pieces)
    bits = 1
    while 2 * bits < replicas:
        half = (half.astype(F32) + swap(half, "dp", replicas, bits).astype(F32)).astype(BF16)
        bits *= 2
    other = swap(half, "dp", replicas, bits) if replicas > 1 else jnp.zeros_like(half)
    other, assembled = lax.optimization_barrier((other, assembled))
    z_out, grad_input, logdet = assembled


    grad, parts = pl.pallas_call(
        functools.partial(norm_kernel, channels=channels),
        out_shape=(
            jax.ShapeDtypeStruct((rows_own, width), F32),
            jax.ShapeDtypeStruct((8, LANES), F32),
        ),
        in_specs=[smem] + [full] * 5,
        out_specs=[full] * 2,
        name="norm_parts",
    )(index, half, other, pack, cols_own, rows)
    pair = parts + swap(parts, "chan", shards, 1)
    totals = [pair[0:1]] + [swap(pair, "chan", shards, 2 * m)[0:1] for m in range(1, chips)]
    totals = jnp.concatenate(totals, axis=0)

    def like(value, dtype=F32):
        return jax.ShapeDtypeStruct(value.shape, dtype)

    arranged_shape = (
        [like(weight1.T)] * 2
        + [jax.ShapeDtypeStruct((rows_own, channels), F32)]
        + [like(weight3)] * 2
        + [like(biases)]
        + [jax.ShapeDtypeStruct((1, rows_own), F32), jax.ShapeDtypeStruct((1, 27), F32)]
        + [jax.ShapeDtypeStruct((1, channels), F32), jax.ShapeDtypeStruct((1, rows_own), F32)]
        + [jax.ShapeDtypeStruct((1, 3), F32), jax.ShapeDtypeStruct((9, rows_own), F32)]
    )
    arranged = pl.pallas_call(
        functools.partial(arrange_kernel, channels=channels),
        out_shape=arranged_shape,
        in_specs=[full] * 3,
        out_specs=[full] * len(arranged_shape),
        name="arrange_gradients",
    )(grad, cols_own, rows)
    vectors = arranged[6:]
    out_shape = (
        [jax.ShapeDtypeStruct((1, 1), F32)]
        + [like(weight1.T)] * 3
        + [like(weight2.T)] * 3
        + [like(weight3)] * 3
        + [like(biases)] * 3
        + [like(small_params)] * 3
        + [like(weight1.T, BF16), like(weight2.T, BF16), like(weight3, BF16)]
    )
    done = pl.pallas_call(
        functools.partial(update_kernel, channels=channels),
        out_shape=out_shape,
        in_specs=[full] * 23,
        out_specs=[full] * len(out_shape),
        name="adam_update",
    )(
        totals, rows, grad, *arranged[:6],
        weight1.T, moment_w1.T, second_w1.T, weight2.T, moment_w2.T, second_w2.T,
        weight3, moment_w3, second_w3, moment_bias, second_bias, small_params, moment_small, second_small,
    )
    norm, updates = done[0], list(done[1:])
    for slot in (0, 1, 2, 3, 4, 5, 15, 16):
        updates[slot] = updates[slot].T
    return (
        z_out,
        logdet,
        grad_input,
        norm.reshape(()),
        *updates,
        vectors[0].reshape(rows_own),
        vectors[1].reshape(27),
        vectors[2].reshape(channels),
        vectors[3].reshape(rows_own),
        vectors[4].reshape(3),
        vectors[5],
    )


def solution(mesh):
    chan_rows = P("chan", None)
    chan_cols = P(None, "chan")
    return jax.shard_map(
        local,
        mesh=mesh,
        in_specs=(
            P(None, "dp"), P("dp"), P("dp", None), P(None, "dp"), P(None, "dp"), P("dp", None),
            chan_rows, chan_cols, chan_cols, chan_cols, P(), P("chan"), P(), P(),
            chan_rows, chan_rows, chan_cols, chan_cols, chan_cols, chan_cols, chan_cols, chan_cols, P(), P(),
        ),
        out_specs=(
            P(None, "dp"), P("dp", None), P(None, "dp"), P(),
            chan_rows, chan_rows, chan_rows, chan_cols, chan_cols, chan_cols, chan_cols, chan_cols, chan_cols,
            chan_cols, chan_cols, chan_cols, P(), P(), P(), chan_rows, chan_cols, chan_cols,
            P("chan"), P(), P(), P("chan"), P(), chan_cols,
        ),
        check_vma=False,
    )
```

```python
import functools

import jax
import jax.numpy as jnp
from jax import lax
from jax.experimental import pallas as pl
from jax.experimental.pallas import tpu as pltpu
from jax.sharding import PartitionSpec as P

NMAX = 4
STEP = 7
SHRINK = 0.98
LR_RATE = 0.05
BETA_ONE = 0.5
BETA_TWO = 0.55
ADAM_EPS = 1e-08
DECAY = 0.01
CLIP_LIMIT = 1.0

WIDTH = 64
FRAME = 4096
BLOCK = 256
HALO = 2 * NMAX * WIDTH
LANES = 128
TAP_ROWS = 72
F32 = jnp.float32
BF16 = jnp.bfloat16
HIGH = lax.Precision.HIGHEST


def iota(shape, dim):
    return lax.broadcasted_iota(jnp.int32, shape, dim)


def dot_nn(left, right, precision=None):
    return lax.dot_general(
        left, right, (((1,), (0,)), ((), ())), precision=precision, preferred_element_type=F32
    )


def dot_nt(left, right, precision=None):
    return lax.dot_general(
        left, right, (((1,), (1,)), ((), ())), precision=precision, preferred_element_type=F32
    )


def dot_tn(left, right, precision=None):
    return lax.dot_general(
        left, right, (((0,), (0,)), ((), ())), precision=precision, preferred_element_type=F32
    )


def spread_one():
    row = iota((27, LANES), 0)
    return (iota((27, LANES), 1) == (row % 9) * 8 + row // 9).astype(F32)


def spread_three():
    row = iota((27, LANES), 0)
    return (iota((27, LANES), 1) == (8 - row % 9) * 8 + 4 + row // 9).astype(F32)


def lane_is_one(lane):
    return (lane % 8 < 3) & (lane < TAP_ROWS)


def lane_is_three(lane):
    return (lane % 8 >= 4) & (lane % 8 < 7) & (lane < TAP_ROWS)


def pack_kernel(w1_ref, w2_ref, w3_ref, bias_ref, u1_ref, out_ref):
    channels = w2_ref.shape[1]
    out_ref[:, 0:channels] = w2_ref[...]
    tile = dot_tn(w1_ref[...], spread_one(), HIGH) + dot_tn(w3_ref[...], spread_three(), HIGH)
    lane = iota((1, LANES), 1)
    for index, row in enumerate((u1_ref[...], bias_ref[0:1, :], bias_ref[1:2, :])):
        column = jnp.broadcast_to(row, (8, row.shape[1])).T[:, 0:1]
        tile = jnp.where(lane == TAP_ROWS + index, column, tile)
    out_ref[:, channels:] = tile


def col_taps(state, masks):
    size = state.shape[1]
    row_up, row_down, col_left, col_right = masks
    left = col_left * pltpu.roll(state, 1, 1)
    right = col_right * pltpu.roll(state, size - 1, 1)
    pieces = []
    for shift_y in (-1, 0, 1):
        for plane in (left, state, right):
            if shift_y == -1:
                plane = row_up * pltpu.roll(plane, WIDTH, 1)
            if shift_y == 1:
                plane = row_down * pltpu.roll(plane, size - WIDTH, 1)
            pieces.append(plane)
    return pieces


def comb_taps(q_ref, lanes, masks):
    size = lanes.size
    row_up, row_down, col_left, col_right = masks
    result = None
    for shift_y in (-1, 0, 1):
        base = 24 * (shift_y + 1)
        line = (
            col_left * pltpu.roll(q_ref[base : base + 8, lanes], 1, 1)
            + q_ref[base + 8 : base + 16, lanes]
            + col_right * pltpu.roll(q_ref[base + 16 : base + 24, lanes], size - 1, 1)
        )
        if shift_y == -1:
            line = row_up * pltpu.roll(line, WIDTH, 1)
        if shift_y == 1:
            line = row_down * pltpu.roll(line, size - WIDTH, 1)
        result = line if result is None else result + line
    return result


def normed_by(values, square):
    return values / jnp.sqrt(square + 1e-12)


def visits(blocks):
    pairs = blocks // 2
    listed = [(2 * (blocks - 1), 2)] if blocks % 2 else []
    return listed + [(4 * j, 4) for j in [pairs - 1] + list(range(pairs - 1)) if pairs]


def margins(uses, valid):
    for extra in range(64):
        for before in range(extra + 1):
            size = extra + valid
            wrong = size < 4
            for first, blocks in uses:
                held = {}
                for at, n in visits(blocks):
                    place = min(max(first + at + before, 0), size - n)
                    for h in range(n):
                        held[place + h] = first + at + h
                wrong = wrong or any(held.get(before + c, c) != c for c in range(valid))
            if not wrong:
                return before, extra - before
    raise ValueError("no margins")


def buffer_plan(own):
    chunks = own // LANES
    blocks = own // BLOCK
    ring = chunks + 2
    return {
        "early": margins([(-4, blocks + 4)], chunks),
        "second": margins([(-3, blocks + 3)], chunks),
        "late": margins([(-2, blocks + 2), (-1, blocks + 1)], chunks),
        "kept": margins([(-2, blocks + 3), (0, blocks + 1), (-1, blocks + 2)], ring),
    }


def main_kernel(index_ref, u3_ref, u2_ref, planes_ref, small_ref, *refs, own, channels, chips):
    packs = refs[: 2 * chips]
    keep_ref, send_ref, og_ref, cols_ref, rows_ref = refs[2 * chips : 2 * chips + 5]
    (
        w_s, w13_s, w2_s, w2t_s, wout_s, bias_s, taps_s, sl1_s, sl2_s, cv1_s, cv2_s,
        lin1a_s, lin2a_s, gt1a_s, gt2a_s, lin1b_s, lin2b_s, gt1b_s, gt2b_s,
        part1_s, part2_s, mid1_s, mid2_s, tan1a_s, tan2a_s, g1a_s, g2a_s, tan1b_s, tan2b_s, g1b_s, g2b_s,
        tan1c_s, tan2c_s, g1c_s, g2c_s, hid1_s, hid2_s,
        q_s, q0_s, comb_s, tile_s, cols_s,
    ) = refs[2 * chips + 5 :]
    me = index_ref[0]
    rows_own = channels // (2 * chips)
    region = own + 2 * HALO
    all_sum = functools.partial(jnp.sum, keepdims=True)

    for shard, ref in enumerate(packs):
        w_s[jnp.bitwise_xor(me, shard)] = ref[...]
    tile = w_s[:, :, channels:].reshape(channels, LANES)
    w2t = w_s[:, :, 0:channels].reshape(channels, channels)
    lane = iota((1, LANES), 1)
    is_one = lane_is_one(lane)
    is_three = lane_is_three(lane)
    taps_one = jnp.where(is_one, tile, 0.0)
    taps_three = jnp.where(is_three, tile, 0.0)
    head = (lane % 8 == 4) & (lane < TAP_ROWS)
    u1 = tile[:, TAP_ROWS : TAP_ROWS + 1]
    u2 = u2_ref[...]
    u3 = jnp.zeros((1, LANES), F32)
    for o in range(3):
        u3 = jnp.where(is_three & (lane % 8 == 4 + o), u3_ref[o], u3)
    for _ in range(2):
        v1 = all_sum(taps_one * u1, axis=0)
        v2 = all_sum(w2t * u2, axis=1)
        mixed = taps_three * u3
        mixed = mixed + pltpu.roll(mixed, LANES - 1, 1) + pltpu.roll(mixed, LANES - 2, 1)
        v3 = jnp.where(head, mixed, 0.0)
        v1 = normed_by(v1, all_sum(v1 * v1))
        v2 = normed_by(v2, all_sum(v2 * v2))
        v3 = normed_by(v3, all_sum(all_sum(v3 * v3, axis=0), axis=1))
        m1 = all_sum(taps_one * v1, axis=1)
        m2 = all_sum(w2t * v2, axis=0)
        spread = v3 + pltpu.roll(v3, 1, 1) + pltpu.roll(v3, 2, 1)
        m3 = all_sum(taps_three * spread, axis=0)
        for shift in (64, 32, 16, 8):
            m3 = m3 + pltpu.roll(m3, shift, 1)
        square1 = all_sum(m1 * m1)
        square2 = all_sum(m2 * m2)
        square3 = all_sum(jnp.where((lane >= 4) & (lane < 7), m3 * m3, 0.0))
        u1 = normed_by(m1, square1)
        u2 = normed_by(m2, square2)
        u3 = jnp.where(is_three, normed_by(m3, square3), 0.0)
    sigma1 = jnp.sqrt(square1)
    sigma2 = jnp.sqrt(square2)
    sigma3 = jnp.sqrt(square3)
    cols_s[...] = jnp.where(lane == 0, u1, jnp.where(lane == 1, v2, v3)).reshape(cols_s.shape)
    cols_ref[...] = cols_s[me]
    sigma_row = jnp.where(lane == 0, sigma1, jnp.where(lane == 1, sigma2, sigma3))
    rows_ref[...] = jnp.zeros(rows_ref.shape, F32)
    rows_ref[0:1, :] = u2
    rows_ref[1:2, 0:LANES] = v1
    rows_ref[2:3, 0:LANES] = u3
    rows_ref[3:4, 0:LANES] = sigma_row

    scaled = taps_one * (SHRINK / sigma1) + taps_three * (SHRINK / sigma3)
    halved = jnp.where(is_one, 0.5 * scaled, 0.0)
    rest1 = 0.5 * tile[:, TAP_ROWS + 1 : TAP_ROWS + 2]
    for i in range(3):
        part = rest1.astype(BF16).astype(F32)
        halved = jnp.where(lane == TAP_ROWS + i, part, halved)
        rest1 = rest1 - part
    w13_s[0:channels] = halved.astype(BF16)
    w13_s[channels:] = jnp.where(is_three, 0.5 * scaled, 0.0).astype(BF16)
    flipped = scaled.T
    blocks = [pltpu.roll(flipped[(8 - t) * 8 : (9 - t) * 8], 4, 0) for t in range(9)]
    flipped = jnp.concatenate(blocks + [jnp.zeros((8, channels), F32)], axis=0)
    first_rows = iota((TAP_ROWS + 8, 1), 0) % 8 < 4
    wout_s[:, 0:channels] = jnp.where(first_rows, flipped, 0.0).astype(BF16)
    wout_s[:, channels:] = jnp.where(first_rows, 0.0, flipped).astype(BF16)
    w2t_scaled = w2t * (0.5 * SHRINK / sigma2)
    w2t_s[...] = w2t_scaled.astype(BF16)
    w2_s[...] = w2t_scaled.T.astype(BF16)
    bias_s[...] = jnp.broadcast_to(0.5 * tile[:, TAP_ROWS + 2 : TAP_ROWS + 3], (channels, LANES))

    shift8 = small_ref[:, 0:1]
    scale8 = small_ref[:, 1:2]
    bias8 = small_ref[:, 2:3]
    extra8 = small_ref[:, 3:4]
    upper = iota((8, 1), 0) >= 4
    probes8 = planes_ref[8:16]
    cot8 = planes_ref[16:24]

    def masks_at(lanes):
        return [planes_ref[32 + i : 33 + i, lanes] for i in range(4)]

    def put_taps(slot, pieces, lanes):
        ones = jnp.where(iota((8, lanes.size), 0) < 3, 1.0 if slot == 0 else 0.0, 0.0)
        full = jnp.concatenate(pieces + [ones], axis=0).astype(BF16)
        for c in range(lanes.size // LANES):
            chunk = lanes.start // LANES + c
            taps_s[slot, chunk] = full[:, c * LANES : (c + 1) * LANES]

    whole = pl.ds(0, region)
    h8 = (planes_ref[0:8] + shift8) * scale8
    sig8 = 0.5 + 0.5 * jnp.tanh(0.5 * h8)
    rest8 = 1.0 - sig8
    slope0 = (sig8 + h8 * sig8 * rest8) / 1.1
    curve0 = sig8 * rest8 * (2.0 + h8 * (1.0 - 2.0 * sig8)) / 1.1
    state = jnp.where(upper, cot8, h8 * sig8 / 1.1)
    put_taps(0, col_taps(state, masks_at(whole)), whole)
    state = probes8 * jnp.where(upper, planes_ref[24 + 7 : 24 + 8], slope0)
    put_taps(1, col_taps(state, masks_at(whole)), whole)

    own_blocks = own // BLOCK
    ring = own + BLOCK
    plan = buffer_plan(own)
    own_before = [plan[name][0] for name in ("early", "second", "late")]
    kept_before = plan["kept"][0]
    tan_s = (
        (tan1a_s, tan2a_s, g1a_s, g2a_s),
        (tan1b_s, tan2b_s, g1b_s, g2b_s),
        (tan1c_s, tan2c_s, g1c_s, g2c_s),
    )
    kept_s = ((lin1a_s, lin2a_s, gt1a_s, gt2a_s), (lin1b_s, lin2b_s, gt1b_s, gt2b_s))

    def over_blocks(count, body, carry=0):
        pairs = count // 2
        if count % 2:
            carry = body((count - 1) * BLOCK, BLOCK, carry)

        def turn(j, kept):
            return body(jnp.where(j == 0, pairs - 1, j - 1) * (2 * BLOCK), 2 * BLOCK, kept)

        return lax.fori_loop(0, pairs, turn, carry)

    def halves(start, size, base, width):
        places = []
        for h in range(size // LANES):
            chunk = start // LANES + h - base // LANES
            chunks = width // LANES
            places.append(jnp.where((chunk >= 0) & (chunk < chunks), chunk, chunks))
        return places

    def run_of(ref, start, size, base, before):
        first = start // LANES - base // LANES + before
        first = jnp.clip(first, 0, ref.shape[0] - size // LANES)
        return [first + h for h in range(size // LANES)]

    def put(ref, places, value):
        for h, place in enumerate(places):
            ref[place] = value[:, h * LANES : (h + 1) * LANES]

    def join(ref, first, count):
        return jnp.concatenate([ref[first + i] for i in range(count)], axis=1)

    def activation(half_act, slope_ref, curve_ref, lanes, ring_places):
        tanh = jnp.tanh(half_act)
        sig = (1.0 / 1.1) + (1.0 / 1.1) * tanh
        hidden = half_act * sig
        bent = tanh * hidden
        slope_ref[:, lanes] = (sig + hidden) - bent
        put(curve_ref, ring_places, ((1.0 - tanh) * (sig - bent)).astype(BF16))
        return hidden.astype(BF16)

    def start_body(at, size, carry):
        start = pl.multiple_of(at, LANES)
        lanes = pl.ds(start, size)
        count = size // LANES
        ring_places = halves(start, size, HALO - LANES, ring)
        own_places = run_of(hid1_s, start, size, HALO, own_before[0])
        act1 = dot_nn(w13_s[0:channels, 0 : TAP_ROWS + 8], join(taps_s.at[0], start // LANES, count))
        hidden1 = activation(act1, sl1_s, cv1_s, lanes, ring_places)
        put(hid1_s, own_places, hidden1)
        act2 = dot_nn(w2_s[...], hidden1)
        bias2 = bias_s[...]
        hidden2 = activation(
            act2 + jnp.concatenate([bias2] * count, axis=1), sl2_s, cv2_s, lanes, ring_places
        )
        put(hid2_s, own_places, hidden2)
        q0_s[:, lanes] = dot_nn(wout_s[:, 0:channels], hidden2)[0:TAP_ROWS]
        return carry

    over_blocks(own_blocks + 4, start_body)


    def series_stage(stage):
        offset = LANES * (stage - 1)
        count = own_blocks + 5 - stage
        tan_slot = min(stage, 3) - 1
        tan_refs = tan_s[tan_slot]

        def body(at, size, carry):
            start = pl.multiple_of(offset + at, LANES)
            lanes = pl.ds(start, size)
            own_places = run_of(tan_refs[0], start, size, HALO, own_before[tan_slot])
            if stage == 1:
                ring_places = halves(start, size, HALO - LANES, ring)
            else:
                ring_places = run_of(mid1_s, start, size, HALO - LANES, kept_before)
            shift = -kept_before if stage == 4 else 0

            def pair_up(value, save_to, partner, add_from, mix_to):
                for h, place in enumerate(ring_places):
                    part = value[:, h * LANES : (h + 1) * LANES]
                    if save_to is not None:
                        save_to[place] = part.astype(BF16)
                        continue
                    part = (part.astype(BF16) * partner[place + shift]).astype(F32)
                    if add_from is not None:
                        part = part + add_from[place].astype(F32)
                    mix_to[place] = part.astype(BF16)

            if stage <= 2:
                lin1_to, lin2_to, gt1_to, gt2_to = kept_s[stage - 1]
                moves = ((lin1_to,), (gt2_to,), (lin2_to,), (gt1_to,))
                moves = [(place, None, None, None) for (place,) in moves]
            else:
                lin1_of, lin2_of, gt1_of, gt2_of = kept_s[4 - stage]
                sum1, sum2 = (None, None) if stage == 3 else (mid1_s, mid2_s)
                end1, end2 = (mid1_s, mid2_s) if stage == 3 else (lin1b_s, lin2b_s)
                moves = (
                    (None, gt1_of, sum1, part1_s),
                    (None, lin2_of, sum2, part2_s),
                    (None, gt2_of, part2_s, end2),
                    (None, lin1_of, part1_s, end1),
                )
            taps = join(taps_s.at[stage], start // LANES, size // LANES)
            lin1 = dot_nn(w13_s[0:channels, 0 : TAP_ROWS + 8], taps)
            tan1 = (sl1_s[:, lanes] * lin1).astype(BF16)
            put(tan_refs[0], own_places, tan1)
            pair_up(lin1, *moves[0])
            gt2 = dot_nn(w13_s[channels:, 0 : TAP_ROWS + 8], taps)
            g2 = (sl2_s[:, lanes] * gt2).astype(BF16)
            put(tan_refs[3], own_places, g2)
            pair_up(gt2, *moves[1])
            lin2 = dot_nn(w2_s[...], tan1)
            tan2 = (sl2_s[:, lanes] * lin2).astype(BF16)
            put(tan_refs[1], own_places, tan2)
            pair_up(lin2, *moves[2])
            gt1 = dot_nn(w2t_s[...], g2)
            g1 = (sl1_s[:, lanes] * gt1).astype(BF16)
            put(tan_refs[2], own_places, g1)
            pair_up(gt1, *moves[3])
            q_fwd = dot_nn(wout_s[:, 0:channels], tan2)[0:TAP_ROWS]
            q_s[:, lanes] = q_fwd + dot_nn(wout_s[:, channels:], g1)[0:TAP_ROWS]
            return carry

        over_blocks(count, body)

        inside = pl.ds(offset, count * BLOCK)
        result = comb_taps(q_s, inside, masks_at(inside))
        core_from = HALO - offset
        comb_s[stage - 1] = result[:, core_from : core_from + own]
        if stage < NMAX:
            nxt = result[:, LANES : count * BLOCK - LANES]
            lanes = pl.ds(offset + LANES, (count - 1) * BLOCK)
            seed = probes8[:, offset + LANES : offset + LANES + (count - 1) * BLOCK]
            coef = planes_ref[24 + 4 + 3 - stage : 24 + 4 + 4 - stage, lanes]
            following = slope0[:, offset + LANES : offset + LANES + (count - 1) * BLOCK] * nxt
            following = following + jnp.where(upper, seed * coef, 0.0)
            put_taps(stage + 1, col_taps(following, masks_at(lanes)), lanes)

    def own_taps(slot):
        return join(taps_s.at[slot], HALO // LANES, own // LANES)

    def add_weight_grads(slot_pairs, tap_pairs, first):
        total = None
        for left, right in slot_pairs:
            part = dot_nt(left, right)
            total = part if total is None else total + part
        one = None
        three = None
        for left_one, left_three, slot in tap_pairs:
            taps = own_taps(slot)
            part_one = dot_nt(taps, left_one)
            part_three = dot_nt(taps, left_three)
            one = part_one if one is None else one + part_one
            three = part_three if three is None else three + part_three
        w2_part = total.reshape(2 * chips, rows_own, channels)
        tile_part = jnp.where(first_rows, one, three)
        if first:
            w_s[:, :, 0:channels] = w2_part
            tile_s[...] = tile_part
        else:
            w_s[:, :, 0:channels] = w_s[:, :, 0:channels] + w2_part
            tile_s[...] = tile_s[...] + tile_part

    def slot_of(kind, slot):
        return join(tan_s[slot][kind], own_before[slot], own // LANES)

    series_stage(1)
    series_stage(2)
    series_stage(3)
    add_weight_grads(
        ((slot_of(0, 1), slot_of(3, 2)), (slot_of(0, 2), slot_of(3, 1))),
        (
            (slot_of(2, 2), slot_of(1, 2), 2),
            (slot_of(2, 1), slot_of(1, 1), 3),
        ),
        True,
    )
    series_stage(4)
    add_weight_grads(
        ((slot_of(0, 0), slot_of(3, 2)), (slot_of(0, 2), slot_of(3, 0))),
        (
            (slot_of(2, 2), slot_of(1, 2), 1),
            (slot_of(2, 0), slot_of(1, 0), 4),
        ),
        False,
    )

    def final_body(at, size, carry):
        bias_one, bias_two = carry
        start = pl.multiple_of(HALO - LANES + at, LANES)
        lanes = pl.ds(start, size)
        count = size // LANES
        ring_from = at // LANES
        own_places = run_of(g1c_s, start, size, HALO, own_before[2])
        gs2 = dot_nn(w13_s[channels:, 0 : TAP_ROWS + 8], join(taps_s.at[0], start // LANES, count))
        acc2 = join(cv2_s, ring_from, count).astype(F32) * join(lin2b_s, ring_from + kept_before, count).astype(F32)
        ga2 = (acc2 + acc2) + sl2_s[:, lanes] * gs2
        low2 = ga2.astype(BF16)
        gs1 = dot_nn(w2t_s[...], low2)
        acc1 = join(cv1_s, ring_from, count).astype(F32) * join(lin1b_s, ring_from + kept_before, count).astype(F32)
        ga1 = (acc1 + acc1) + sl1_s[:, lanes] * gs1
        low1 = ga1.astype(BF16)
        q_s[:, lanes] = q0_s[:, lanes] + dot_nn(wout_s[:, channels:], low1)[0:TAP_ROWS]
        put(g2c_s, own_places, low2)
        put(g1c_s, own_places, low1)
        for c in range(count):
            chunk = (start - HALO) // LANES + c
            here = jnp.where((chunk >= 0) & (chunk < own // LANES), 1.0, 0.0)
            bias_one = bias_one + here * ga1[:, c * LANES : (c + 1) * LANES]
            bias_two = bias_two + here * ga2[:, c * LANES : (c + 1) * LANES]
        return bias_one, bias_two

    zero = jnp.zeros((channels, LANES), F32)
    bias_one, bias_two = over_blocks(own_blocks + 1, final_body, (zero, zero))
    add_weight_grads(
        ((join(hid1_s, own_before[0], own // LANES), slot_of(3, 2)),), ((slot_of(2, 2), join(hid2_s, own_before[0], own // LANES), 0),), False
    )

    inside = pl.ds(HALO - LANES, own + BLOCK)
    result = comb_taps(q_s, inside, masks_at(inside))[:, LANES : LANES + own]
    mine = slice(HALO, HALO + own)
    h_own = h8[:, mine]
    cot_own = cot8[:, mine]
    probes_own = probes8[:, mine]
    mixed = comb_s[0] * pltpu.roll(comb_s[2], 4, 0)
    mixed = mixed + comb_s[1] * pltpu.roll(comb_s[1], 4, 0)
    mixed = mixed + comb_s[2] * pltpu.roll(comb_s[0], 4, 0)
    mixed = mixed + comb_s[3] * probes_own
    grad_h = cot_own + slope0[:, mine] * result + curve0[:, mine] * mixed
    grad_in = grad_h * scale8
    density = planes_ref[24:25, mine] * comb_s[0]
    for k in range(1, NMAX):
        density = density + planes_ref[24 + k : 25 + k, mine] * comb_s[k]
    density = density * probes_own
    density = density[0:1] + density[1:2] + density[2:3]
    row8 = iota((8, 1), 0)
    high = density.astype(BF16).astype(F32)
    out = jnp.where(row8 < 3, h_own + result + bias8, jnp.where(row8 == 3, high, grad_in))
    out = jnp.where(row8 == 7, density - high, out)
    if own < channels:
        out = jnp.concatenate([out, jnp.zeros((8, channels - own), F32)], axis=1)
    lines = [out[:, c * channels : (c + 1) * channels] for c in range(out.shape[1] // channels)]
    if len(lines) == 1:
        lines.append(jnp.zeros((8, channels), F32))
    out = jnp.concatenate(lines, axis=0).astype(BF16)
    og_ref[...] = jnp.zeros(og_ref.shape, BF16)
    og_ref[:, 0:channels] = out
    send_ref[chips * rows_own :, 0:channels] = out
    send_ref[chips * rows_own :, channels:] = jnp.zeros((out.shape[0], LANES), BF16)

    sums = (
        all_sum(grad_in, axis=1),
        all_sum(grad_h * h_own, axis=1) + extra8,
        all_sum(cot_own, axis=1),
    )
    small_row = jnp.zeros((1, LANES), F32)
    for a, column in enumerate(sums):
        for i in range(3):
            small_row = jnp.where(lane == TAP_ROWS + 2 + 3 * a + i, column[4 + i : 5 + i], small_row)
    bias_one = all_sum(bias_one, axis=1)
    bias_two = all_sum(bias_two, axis=1)
    extras = jnp.where(lane == TAP_ROWS, bias_one, jnp.where(lane == TAP_ROWS + 1, bias_two, small_row))
    blank = jnp.zeros((LANES - TAP_ROWS - 8, channels), F32)
    flat = jnp.concatenate([tile_s[...], blank], axis=0).T
    extras = jnp.where(lane < TAP_ROWS, flat, extras)
    w_s[:, :, channels:] = extras.reshape(2 * chips, rows_own, LANES)

    core = jnp.bitwise_and(me, 1)
    chip = jnp.right_shift(me, 1)
    for m in range(chips):
        block = 2 * jnp.bitwise_xor(chip, m)
        keep_ref[m] = w_s[block + core]
        send_ref[m * rows_own : (m + 1) * rows_own] = w_s[block + 1 - core].astype(BF16)


def output_rows(own, channels):
    return max(8 * (own // channels), 16)


def call_main(me, u3, u2, planes, small, packs, own, channels, chips):
    rows_own = channels // (2 * chips)
    region = own + 2 * HALO
    wide = (own + BLOCK) // LANES + 1
    width = channels + LANES
    out_shape = (
        pltpu.VMEM((chips, rows_own, width), F32),
        pltpu.VMEM((chips * rows_own + output_rows(own, channels), width), BF16),
        pltpu.VMEM((output_rows(own, channels), width), BF16),
        pltpu.VMEM((rows_own, LANES), F32),
        pltpu.VMEM((8, channels), F32),
    )
    vmem = pltpu.VMEM
    plan = buffer_plan(own)

    def buffer(name, lanes):
        return vmem((lanes // LANES + sum(plan[name]), channels, LANES), BF16)

    scratch = [
        vmem((2 * chips, rows_own, width), F32),
        vmem((2 * channels, LANES), BF16),
        vmem((channels, channels), BF16),
        vmem((channels, channels), BF16),
        vmem((TAP_ROWS + 8, 2 * channels), BF16),
        vmem((channels, LANES), F32),
        vmem((NMAX + 1, region // LANES, TAP_ROWS + 8, LANES), BF16),
        vmem((channels, region), F32),
        vmem((channels, region), F32),
        *[vmem((wide, channels, LANES), BF16)] * 6,
        *[buffer("kept", own + BLOCK)] * 8,
        *[buffer("early", own)] * 4,
        *[buffer("second", own)] * 4,
        *[buffer("late", own)] * 4,
        *[buffer("early", own)] * 2,
        vmem((TAP_ROWS, region), F32),
        vmem((TAP_ROWS, region), F32),
        vmem((NMAX, 8, own), F32),
        vmem((TAP_ROWS + 8, channels), F32),
        vmem((2 * chips, rows_own, LANES), F32),
    ]
    full = pl.BlockSpec(memory_space=pltpu.VMEM)
    return pl.pallas_call(
        functools.partial(main_kernel, own=own, channels=channels, chips=chips),
        out_shape=out_shape,
        in_specs=[pl.BlockSpec(memory_space=pltpu.SMEM)] * 2 + [full] * (3 + 2 * chips),
        out_specs=[full] * 5,
        scratch_shapes=scratch,
        compiler_params=pltpu.CompilerParams(vmem_limit_bytes=61 * 1024 * 1024),
        name="flow_block",
    )(me, u3, u2, planes, small, *packs)


def assemble_kernel(index_ref, kinds_ref, small_ref, *refs, own, channels, chips, frames):
    pieces = refs[: chips + 1]
    z_ref, gin_ref, logdet_ref, dens_s = refs[chips + 1 :]
    me = index_ref[0]
    lines = max(own // channels, 1)
    size = min(own, channels)
    rows = output_rows(own, channels)
    for m in range(chips):
        for b in range(2):
            shard = jnp.bitwise_xor(me, 2 * m + b)
            if m == 0:
                block = pieces[b][...]
            else:
                message = pieces[m + 1]
                first = message.shape[0] - (2 - b) * rows
                block = message[first : first + rows]
            block = block.astype(F32)
            for c in range(lines):
                lanes = pl.ds(pl.multiple_of(shard * own + c * size, LANES), size)
                piece = block[8 * c : 8 * c + 8, 0:size]
                z_ref[:, lanes] = piece[0:3]
                gin_ref[:, lanes] = piece[4:7]
                dens_s[:, lanes] = piece[3:4] + piece[7:8]
    scale_sum = small_ref[1, 0] + small_ref[1, 1] + small_ref[1, 2]
    pixel = iota((1, FRAME), 1)
    bottom = (pixel // (WIDTH * 32)) % 2
    right = (pixel // 32) % 2
    lane = iota((1, 4), 1)
    for f in range(frames):
        line = dens_s[:, f * FRAME : (f + 1) * FRAME]
        quads = jnp.zeros((1, 4), F32)
        total = jnp.zeros((1, 1), F32)
        for slot in range(4):
            picked = jnp.where(bottom * 2 + right == slot, line, 0.0)
            picked = jnp.sum(picked, axis=1, keepdims=True)
            quads = jnp.where(lane == slot, picked, quads)
            total = total + picked
        split = kinds_ref[f] == 2
        whole = jnp.where(lane == 0, total + 4096.0 * scale_sum, 0.0)
        logdet_ref[f : f + 1, :] = jnp.where(split, quads + 1024.0 * scale_sum, whole)


def norm_kernel(index_ref, a_ref, b_ref, pack_ref, cols_ref, rows_ref, grad_ref, out_ref, *, channels):
    grad = a_ref[...].astype(F32) + b_ref[...].astype(F32)
    grad_ref[...] = grad
    lane = iota((1, LANES), 1)
    is_one = lane_is_one(lane)
    is_three = lane_is_three(lane)
    tile = grad[:, channels:]
    weights = pack_ref[:, channels:]
    cols = cols_ref[...]
    u1 = cols[:, 0:1]
    v2 = cols[:, 1:2]
    spread = jnp.where((lane % 8 == 4) & (lane < TAP_ROWS), cols, 0.0)
    spread = spread + pltpu.roll(spread, 1, 1) + pltpu.roll(spread, 2, 1)
    outer_one = u1 * rows_ref[1:2, 0:LANES]
    outer_three = spread * rows_ref[2:3, 0:LANES]
    outer_two = v2 * rows_ref[0:1, :]
    grad_two = grad[:, 0:channels]
    weight_two = pack_ref[:, 0:channels]

    def total(values):
        return jnp.sum(jnp.sum(values, axis=0, keepdims=True), axis=1, keepdims=True)

    bias = (lane == TAP_ROWS) | (lane == TAP_ROWS + 1)
    parts = (
        total(jnp.where(is_one, tile * tile, 0.0)),
        total(grad_two * grad_two),
        total(jnp.where(is_three, tile * tile, 0.0)),
        total(jnp.where(is_one, tile * weights, 0.0)),
        total(grad_two * weight_two),
        total(jnp.where(is_three, tile * weights, 0.0)),
        total(jnp.where(is_one, tile * outer_one, 0.0)),
        total(grad_two * outer_two),
        total(jnp.where(is_three, tile * outer_three, 0.0)),
        total(jnp.where(is_one, outer_one * outer_one, 0.0)),
        total(outer_two * outer_two),
        total(jnp.where(is_three, outer_three * outer_three, 0.0)),
        total(jnp.where(bias, tile * tile, 0.0)),
    )
    row = jnp.zeros((1, LANES), F32)
    for index, part in enumerate(parts):
        row = jnp.where(lane == index, part, row)
    small = (lane >= TAP_ROWS + 2) & (lane < TAP_ROWS + 11) & (index_ref[0] == 0)
    row = jnp.where(small, tile[0:1], row)
    out_ref[...] = jnp.broadcast_to(row, out_ref.shape)


def moment_step(grad, moment, second):
    new_moment = BETA_ONE * moment + (1.0 - BETA_ONE) * grad
    new_second = BETA_TWO * second + (1.0 - BETA_TWO) * grad * grad
    return (new_moment, new_second)


def adam_step(param, grad, moment, second):
    new_moment, new_second = moment_step(grad, moment, second)
    fix_one = 1.0 - BETA_ONE**STEP
    fix_two = 1.0 - BETA_TWO**STEP
    update = new_moment / fix_one / (jnp.sqrt(new_second / fix_two) + ADAM_EPS) + DECAY * param
    return (param - LR_RATE * update, new_moment, new_second)


def arrange_kernel(
    grad_ref, cols_ref, rows_ref,
    g1_out, o1_out, o2_out, g3_out, o3_out, bias_out, u1_out, v1_out, u2_out, v2_out, u3_out, v3_out, *, channels,
):
    lane = iota((1, LANES), 1)
    cols = cols_ref[...]
    tile = grad_ref[:, channels:]
    is_one = lane_is_one(lane)
    is_three = lane_is_three(lane)
    spread = jnp.where((lane % 8 == 4) & (lane < TAP_ROWS), cols, 0.0)
    spread = spread + pltpu.roll(spread, 1, 1) + pltpu.roll(spread, 2, 1)
    outer_one = jnp.where(is_one, cols[:, 0:1] * rows_ref[1:2, 0:LANES], 0.0)
    outer_three = jnp.where(is_three, spread * rows_ref[2:3, 0:LANES], 0.0)
    o2_out[...] = cols[:, 1:2] * rows_ref[0:1, :]
    g1_out[...] = dot_nt(spread_one(), jnp.where(is_one, tile, 0.0), HIGH)
    o1_out[...] = dot_nt(spread_one(), outer_one, HIGH)
    g3_out[...] = dot_nt(spread_three(), jnp.where(is_three, tile, 0.0), HIGH)
    o3_out[...] = dot_nt(spread_three(), outer_three, HIGH)
    bias_out[...] = tile.T[TAP_ROWS : TAP_ROWS + 2, :]
    flipped = cols.T
    u1_out[...] = flipped[0:1]
    v2_out[...] = flipped[1:2]
    tap = iota((9, LANES), 0)
    select = (iota((9, LANES), 1) == (8 - tap) * 8 + 4).astype(F32)
    v3_out[...] = dot_nn(select, flipped, HIGH)
    v1_out[...] = dot_nt(rows_ref[1:2, 0:LANES], spread_one(), HIGH)
    u2_out[...] = rows_ref[0:1, :]
    u3_out[...] = rows_ref[2:3, 4:7]


def update_kernel(
    totals_ref, rows_ref, grad_ref, g1_ref, o1_ref, o2_ref, g3_ref, o3_ref, bias_ref,
    w1_ref, m1_ref, s1_ref, w2_ref, m2_ref, s2_ref, w3_ref, m3_ref, s3_ref,
    mb_ref, sb_ref, small_ref, msmall_ref, ssmall_ref,
    norm_out, nw1, nm1, ns1, nw2, nm2, ns2, nw3, nm3, ns3, cb, nmb, nsb, nsm, nmsm, nssm, lw1, lw2, lw3, *, channels,
):
    lane = iota((1, LANES), 1)
    lines = [totals_ref[m : m + 1] for m in range(totals_ref.shape[0])]
    while len(lines) > 1:
        lines = [lines[m] + lines[m + 1] for m in range(0, len(lines), 2)]
    row = lines[0]

    def pick(index):
        return row[:, index : index + 1]

    small_row = jnp.where((lane >= TAP_ROWS + 2) & (lane < TAP_ROWS + 11), row, 0.0)
    square = pick(12) + jnp.sum(small_row * small_row, axis=1, keepdims=True)
    scales = []
    for j in range(3):
        sigma = rows_ref[3:4, j : j + 1]
        ratio = SHRINK / sigma
        factor = pick(3 + j) / sigma
        fixed = pick(j) - 2.0 * factor * pick(6 + j) + factor * factor * pick(9 + j)
        square = square + ratio * ratio * jnp.maximum(fixed, 0.0)
        scales.append((ratio, factor))
    norm = jnp.sqrt(square)
    norm_out[...] = norm
    clip = jnp.minimum(1.0, CLIP_LIMIT / (norm + 1e-06))

    for index, grad, outer, w_ref, m_ref, s_ref, nw, nm, ns, lw in (
        (0, g1_ref[...], o1_ref, w1_ref, m1_ref, s1_ref, nw1, nm1, ns1, lw1),
        (1, grad_ref[:, 0:channels], o2_ref, w2_ref, m2_ref, s2_ref, nw2, nm2, ns2, lw2),
        (2, g3_ref[...], o3_ref, w3_ref, m3_ref, s3_ref, nw3, nm3, ns3, lw3),
    ):
        ratio, factor = scales[index]
        fixed = (clip * ratio) * (grad - factor * outer[...])
        new, moment, second = adam_step(w_ref[...], fixed, m_ref[...], s_ref[...])
        nw[...] = new
        nm[...] = moment
        ns[...] = second
        lw[...] = new.astype(BF16)

    bias = bias_ref[...] * clip
    cb[...] = bias
    moment, second = moment_step(bias, mb_ref[...], sb_ref[...])
    nmb[...] = moment
    nsb[...] = second

    small_row = small_row * clip
    lane3 = iota((1, 3), 1)
    rows = []
    for a in range(3):
        line = jnp.zeros((1, 3), F32)
        for i in range(3):
            at = TAP_ROWS + 2 + 3 * a + i
            line = jnp.where(lane3 == i, small_row[:, at : at + 1], line)
        rows.append(line)
    small_grad = jnp.concatenate(rows, axis=0)
    new, moment, second = adam_step(small_ref[...], small_grad, msmall_ref[...], ssmall_ref[...])
    nsm[...] = new
    nmsm[...] = moment
    nssm[...] = second


def prepare_kernel(
    index_ref, kinds_ref, len_ref, cot_ref, params_ref, images_ref, probes_ref, cot_z_ref,
    planes_ref, small_ref, *, own, frames,
):
    region = planes_ref.shape[1]
    pixels = images_ref.shape[1]
    me = index_ref[0]
    first = me * own - HALO
    planes_ref[...] = jnp.zeros(planes_ref.shape, F32)
    for chunk in range(region // LANES):
        start = first + chunk * LANES
        source = pl.ds(pl.multiple_of(jnp.clip(start, 0, pixels - LANES), LANES), LANES)
        lanes = pl.ds(chunk * LANES, LANES)
        inside = (start >= 0) & (start < pixels)
        for row, ref in ((0, images_ref), (4, images_ref), (8, probes_ref), (12, probes_ref), (20, cot_z_ref)):
            planes_ref[row : row + 3, lanes] = jnp.where(inside, ref[:, source], 0.0)

    position = first + iota((1, region), 1)
    frame = jnp.right_shift(position, 12)
    pixel = jnp.bitwise_and(position, FRAME - 1)
    row = jnp.right_shift(pixel, 6)
    col = jnp.bitwise_and(pixel, WIDTH - 1)
    half = WIDTH // 2
    quad = 2 * jnp.right_shift(row, 5) + jnp.right_shift(col, 5)
    split = jnp.zeros((1, region), jnp.int32)
    for f in range(frames):
        split = jnp.where(frame == f, jnp.where(kinds_ref[f] == 2, 1, 0), split)
    slot = 4 * frame + jnp.where(split == 1, quad, 0)
    length = jnp.zeros((1, region), jnp.int32)
    weight = jnp.zeros((1, region), F32)
    for f in range(frames):
        for q in range(4):
            here = slot == 4 * f + q
            length = jnp.where(here, len_ref[f, q], length)
            weight = jnp.where(here, cot_ref[f, q], weight)
    for k in range(NMAX):
        coef = jnp.where(length >= k + 1, (-1.0) ** k / (k + 1), 0.0)
        planes_ref[24 + k : 25 + k] = coef
        planes_ref[24 + NMAX + k : 25 + NMAX + k] = coef * weight
    for index, line in enumerate((row, col)):
        low = (line == 0) | ((split == 1) & (line == half))
        high = (line == WIDTH - 1) | ((split == 1) & (line == half - 1))
        planes_ref[32 + 2 * index : 33 + 2 * index] = jnp.where(low, 0.0, 1.0)
        planes_ref[33 + 2 * index : 34 + 2 * index] = jnp.where(high, 0.0, 1.0)

    extra = jnp.float32(0.0)
    for f in range(frames):
        whole = 4096.0 * cot_ref[f, 0]
        quads = 1024.0 * (cot_ref[f, 0] + cot_ref[f, 1] + cot_ref[f, 2] + cot_ref[f, 3])
        extra = extra + jnp.where(kinds_ref[f] == 2, quads, whole)
    extra = jnp.where(me == 0, extra, 0.0)
    row8 = iota((8, LANES), 0)
    lane = iota((8, LANES), 1)
    values = []
    for a in range(3):
        value = jnp.zeros((8, LANES), F32)
        for i in range(3):
            value = jnp.where(row8 % 4 == i, params_ref[a, i], value)
        values.append(value)
    result = jnp.where(lane == 0, values[0], jnp.where(lane == 1, jnp.exp(values[1]), values[2]))
    small_ref[...] = jnp.where(row8 % 4 == 3, 0.0, jnp.where(lane == 3, extra, result))


def local(
    images, frame_kinds, series_len, probes, cot_z, cot_logdet, weight1, weight2, weight3, biases,
    small_params, power_u1, power_u2, power_u3, moment_w1, second_w1, moment_w2, second_w2,
    moment_w3, second_w3, moment_bias, second_bias, moment_small, second_small,
):
    shards = lax.axis_size("chan")
    replicas = lax.axis_size("dp")
    chips = shards // 2
    me = lax.axis_index("chan")
    channels = weight2.shape[0]
    rows_own = weight1.shape[0]
    pixels = images.shape[1]
    frames = frame_kinds.shape[0]
    own = pixels // shards
    width = channels + LANES
    full = pl.BlockSpec(memory_space=pltpu.VMEM)
    smem = pl.BlockSpec(memory_space=pltpu.SMEM)
    index = me.reshape(1).astype(jnp.int32)

    def near_memory(values):
        return pltpu.with_memory_space_constraint(values, pltpu.VMEM)

    def swap(values, axis, size, bits):
        return lax.ppermute(values, axis, [(j, j ^ bits) for j in range(size)])

    pack = pl.pallas_call(
        pack_kernel,
        out_shape=pltpu.VMEM((rows_own, width), F32),
        in_specs=[full] * 5,
        out_specs=full,
        name="pack_weights",
    )(weight1.T, weight2.T, weight3, biases, power_u1.reshape(1, rows_own))
    near = [pack] + [swap(pack, "chan", shards, 2 * m) for m in range(1, chips)]
    planes, small = pl.pallas_call(
        functools.partial(prepare_kernel, own=own, frames=frames),
        out_shape=(
            pltpu.VMEM((40, own + 2 * HALO), F32),
            pltpu.VMEM((8, LANES), F32),
        ),
        in_specs=[smem] * 5 + [full] * 3,
        out_specs=[full] * 2,
        name="prepare_planes",
    )(index, frame_kinds, series_len, cot_logdet, small_params, images, probes, cot_z)

    near[-1], planes = lax.optimization_barrier((near[-1], planes))
    packs = []
    for values in near:
        packs += [values, swap(values, "chan", shards, 1)]

    keep, send, og, cols_own, rows = call_main(
        index, power_u3, power_u2.reshape(1, channels), near_memory(planes), near_memory(small),
        [near_memory(values) for values in packs], own, channels, chips
    )

    got = swap(send, "chan", shards, 1)
    og_other = got[chips * rows_own :]
    summed = keep + got[: chips * rows_own].reshape(keep.shape).astype(F32)
    total = summed[0]
    pieces = [og, og_other]
    for m in range(1, chips):
        message = jnp.concatenate([summed[m].astype(BF16), og, og_other], axis=0)
        message = swap(message, "chan", shards, 2 * m)
        total = total + message[:rows_own].astype(F32)
        pieces.append(message)
    half = total.astype(BF16)
    assembled = pl.pallas_call(
        functools.partial(assemble_kernel, own=own, channels=channels, chips=chips, frames=frames),
        out_shape=(
            jax.ShapeDtypeStruct((3, pixels), F32),
            jax.ShapeDtypeStruct((3, pixels), F32),
            jax.ShapeDtypeStruct((frames, 4), F32),
        ),
        in_specs=[smem] * 3 + [full] * (chips + 1),
        out_specs=[full] * 3,
        scratch_shapes=[pltpu.VMEM((1, pixels), F32)],
        name="assemble_outputs",
    )(index, frame_kinds, small_params, *[near_memory(piece) for piece in pieces])
    bits = 1
    while 2 * bits < replicas:
        half = (half.astype(F32) + swap(half, "dp", replicas, bits).astype(F32)).astype(BF16)
        bits *= 2
    other = swap(half, "dp", replicas, bits) if replicas > 1 else jnp.zeros_like(half)
    other, assembled = lax.optimization_barrier((other, assembled))
    z_out, grad_input, logdet = assembled


    grad, parts = pl.pallas_call(
        functools.partial(norm_kernel, channels=channels),
        out_shape=(
            pltpu.VMEM((rows_own, width), F32),
            pltpu.VMEM((8, LANES), F32),
        ),
        in_specs=[smem] + [full] * 5,
        out_specs=[full] * 2,
        name="norm_parts",
    )(index, near_memory(half), near_memory(other), near_memory(pack), near_memory(cols_own), near_memory(rows))
    pair = parts + swap(parts, "chan", shards, 1)
    totals = [pair[0:1]] + [swap(pair, "chan", shards, 2 * m)[0:1] for m in range(1, chips)]
    totals = jnp.concatenate(totals, axis=0)

    def like(value, dtype=F32):
        return jax.ShapeDtypeStruct(value.shape, dtype)

    arranged_shape = (
        [pltpu.VMEM(weight1.T.shape, F32)] * 2
        + [pltpu.VMEM((rows_own, channels), F32)]
        + [pltpu.VMEM(weight3.shape, F32)] * 2
        + [pltpu.VMEM(biases.shape, F32)]
        + [jax.ShapeDtypeStruct((1, rows_own), F32), jax.ShapeDtypeStruct((1, 27), F32)]
        + [jax.ShapeDtypeStruct((1, channels), F32), jax.ShapeDtypeStruct((1, rows_own), F32)]
        + [jax.ShapeDtypeStruct((1, 3), F32), jax.ShapeDtypeStruct((9, rows_own), F32)]
    )
    arranged = pl.pallas_call(
        functools.partial(arrange_kernel, channels=channels),
        out_shape=arranged_shape,
        in_specs=[full] * 3,
        out_specs=[full] * len(arranged_shape),
        name="arrange_gradients",
    )(near_memory(grad), near_memory(cols_own), near_memory(rows))
    vectors = arranged[6:]
    out_shape = (
        [jax.ShapeDtypeStruct((1, 1), F32)]
        + [like(weight1.T)] * 3
        + [like(weight2.T)] * 3
        + [like(weight3)] * 3
        + [like(biases)] * 3
        + [like(small_params)] * 3
        + [like(weight1.T, BF16), like(weight2.T, BF16), like(weight3, BF16)]
    )
    done = pl.pallas_call(
        functools.partial(update_kernel, channels=channels),
        out_shape=out_shape,
        in_specs=[full] * 23,
        out_specs=[full] * len(out_shape),
        name="adam_update",
    )(
        *[near_memory(values) for values in (totals, rows, grad, *arranged[:6])],
        weight1.T, moment_w1.T, second_w1.T, weight2.T, moment_w2.T, second_w2.T,
        weight3, moment_w3, second_w3, moment_bias, second_bias, small_params, moment_small, second_small,
    )
    norm, updates = done[0], list(done[1:])
    for slot in (0, 1, 2, 3, 4, 5, 15, 16):
        updates[slot] = updates[slot].T
    return (
        z_out,
        logdet,
        grad_input,
        norm.reshape(()),
        *updates,
        vectors[0].reshape(rows_own),
        vectors[1].reshape(27),
        vectors[2].reshape(channels),
        vectors[3].reshape(rows_own),
        vectors[4].reshape(3),
        vectors[5],
    )


def solution(mesh):
    chan_rows = P("chan", None)
    chan_cols = P(None, "chan")
    return jax.shard_map(
        local,
        mesh=mesh,
        in_specs=(
            P(None, "dp"), P("dp"), P("dp", None), P(None, "dp"), P(None, "dp"), P("dp", None),
            chan_rows, chan_cols, chan_cols, chan_cols, P(), P("chan"), P(), P(),
            chan_rows, chan_rows, chan_cols, chan_cols, chan_cols, chan_cols, chan_cols, chan_cols, P(), P(),
        ),
        out_specs=(
            P(None, "dp"), P("dp", None), P(None, "dp"), P(),
            chan_rows, chan_rows, chan_rows, chan_cols, chan_cols, chan_cols, chan_cols, chan_cols, chan_cols,
            chan_cols, chan_cols, chan_cols, P(), P(), P(), chan_rows, chan_cols, chan_cols,
            P("chan"), P(), P(), P("chan"), P(), chan_cols,
        ),
        check_vma=False,
    )
```

```python
import functools

import jax
import jax.numpy as jnp
from jax import lax
from jax.experimental import pallas as pl
from jax.experimental.pallas import tpu as pltpu
from jax.sharding import PartitionSpec as P

NMAX = 4
STEP = 7
SHRINK = 0.98
LR_RATE = 0.05
BETA_ONE = 0.5
BETA_TWO = 0.55
ADAM_EPS = 1e-08
DECAY = 0.01
CLIP_LIMIT = 1.0

WIDTH = 64
FRAME = 4096
BLOCK = 256
HALO = 2 * NMAX * WIDTH
LANES = 128
TAP_ROWS = 72
F32 = jnp.float32
BF16 = jnp.bfloat16
HIGH = lax.Precision.HIGHEST


def iota(shape, dim):
    return lax.broadcasted_iota(jnp.int32, shape, dim)


def dot_nn(left, right, precision=None):
    return lax.dot_general(
        left, right, (((1,), (0,)), ((), ())), precision=precision, preferred_element_type=F32
    )


def dot_nt(left, right, precision=None):
    return lax.dot_general(
        left, right, (((1,), (1,)), ((), ())), precision=precision, preferred_element_type=F32
    )


def dot_tn(left, right, precision=None):
    return lax.dot_general(
        left, right, (((0,), (0,)), ((), ())), precision=precision, preferred_element_type=F32
    )


def spread_one():
    row = iota((27, LANES), 0)
    return (iota((27, LANES), 1) == (row % 9) * 8 + row // 9).astype(F32)


def spread_three():
    row = iota((27, LANES), 0)
    return (iota((27, LANES), 1) == (8 - row % 9) * 8 + 4 + row // 9).astype(F32)


def lane_is_one(lane):
    return (lane % 8 < 3) & (lane < TAP_ROWS)


def lane_is_three(lane):
    return (lane % 8 >= 4) & (lane % 8 < 7) & (lane < TAP_ROWS)


def pack_kernel(w1_ref, w2_ref, w3_ref, bias_ref, u1_ref, out_ref):
    channels = w2_ref.shape[1]
    out_ref[:, 0:channels] = w2_ref[...]
    tile = dot_tn(w1_ref[...], spread_one(), HIGH) + dot_tn(w3_ref[...], spread_three(), HIGH)
    lane = iota((1, LANES), 1)
    for index, row in enumerate((u1_ref[...], bias_ref[0:1, :], bias_ref[1:2, :])):
        column = jnp.broadcast_to(row, (8, row.shape[1])).T[:, 0:1]
        tile = jnp.where(lane == TAP_ROWS + index, column, tile)
    out_ref[:, channels:] = tile


def col_taps(state, masks):
    size = state.shape[1]
    row_up, row_down, col_left, col_right = masks
    left = col_left * pltpu.roll(state, 1, 1)
    right = col_right * pltpu.roll(state, size - 1, 1)
    pieces = []
    for shift_y in (-1, 0, 1):
        for plane in (left, state, right):
            if shift_y == -1:
                plane = row_up * pltpu.roll(plane, WIDTH, 1)
            if shift_y == 1:
                plane = row_down * pltpu.roll(plane, size - WIDTH, 1)
            pieces.append(plane)
    return pieces


def comb_taps(q_ref, lanes, masks):
    size = lanes.size
    row_up, row_down, col_left, col_right = masks
    result = None
    for shift_y in (-1, 0, 1):
        base = 24 * (shift_y + 1)
        line = (
            col_left * pltpu.roll(q_ref[base : base + 8, lanes], 1, 1)
            + q_ref[base + 8 : base + 16, lanes]
            + col_right * pltpu.roll(q_ref[base + 16 : base + 24, lanes], size - 1, 1)
        )
        if shift_y == -1:
            line = row_up * pltpu.roll(line, WIDTH, 1)
        if shift_y == 1:
            line = row_down * pltpu.roll(line, size - WIDTH, 1)
        result = line if result is None else result + line
    return result


def normed_by(values, square):
    return values / jnp.sqrt(square + 1e-12)


def visits(blocks):
    pairs = blocks // 2
    listed = [(2 * (blocks - 1), 2)] if blocks % 2 else []
    return listed + [(4 * j, 4) for j in [pairs - 1] + list(range(pairs - 1)) if pairs]


def margins(uses, valid):
    for extra in range(64):
        for before in range(extra + 1):
            size = extra + valid
            wrong = size < 4
            for first, blocks in uses:
                held = {}
                for at, n in visits(blocks):
                    place = min(max(first + at + before, 0), size - n)
                    for h in range(n):
                        held[place + h] = first + at + h
                wrong = wrong or any(held.get(before + c, c) != c for c in range(valid))
            if not wrong:
                return before, extra - before
    raise ValueError("no margins")


def buffer_plan(own):
    chunks = own // LANES
    blocks = own // BLOCK
    ring = chunks + 2
    return {
        "early": margins([(-4, blocks + 4)], chunks),
        "second": margins([(-3, blocks + 3)], chunks),
        "late": margins([(-2, blocks + 2), (-1, blocks + 1)], chunks),
        "kept": margins([(-2, blocks + 3), (0, blocks + 1), (-1, blocks + 2)], ring),
    }


def main_kernel(index_ref, u3_ref, u2_ref, planes_ref, small_ref, *refs, own, channels, chips):
    packs = refs[: 2 * chips]
    keep_ref, send_ref, og_ref, cols_ref, rows_ref = refs[2 * chips : 2 * chips + 5]
    (
        w_s, w13_s, w2_s, w2t_s, wout_s, bias_s, taps_s, sl1_s, sl2_s, cv1_s, cv2_s,
        lin1a_s, lin2a_s, gt1a_s, gt2a_s, lin1b_s, lin2b_s, gt1b_s, gt2b_s,
        part1_s, part2_s, mid1_s, mid2_s, tan1a_s, tan2a_s, g1a_s, g2a_s, tan1b_s, tan2b_s, g1b_s, g2b_s,
        tan1c_s, tan2c_s, g1c_s, g2c_s, hid1_s, hid2_s,
        q_s, q0_s, comb_s, tile_s, cols_s,
    ) = refs[2 * chips + 5 :]
    me = index_ref[0]
    rows_own = channels // (2 * chips)
    region = own + 2 * HALO
    all_sum = functools.partial(jnp.sum, keepdims=True)

    for shard, ref in enumerate(packs):
        w_s[jnp.bitwise_xor(me, shard)] = ref[...]
    tile = w_s[:, :, channels:].reshape(channels, LANES)
    w2t = w_s[:, :, 0:channels].reshape(channels, channels)
    lane = iota((1, LANES), 1)
    is_one = lane_is_one(lane)
    is_three = lane_is_three(lane)
    taps_one = jnp.where(is_one, tile, 0.0)
    taps_three = jnp.where(is_three, tile, 0.0)
    head = (lane % 8 == 4) & (lane < TAP_ROWS)
    u1 = tile[:, TAP_ROWS : TAP_ROWS + 1]
    u2 = u2_ref[...]
    u3 = jnp.zeros((1, LANES), F32)
    for o in range(3):
        u3 = jnp.where(is_three & (lane % 8 == 4 + o), u3_ref[o], u3)
    for _ in range(2):
        v1 = all_sum(taps_one * u1, axis=0)
        v2 = all_sum(w2t * u2, axis=1)
        mixed = taps_three * u3
        mixed = mixed + pltpu.roll(mixed, LANES - 1, 1) + pltpu.roll(mixed, LANES - 2, 1)
        v3 = jnp.where(head, mixed, 0.0)
        v1 = normed_by(v1, all_sum(v1 * v1))
        v2 = normed_by(v2, all_sum(v2 * v2))
        v3 = normed_by(v3, all_sum(all_sum(v3 * v3, axis=0), axis=1))
        m1 = all_sum(taps_one * v1, axis=1)
        m2 = all_sum(w2t * v2, axis=0)
        spread = v3 + pltpu.roll(v3, 1, 1) + pltpu.roll(v3, 2, 1)
        m3 = all_sum(taps_three * spread, axis=0)
        for shift in (64, 32, 16, 8):
            m3 = m3 + pltpu.roll(m3, shift, 1)
        square1 = all_sum(m1 * m1)
        square2 = all_sum(m2 * m2)
        square3 = all_sum(jnp.where((lane >= 4) & (lane < 7), m3 * m3, 0.0))
        u1 = normed_by(m1, square1)
        u2 = normed_by(m2, square2)
        u3 = jnp.where(is_three, normed_by(m3, square3), 0.0)
    sigma1 = jnp.sqrt(square1)
    sigma2 = jnp.sqrt(square2)
    sigma3 = jnp.sqrt(square3)
    cols_s[...] = jnp.where(lane == 0, u1, jnp.where(lane == 1, v2, v3)).reshape(cols_s.shape)
    cols_ref[...] = cols_s[me]
    sigma_row = jnp.where(lane == 0, sigma1, jnp.where(lane == 1, sigma2, sigma3))
    rows_ref[...] = jnp.zeros(rows_ref.shape, F32)
    rows_ref[0:1, :] = u2
    rows_ref[1:2, 0:LANES] = v1
    rows_ref[2:3, 0:LANES] = u3
    rows_ref[3:4, 0:LANES] = sigma_row

    scaled = taps_one * (SHRINK / sigma1) + taps_three * (SHRINK / sigma3)
    halved = jnp.where(is_one, 0.5 * scaled, 0.0)
    rest1 = 0.5 * tile[:, TAP_ROWS + 1 : TAP_ROWS + 2]
    for i in range(3):
        part = rest1.astype(BF16).astype(F32)
        halved = jnp.where(lane == TAP_ROWS + i, part, halved)
        rest1 = rest1 - part
    w13_s[0:channels] = halved.astype(BF16)
    w13_s[channels:] = jnp.where(is_three, 0.5 * scaled, 0.0).astype(BF16)
    flipped = scaled.T
    blocks = [pltpu.roll(flipped[(8 - t) * 8 : (9 - t) * 8], 4, 0) for t in range(9)]
    flipped = jnp.concatenate(blocks + [jnp.zeros((8, channels), F32)], axis=0)
    first_rows = iota((TAP_ROWS + 8, 1), 0) % 8 < 4
    wout_s[:, 0:channels] = jnp.where(first_rows, flipped, 0.0).astype(BF16)
    wout_s[:, channels:] = jnp.where(first_rows, 0.0, flipped).astype(BF16)
    w2t_scaled = w2t * (0.5 * SHRINK / sigma2)
    w2t_s[...] = w2t_scaled.astype(BF16)
    w2_s[...] = w2t_scaled.T.astype(BF16)
    bias_s[...] = jnp.broadcast_to(0.5 * tile[:, TAP_ROWS + 2 : TAP_ROWS + 3], (channels, LANES))

    shift8 = small_ref[:, 0:1]
    scale8 = small_ref[:, 1:2]
    bias8 = small_ref[:, 2:3]
    extra8 = small_ref[:, 3:4]
    upper = iota((8, 1), 0) >= 4
    probes8 = planes_ref[8:16]
    cot8 = planes_ref[16:24]

    def masks_at(lanes):
        return [planes_ref[32 + i : 33 + i, lanes] for i in range(4)]

    def put_taps(slot, pieces, lanes):
        ones = jnp.where(iota((8, lanes.size), 0) < 3, 1.0 if slot == 0 else 0.0, 0.0)
        full = jnp.concatenate(pieces + [ones], axis=0).astype(BF16)
        for c in range(lanes.size // LANES):
            chunk = lanes.start // LANES + c
            taps_s[slot, chunk] = full[:, c * LANES : (c + 1) * LANES]

    whole = pl.ds(0, region)
    h8 = (planes_ref[0:8] + shift8) * scale8
    sig8 = 0.5 + 0.5 * jnp.tanh(0.5 * h8)
    rest8 = 1.0 - sig8
    slope0 = (sig8 + h8 * sig8 * rest8) / 1.1
    curve0 = sig8 * rest8 * (2.0 + h8 * (1.0 - 2.0 * sig8)) / 1.1
    state = jnp.where(upper, cot8, h8 * sig8 / 1.1)
    put_taps(0, col_taps(state, masks_at(whole)), whole)
    state = probes8 * jnp.where(upper, planes_ref[24 + 7 : 24 + 8], slope0)
    put_taps(1, col_taps(state, masks_at(whole)), whole)

    own_blocks = own // BLOCK
    ring = own + BLOCK
    plan = buffer_plan(own)
    own_before = [plan[name][0] for name in ("early", "second", "late")]
    kept_before = plan["kept"][0]
    tan_s = (
        (tan1a_s, tan2a_s, g1a_s, g2a_s),
        (tan1b_s, tan2b_s, g1b_s, g2b_s),
        (tan1c_s, tan2c_s, g1c_s, g2c_s),
    )
    kept_s = ((lin1a_s, lin2a_s, gt1a_s, gt2a_s), (lin1b_s, lin2b_s, gt1b_s, gt2b_s))

    def over_blocks(count, body, carry=0):
        pairs = count // 2
        if count % 2:
            carry = body((count - 1) * BLOCK, BLOCK, carry)

        def turn(j, kept):
            return body(jnp.where(j == 0, pairs - 1, j - 1) * (2 * BLOCK), 2 * BLOCK, kept)

        return lax.fori_loop(0, pairs, turn, carry)

    def halves(start, size, base, width):
        places = []
        for h in range(size // LANES):
            chunk = start // LANES + h - base // LANES
            chunks = width // LANES
            places.append(jnp.where((chunk >= 0) & (chunk < chunks), chunk, chunks))
        return places

    def run_of(ref, start, size, base, before):
        first = start // LANES - base // LANES + before
        first = jnp.clip(first, 0, ref.shape[0] - size // LANES)
        return [first + h for h in range(size // LANES)]

    def put(ref, places, value):
        for h, place in enumerate(places):
            ref[place] = value[:, h * LANES : (h + 1) * LANES]

    def join(ref, first, count):
        return jnp.concatenate([ref[first + i] for i in range(count)], axis=1)

    def activation(half_act, slope_ref, curve_ref, lanes, ring_places):
        tanh = jnp.tanh(half_act)
        sig = (1.0 / 1.1) + (1.0 / 1.1) * tanh
        hidden = half_act * sig
        bent = tanh * hidden
        slope_ref[:, lanes] = (sig + hidden) - bent
        put(curve_ref, ring_places, ((1.0 - tanh) * (sig - bent)).astype(BF16))
        return hidden.astype(BF16)

    def start_body(at, size, carry):
        start = pl.multiple_of(at, LANES)
        lanes = pl.ds(start, size)
        count = size // LANES
        ring_places = halves(start, size, HALO - LANES, ring)
        own_places = run_of(hid1_s, start, size, HALO, own_before[0])
        act1 = dot_nn(w13_s[0:channels, 0 : TAP_ROWS + 8], join(taps_s.at[0], start // LANES, count))
        hidden1 = activation(act1, sl1_s, cv1_s, lanes, ring_places)
        put(hid1_s, own_places, hidden1)
        act2 = dot_nn(w2_s[...], hidden1)
        bias2 = bias_s[...]
        hidden2 = activation(
            act2 + jnp.concatenate([bias2] * count, axis=1), sl2_s, cv2_s, lanes, ring_places
        )
        put(hid2_s, own_places, hidden2)
        q0_s[:, lanes] = dot_nn(wout_s[:, 0:channels], hidden2)[0:TAP_ROWS]
        return carry

    over_blocks(own_blocks + 4, start_body)


    def series_stage(stage):
        offset = LANES * (stage - 1)
        count = own_blocks + 5 - stage
        tan_slot = min(stage, 3) - 1
        tan_refs = tan_s[tan_slot]

        def body(at, size, carry):
            start = pl.multiple_of(offset + at, LANES)
            lanes = pl.ds(start, size)
            own_places = run_of(tan_refs[0], start, size, HALO, own_before[tan_slot])
            if stage == 1:
                ring_places = halves(start, size, HALO - LANES, ring)
            else:
                ring_places = run_of(mid1_s, start, size, HALO - LANES, kept_before)
            shift = -kept_before if stage == 4 else 0

            def pair_up(value, save_to, partner, add_from, mix_to):
                for h, place in enumerate(ring_places):
                    part = value[:, h * LANES : (h + 1) * LANES]
                    if save_to is not None:
                        save_to[place] = part.astype(BF16)
                        continue
                    part = (part.astype(BF16) * partner[place + shift]).astype(F32)
                    if add_from is not None:
                        part = part + add_from[place].astype(F32)
                    mix_to[place] = part.astype(BF16)

            if stage <= 2:
                lin1_to, lin2_to, gt1_to, gt2_to = kept_s[stage - 1]
                moves = ((lin1_to,), (gt2_to,), (lin2_to,), (gt1_to,))
                moves = [(place, None, None, None) for (place,) in moves]
            else:
                lin1_of, lin2_of, gt1_of, gt2_of = kept_s[4 - stage]
                sum1, sum2 = (None, None) if stage == 3 else (mid1_s, mid2_s)
                end1, end2 = (mid1_s, mid2_s) if stage == 3 else (lin1b_s, lin2b_s)
                moves = (
                    (None, gt1_of, sum1, part1_s),
                    (None, lin2_of, sum2, part2_s),
                    (None, gt2_of, part2_s, end2),
                    (None, lin1_of, part1_s, end1),
                )
            taps = join(taps_s.at[stage], start // LANES, size // LANES)
            lin1 = dot_nn(w13_s[0:channels, 0 : TAP_ROWS + 8], taps)
            tan1 = (sl1_s[:, lanes] * lin1).astype(BF16)
            put(tan_refs[0], own_places, tan1)
            pair_up(lin1, *moves[0])
            gt2 = dot_nn(w13_s[channels:, 0 : TAP_ROWS + 8], taps)
            g2 = (sl2_s[:, lanes] * gt2).astype(BF16)
            put(tan_refs[3], own_places, g2)
            pair_up(gt2, *moves[1])
            lin2 = dot_nn(w2_s[...], tan1)
            tan2 = (sl2_s[:, lanes] * lin2).astype(BF16)
            put(tan_refs[1], own_places, tan2)
            pair_up(lin2, *moves[2])
            gt1 = dot_nn(w2t_s[...], g2)
            g1 = (sl1_s[:, lanes] * gt1).astype(BF16)
            put(tan_refs[2], own_places, g1)
            pair_up(gt1, *moves[3])
            q_fwd = dot_nn(wout_s[:, 0:channels], tan2)[0:TAP_ROWS]
            q_s[:, lanes] = q_fwd + dot_nn(wout_s[:, channels:], g1)[0:TAP_ROWS]
            return carry

        over_blocks(count, body)

        inside = pl.ds(offset, count * BLOCK)
        result = comb_taps(q_s, inside, masks_at(inside))
        core_from = HALO - offset
        comb_s[stage - 1] = result[:, core_from : core_from + own]
        if stage < NMAX:
            nxt = result[:, LANES : count * BLOCK - LANES]
            lanes = pl.ds(offset + LANES, (count - 1) * BLOCK)
            seed = probes8[:, offset + LANES : offset + LANES + (count - 1) * BLOCK]
            coef = planes_ref[24 + 4 + 3 - stage : 24 + 4 + 4 - stage, lanes]
            following = slope0[:, offset + LANES : offset + LANES + (count - 1) * BLOCK] * nxt
            following = following + jnp.where(upper, seed * coef, 0.0)
            put_taps(stage + 1, col_taps(following, masks_at(lanes)), lanes)

    def own_taps(slot):
        return join(taps_s.at[slot], HALO // LANES, own // LANES)

    def add_weight_grads(slot_pairs, tap_pairs, first):
        total = None
        for left, right in slot_pairs:
            part = dot_nt(left, right)
            total = part if total is None else total + part
        one = None
        three = None
        for left_one, left_three, slot in tap_pairs:
            taps = own_taps(slot)
            part_one = dot_nt(taps, left_one)
            part_three = dot_nt(taps, left_three)
            one = part_one if one is None else one + part_one
            three = part_three if three is None else three + part_three
        w2_part = total.reshape(2 * chips, rows_own, channels)
        tile_part = jnp.where(first_rows, one, three)
        if first:
            w_s[:, :, 0:channels] = w2_part
            tile_s[...] = tile_part
        else:
            w_s[:, :, 0:channels] = w_s[:, :, 0:channels] + w2_part
            tile_s[...] = tile_s[...] + tile_part

    def slot_of(kind, slot):
        return join(tan_s[slot][kind], own_before[slot], own // LANES)

    series_stage(1)
    series_stage(2)
    series_stage(3)
    add_weight_grads(
        ((slot_of(0, 1), slot_of(3, 2)), (slot_of(0, 2), slot_of(3, 1))),
        (
            (slot_of(2, 2), slot_of(1, 2), 2),
            (slot_of(2, 1), slot_of(1, 1), 3),
        ),
        True,
    )
    series_stage(4)
    add_weight_grads(
        ((slot_of(0, 0), slot_of(3, 2)), (slot_of(0, 2), slot_of(3, 0))),
        (
            (slot_of(2, 2), slot_of(1, 2), 1),
            (slot_of(2, 0), slot_of(1, 0), 4),
        ),
        False,
    )

    def final_body(at, size, carry):
        bias_one, bias_two = carry
        start = pl.multiple_of(HALO - LANES + at, LANES)
        lanes = pl.ds(start, size)
        count = size // LANES
        ring_from = at // LANES
        own_places = run_of(g1c_s, start, size, HALO, own_before[2])
        gs2 = dot_nn(w13_s[channels:, 0 : TAP_ROWS + 8], join(taps_s.at[0], start // LANES, count))
        acc2 = join(cv2_s, ring_from, count).astype(F32) * join(lin2b_s, ring_from + kept_before, count).astype(F32)
        ga2 = (acc2 + acc2) + sl2_s[:, lanes] * gs2
        low2 = ga2.astype(BF16)
        gs1 = dot_nn(w2t_s[...], low2)
        acc1 = join(cv1_s, ring_from, count).astype(F32) * join(lin1b_s, ring_from + kept_before, count).astype(F32)
        ga1 = (acc1 + acc1) + sl1_s[:, lanes] * gs1
        low1 = ga1.astype(BF16)
        q_s[:, lanes] = q0_s[:, lanes] + dot_nn(wout_s[:, channels:], low1)[0:TAP_ROWS]
        put(g2c_s, own_places, low2)
        put(g1c_s, own_places, low1)
        for c in range(count):
            chunk = (start - HALO) // LANES + c
            here = jnp.where((chunk >= 0) & (chunk < own // LANES), 1.0, 0.0)
            bias_one = bias_one + here * ga1[:, c * LANES : (c + 1) * LANES]
            bias_two = bias_two + here * ga2[:, c * LANES : (c + 1) * LANES]
        return bias_one, bias_two

    zero = jnp.zeros((channels, LANES), F32)
    bias_one, bias_two = over_blocks(own_blocks + 1, final_body, (zero, zero))
    add_weight_grads(
        ((join(hid1_s, own_before[0], own // LANES), slot_of(3, 2)),), ((slot_of(2, 2), join(hid2_s, own_before[0], own // LANES), 0),), False
    )

    inside = pl.ds(HALO - LANES, own + BLOCK)
    result = comb_taps(q_s, inside, masks_at(inside))[:, LANES : LANES + own]
    mine = slice(HALO, HALO + own)
    h_own = h8[:, mine]
    cot_own = cot8[:, mine]
    probes_own = probes8[:, mine]
    mixed = comb_s[0] * pltpu.roll(comb_s[2], 4, 0)
    mixed = mixed + comb_s[1] * pltpu.roll(comb_s[1], 4, 0)
    mixed = mixed + comb_s[2] * pltpu.roll(comb_s[0], 4, 0)
    mixed = mixed + comb_s[3] * probes_own
    grad_h = cot_own + slope0[:, mine] * result + curve0[:, mine] * mixed
    grad_in = grad_h * scale8
    density = planes_ref[24:25, mine] * comb_s[0]
    for k in range(1, NMAX):
        density = density + planes_ref[24 + k : 25 + k, mine] * comb_s[k]
    density = density * probes_own
    density = density[0:1] + density[1:2] + density[2:3]
    row8 = iota((8, 1), 0)
    high = density.astype(BF16).astype(F32)
    out = jnp.where(row8 < 3, h_own + result + bias8, jnp.where(row8 == 3, high, grad_in))
    out = jnp.where(row8 == 7, density - high, out)
    if own < channels:
        out = jnp.concatenate([out, jnp.zeros((8, channels - own), F32)], axis=1)
    lines = [out[:, c * channels : (c + 1) * channels] for c in range(out.shape[1] // channels)]
    if len(lines) == 1:
        lines.append(jnp.zeros((8, channels), F32))
    out = jnp.concatenate(lines, axis=0).astype(BF16)
    og_ref[...] = jnp.zeros(og_ref.shape, BF16)
    og_ref[:, 0:channels] = out
    send_ref[chips * rows_own :, 0:channels] = out
    send_ref[chips * rows_own :, channels:] = jnp.zeros((out.shape[0], LANES), BF16)

    sums = (
        all_sum(grad_in, axis=1),
        all_sum(grad_h * h_own, axis=1) + extra8,
        all_sum(cot_own, axis=1),
    )
    small_row = jnp.zeros((1, LANES), F32)
    for a, column in enumerate(sums):
        for i in range(3):
            small_row = jnp.where(lane == TAP_ROWS + 2 + 3 * a + i, column[4 + i : 5 + i], small_row)
    bias_one = all_sum(bias_one, axis=1)
    bias_two = all_sum(bias_two, axis=1)
    extras = jnp.where(lane == TAP_ROWS, bias_one, jnp.where(lane == TAP_ROWS + 1, bias_two, small_row))
    blank = jnp.zeros((LANES - TAP_ROWS - 8, channels), F32)
    flat = jnp.concatenate([tile_s[...], blank], axis=0).T
    extras = jnp.where(lane < TAP_ROWS, flat, extras)
    w_s[:, :, channels:] = extras.reshape(2 * chips, rows_own, LANES)

    core = jnp.bitwise_and(me, 1)
    chip = jnp.right_shift(me, 1)
    for m in range(chips):
        block = 2 * jnp.bitwise_xor(chip, m)
        keep_ref[m] = w_s[block + core]
        send_ref[m * rows_own : (m + 1) * rows_own] = w_s[block + 1 - core].astype(BF16)


def output_rows(own, channels):
    return max(8 * (own // channels), 16)


def call_main(me, u3, u2, planes, small, packs, own, channels, chips):
    rows_own = channels // (2 * chips)
    region = own + 2 * HALO
    wide = (own + BLOCK) // LANES + 1
    width = channels + LANES
    out_shape = (
        pltpu.VMEM((chips, rows_own, width), F32),
        pltpu.VMEM((chips * rows_own + output_rows(own, channels), width), BF16),
        pltpu.VMEM((output_rows(own, channels), width), BF16),
        pltpu.VMEM((rows_own, LANES), F32),
        pltpu.VMEM((8, channels), F32),
    )
    vmem = pltpu.VMEM
    plan = buffer_plan(own)

    def buffer(name, lanes):
        return vmem((lanes // LANES + sum(plan[name]), channels, LANES), BF16)

    scratch = [
        vmem((2 * chips, rows_own, width), F32),
        vmem((2 * channels, LANES), BF16),
        vmem((channels, channels), BF16),
        vmem((channels, channels), BF16),
        vmem((TAP_ROWS + 8, 2 * channels), BF16),
        vmem((channels, LANES), F32),
        vmem((NMAX + 1, region // LANES, TAP_ROWS + 8, LANES), BF16),
        vmem((channels, region), F32),
        vmem((channels, region), F32),
        *[vmem((wide, channels, LANES), BF16)] * 6,
        *[buffer("kept", own + BLOCK)] * 8,
        *[buffer("early", own)] * 4,
        *[buffer("second", own)] * 4,
        *[buffer("late", own)] * 4,
        *[buffer("early", own)] * 2,
        vmem((TAP_ROWS, region), F32),
        vmem((TAP_ROWS, region), F32),
        vmem((NMAX, 8, own), F32),
        vmem((TAP_ROWS + 8, channels), F32),
        vmem((2 * chips, rows_own, LANES), F32),
    ]
    full = pl.BlockSpec(memory_space=pltpu.VMEM)
    return pl.pallas_call(
        functools.partial(main_kernel, own=own, channels=channels, chips=chips),
        out_shape=out_shape,
        in_specs=[pl.BlockSpec(memory_space=pltpu.SMEM)] * 2 + [full] * (3 + 2 * chips),
        out_specs=[full] * 5,
        scratch_shapes=scratch,
        compiler_params=pltpu.CompilerParams(vmem_limit_bytes=61 * 1024 * 1024),
        name="flow_block",
    )(me, u3, u2, planes, small, *packs)


def assemble_kernel(index_ref, kinds_ref, small_ref, *refs, own, channels, chips, frames):
    count = chips + 1 + (chips > 1)
    pieces = refs[:count]
    z_ref, gin_ref, logdet_ref, dens_s = refs[count:]
    me = index_ref[0]
    lines = max(own // channels, 1)
    size = min(own, channels)
    rows = output_rows(own, channels)
    for m in range(chips):
        for b in range(2):
            shard = jnp.bitwise_xor(me, 2 * m + b)
            if b == 0:
                block = pieces[m][pieces[m].shape[0] - rows :]
            elif m == 0:
                block = pieces[chips][...]
            else:
                block = pieces[chips + 1][(m - 1) * rows : m * rows]
            block = block.astype(F32)
            for c in range(lines):
                lanes = pl.ds(pl.multiple_of(shard * own + c * size, LANES), size)
                piece = block[8 * c : 8 * c + 8, 0:size]
                z_ref[:, lanes] = piece[0:3]
                gin_ref[:, lanes] = piece[4:7]
                dens_s[:, lanes] = piece[3:4] + piece[7:8]
    scale_sum = small_ref[1, 0] + small_ref[1, 1] + small_ref[1, 2]
    pixel = iota((1, FRAME), 1)
    bottom = (pixel // (WIDTH * 32)) % 2
    right = (pixel // 32) % 2
    lane = iota((1, 4), 1)
    for f in range(frames):
        line = dens_s[:, f * FRAME : (f + 1) * FRAME]
        quads = jnp.zeros((1, 4), F32)
        total = jnp.zeros((1, 1), F32)
        for slot in range(4):
            picked = jnp.where(bottom * 2 + right == slot, line, 0.0)
            picked = jnp.sum(picked, axis=1, keepdims=True)
            quads = jnp.where(lane == slot, picked, quads)
            total = total + picked
        split = kinds_ref[f] == 2
        whole = jnp.where(lane == 0, total + 4096.0 * scale_sum, 0.0)
        logdet_ref[f : f + 1, :] = jnp.where(split, quads + 1024.0 * scale_sum, whole)


def norm_kernel(index_ref, a_ref, b_ref, pack_ref, cols_ref, rows_ref, grad_ref, out_ref, *, channels):
    grad = a_ref[...].astype(F32) + b_ref[...].astype(F32)
    grad_ref[...] = grad
    lane = iota((1, LANES), 1)
    is_one = lane_is_one(lane)
    is_three = lane_is_three(lane)
    tile = grad[:, channels:]
    weights = pack_ref[:, channels:]
    cols = cols_ref[...]
    u1 = cols[:, 0:1]
    v2 = cols[:, 1:2]
    spread = jnp.where((lane % 8 == 4) & (lane < TAP_ROWS), cols, 0.0)
    spread = spread + pltpu.roll(spread, 1, 1) + pltpu.roll(spread, 2, 1)
    outer_one = u1 * rows_ref[1:2, 0:LANES]
    outer_three = spread * rows_ref[2:3, 0:LANES]
    outer_two = v2 * rows_ref[0:1, :]
    grad_two = grad[:, 0:channels]
    weight_two = pack_ref[:, 0:channels]

    def total(values):
        return jnp.sum(jnp.sum(values, axis=0, keepdims=True), axis=1, keepdims=True)

    bias = (lane == TAP_ROWS) | (lane == TAP_ROWS + 1)
    parts = (
        total(jnp.where(is_one, tile * tile, 0.0)),
        total(grad_two * grad_two),
        total(jnp.where(is_three, tile * tile, 0.0)),
        total(jnp.where(is_one, tile * weights, 0.0)),
        total(grad_two * weight_two),
        total(jnp.where(is_three, tile * weights, 0.0)),
        total(jnp.where(is_one, tile * outer_one, 0.0)),
        total(grad_two * outer_two),
        total(jnp.where(is_three, tile * outer_three, 0.0)),
        total(jnp.where(is_one, outer_one * outer_one, 0.0)),
        total(outer_two * outer_two),
        total(jnp.where(is_three, outer_three * outer_three, 0.0)),
        total(jnp.where(bias, tile * tile, 0.0)),
    )
    row = jnp.zeros((1, LANES), F32)
    for index, part in enumerate(parts):
        row = jnp.where(lane == index, part, row)
    small = (lane >= TAP_ROWS + 2) & (lane < TAP_ROWS + 11) & (index_ref[0] == 0)
    row = jnp.where(small, tile[0:1], row)
    out_ref[...] = jnp.broadcast_to(row, out_ref.shape)


def moment_step(grad, moment, second):
    new_moment = BETA_ONE * moment + (1.0 - BETA_ONE) * grad
    new_second = BETA_TWO * second + (1.0 - BETA_TWO) * grad * grad
    return (new_moment, new_second)


def adam_step(param, grad, moment, second):
    new_moment, new_second = moment_step(grad, moment, second)
    fix_one = 1.0 - BETA_ONE**STEP
    fix_two = 1.0 - BETA_TWO**STEP
    update = new_moment / fix_one / (jnp.sqrt(new_second / fix_two) + ADAM_EPS) + DECAY * param
    return (param - LR_RATE * update, new_moment, new_second)


def arrange_kernel(grad_ref, cols_ref, rows_ref, *refs, channels):
    for source, kept in zip(refs[:9], refs[9:18]):
        kept[...] = source[...]
    arrange_gradients(grad_ref, cols_ref, rows_ref, *refs[18:], channels=channels)


def arrange_gradients(
    grad_ref, cols_ref, rows_ref,
    g1_out, o1_out, o2_out, g3_out, o3_out, bias_out, u1_out, v1_out, u2_out, v2_out, u3_out, v3_out, *, channels,
):
    lane = iota((1, LANES), 1)
    cols = cols_ref[...]
    tile = grad_ref[:, channels:]
    is_one = lane_is_one(lane)
    is_three = lane_is_three(lane)
    spread = jnp.where((lane % 8 == 4) & (lane < TAP_ROWS), cols, 0.0)
    spread = spread + pltpu.roll(spread, 1, 1) + pltpu.roll(spread, 2, 1)
    outer_one = jnp.where(is_one, cols[:, 0:1] * rows_ref[1:2, 0:LANES], 0.0)
    outer_three = jnp.where(is_three, spread * rows_ref[2:3, 0:LANES], 0.0)
    o2_out[...] = cols[:, 1:2] * rows_ref[0:1, :]
    g1_out[...] = dot_nt(spread_one(), jnp.where(is_one, tile, 0.0), HIGH)
    o1_out[...] = dot_nt(spread_one(), outer_one, HIGH)
    g3_out[...] = dot_nt(spread_three(), jnp.where(is_three, tile, 0.0), HIGH)
    o3_out[...] = dot_nt(spread_three(), outer_three, HIGH)
    bias_out[...] = tile.T[TAP_ROWS : TAP_ROWS + 2, :]
    flipped = cols.T
    u1_out[...] = flipped[0:1]
    v2_out[...] = flipped[1:2]
    tap = iota((9, LANES), 0)
    select = (iota((9, LANES), 1) == (8 - tap) * 8 + 4).astype(F32)
    v3_out[...] = dot_nn(select, flipped, HIGH)
    v1_out[...] = dot_nt(rows_ref[1:2, 0:LANES], spread_one(), HIGH)
    u2_out[...] = rows_ref[0:1, :]
    u3_out[...] = rows_ref[2:3, 4:7]


def update_kernel(
    totals_ref, rows_ref, grad_ref, g1_ref, o1_ref, o2_ref, g3_ref, o3_ref, bias_ref,
    w1_ref, m1_ref, s1_ref, w2_ref, m2_ref, s2_ref, w3_ref, m3_ref, s3_ref,
    mb_ref, sb_ref, small_ref, msmall_ref, ssmall_ref,
    norm_out, nw1, nm1, ns1, nw2, nm2, ns2, nw3, nm3, ns3, cb, nmb, nsb, nsm, nmsm, nssm, lw1, lw2, lw3, *, channels,
):
    lane = iota((1, LANES), 1)
    lines = [totals_ref[m : m + 1] for m in range(totals_ref.shape[0])]
    while len(lines) > 1:
        lines = [lines[m] + lines[m + 1] for m in range(0, len(lines), 2)]
    row = lines[0]

    def pick(index):
        return row[:, index : index + 1]

    small_row = jnp.where((lane >= TAP_ROWS + 2) & (lane < TAP_ROWS + 11), row, 0.0)
    square = pick(12) + jnp.sum(small_row * small_row, axis=1, keepdims=True)
    scales = []
    for j in range(3):
        sigma = rows_ref[3:4, j : j + 1]
        ratio = SHRINK / sigma
        factor = pick(3 + j) / sigma
        fixed = pick(j) - 2.0 * factor * pick(6 + j) + factor * factor * pick(9 + j)
        square = square + ratio * ratio * jnp.maximum(fixed, 0.0)
        scales.append((ratio, factor))
    norm = jnp.sqrt(square)
    norm_out[...] = norm
    clip = jnp.minimum(1.0, CLIP_LIMIT / (norm + 1e-06))

    for index, grad, outer, w_ref, m_ref, s_ref, nw, nm, ns, lw in (
        (0, g1_ref[...], o1_ref, w1_ref, m1_ref, s1_ref, nw1, nm1, ns1, lw1),
        (1, grad_ref[:, 0:channels], o2_ref, w2_ref, m2_ref, s2_ref, nw2, nm2, ns2, lw2),
        (2, g3_ref[...], o3_ref, w3_ref, m3_ref, s3_ref, nw3, nm3, ns3, lw3),
    ):
        ratio, factor = scales[index]
        fixed = (clip * ratio) * (grad - factor * outer[...])
        new, moment, second = adam_step(w_ref[...], fixed, m_ref[...], s_ref[...])
        nw[...] = new
        nm[...] = moment
        ns[...] = second
        lw[...] = new.astype(BF16)

    bias = bias_ref[...] * clip
    cb[...] = bias
    moment, second = moment_step(bias, mb_ref[...], sb_ref[...])
    nmb[...] = moment
    nsb[...] = second

    small_row = small_row * clip
    lane3 = iota((1, 3), 1)
    rows = []
    for a in range(3):
        line = jnp.zeros((1, 3), F32)
        for i in range(3):
            at = TAP_ROWS + 2 + 3 * a + i
            line = jnp.where(lane3 == i, small_row[:, at : at + 1], line)
        rows.append(line)
    small_grad = jnp.concatenate(rows, axis=0)
    new, moment, second = adam_step(small_ref[...], small_grad, msmall_ref[...], ssmall_ref[...])
    nsm[...] = new
    nmsm[...] = moment
    nssm[...] = second


def prepare_kernel(
    index_ref, kinds_ref, len_ref, cot_ref, params_ref, images_ref, probes_ref, cot_z_ref,
    planes_ref, small_ref, *, own, frames,
):
    region = planes_ref.shape[1]
    pixels = images_ref.shape[1]
    me = index_ref[0]
    first = me * own - HALO
    planes_ref[...] = jnp.zeros(planes_ref.shape, F32)
    for chunk in range(region // LANES):
        start = first + chunk * LANES
        source = pl.ds(pl.multiple_of(jnp.clip(start, 0, pixels - LANES), LANES), LANES)
        lanes = pl.ds(chunk * LANES, LANES)
        inside = (start >= 0) & (start < pixels)
        for row, ref in ((0, images_ref), (4, images_ref), (8, probes_ref), (12, probes_ref), (20, cot_z_ref)):
            planes_ref[row : row + 3, lanes] = jnp.where(inside, ref[:, source], 0.0)

    position = first + iota((1, region), 1)
    frame = jnp.right_shift(position, 12)
    pixel = jnp.bitwise_and(position, FRAME - 1)
    row = jnp.right_shift(pixel, 6)
    col = jnp.bitwise_and(pixel, WIDTH - 1)
    half = WIDTH // 2
    quad = 2 * jnp.right_shift(row, 5) + jnp.right_shift(col, 5)
    split = jnp.zeros((1, region), jnp.int32)
    for f in range(frames):
        split = jnp.where(frame == f, jnp.where(kinds_ref[f] == 2, 1, 0), split)
    slot = 4 * frame + jnp.where(split == 1, quad, 0)
    length = jnp.zeros((1, region), jnp.int32)
    weight = jnp.zeros((1, region), F32)
    for f in range(frames):
        for q in range(4):
            here = slot == 4 * f + q
            length = jnp.where(here, len_ref[f, q], length)
            weight = jnp.where(here, cot_ref[f, q], weight)
    for k in range(NMAX):
        coef = jnp.where(length >= k + 1, (-1.0) ** k / (k + 1), 0.0)
        planes_ref[24 + k : 25 + k] = coef
        planes_ref[24 + NMAX + k : 25 + NMAX + k] = coef * weight
    for index, line in enumerate((row, col)):
        low = (line == 0) | ((split == 1) & (line == half))
        high = (line == WIDTH - 1) | ((split == 1) & (line == half - 1))
        planes_ref[32 + 2 * index : 33 + 2 * index] = jnp.where(low, 0.0, 1.0)
        planes_ref[33 + 2 * index : 34 + 2 * index] = jnp.where(high, 0.0, 1.0)

    extra = jnp.float32(0.0)
    for f in range(frames):
        whole = 4096.0 * cot_ref[f, 0]
        quads = 1024.0 * (cot_ref[f, 0] + cot_ref[f, 1] + cot_ref[f, 2] + cot_ref[f, 3])
        extra = extra + jnp.where(kinds_ref[f] == 2, quads, whole)
    extra = jnp.where(me == 0, extra, 0.0)
    row8 = iota((8, LANES), 0)
    lane = iota((8, LANES), 1)
    values = []
    for a in range(3):
        value = jnp.zeros((8, LANES), F32)
        for i in range(3):
            value = jnp.where(row8 % 4 == i, params_ref[a, i], value)
        values.append(value)
    result = jnp.where(lane == 0, values[0], jnp.where(lane == 1, jnp.exp(values[1]), values[2]))
    small_ref[...] = jnp.where(row8 % 4 == 3, 0.0, jnp.where(lane == 3, extra, result))


def local(
    images, frame_kinds, series_len, probes, cot_z, cot_logdet, weight1, weight2, weight3, biases,
    small_params, power_u1, power_u2, power_u3, moment_w1, second_w1, moment_w2, second_w2,
    moment_w3, second_w3, moment_bias, second_bias, moment_small, second_small,
):
    shards = lax.axis_size("chan")
    replicas = lax.axis_size("dp")
    chips = shards // 2
    me = lax.axis_index("chan")
    channels = weight2.shape[0]
    rows_own = weight1.shape[0]
    pixels = images.shape[1]
    frames = frame_kinds.shape[0]
    own = pixels // shards
    width = channels + LANES
    full = pl.BlockSpec(memory_space=pltpu.VMEM)
    smem = pl.BlockSpec(memory_space=pltpu.SMEM)
    index = me.reshape(1).astype(jnp.int32)

    def near_memory(values):
        return pltpu.with_memory_space_constraint(values, pltpu.VMEM)

    def swap(values, axis, size, bits):
        return lax.ppermute(values, axis, [(j, j ^ bits) for j in range(size)])

    pack = pl.pallas_call(
        pack_kernel,
        out_shape=pltpu.VMEM((rows_own, width), F32),
        in_specs=[full] * 5,
        out_specs=full,
        name="pack_weights",
    )(weight1.T, weight2.T, weight3, biases, power_u1.reshape(1, rows_own))
    near = [pack] + [swap(pack, "chan", shards, 2 * m) for m in range(1, chips)]
    planes, small = pl.pallas_call(
        functools.partial(prepare_kernel, own=own, frames=frames),
        out_shape=(
            pltpu.VMEM((40, own + 2 * HALO), F32),
            pltpu.VMEM((8, LANES), F32),
        ),
        in_specs=[smem] * 5 + [full] * 3,
        out_specs=[full] * 2,
        name="prepare_planes",
    )(index, frame_kinds, series_len, cot_logdet, small_params, images, probes, cot_z)

    near[-1], planes = lax.optimization_barrier((near[-1], planes))
    packs = []
    for values in near:
        packs += [values, swap(values, "chan", shards, 1)]

    keep, send, og, cols_own, rows = call_main(
        index, power_u3, power_u2.reshape(1, channels), near_memory(planes), near_memory(small),
        [near_memory(values) for values in packs], own, channels, chips
    )

    got = swap(send, "chan", shards, 1)
    og_other = got[chips * rows_own :]
    summed = keep + got[: chips * rows_own].reshape(keep.shape).astype(F32)
    total = summed[0]
    near_og = [og]
    for m in range(1, chips):
        message = jnp.concatenate([summed[m].astype(BF16), og], axis=0)
        message = swap(message, "chan", shards, 2 * m)
        total = total + message[:rows_own].astype(F32)
        near_og.append(message)
    tails = [message[rows_own:] for message in near_og[1:]]
    pieces = near_og + [og_other]
    if tails:
        pieces.append(swap(jnp.concatenate(tails, axis=0), "chan", shards, 1))
    half = total.astype(BF16)
    assembled = pl.pallas_call(
        functools.partial(assemble_kernel, own=own, channels=channels, chips=chips, frames=frames),
        out_shape=(
            jax.ShapeDtypeStruct((3, pixels), F32),
            jax.ShapeDtypeStruct((3, pixels), F32),
            jax.ShapeDtypeStruct((frames, 4), F32),
        ),
        in_specs=[smem] * 3 + [full] * len(pieces),
        out_specs=[full] * 3,
        scratch_shapes=[pltpu.VMEM((1, pixels), F32)],
        name="assemble_outputs",
    )(index, frame_kinds, small_params, *[near_memory(piece) for piece in pieces])
    bits = 1
    while 2 * bits < replicas:
        half = (half.astype(F32) + swap(half, "dp", replicas, bits).astype(F32)).astype(BF16)
        bits *= 2
    other = swap(half, "dp", replicas, bits) if replicas > 1 else jnp.zeros_like(half)
    other, assembled = lax.optimization_barrier((other, assembled))
    z_out, grad_input, logdet = assembled


    grad, parts = pl.pallas_call(
        functools.partial(norm_kernel, channels=channels),
        out_shape=(
            pltpu.VMEM((rows_own, width), F32),
            pltpu.VMEM((8, LANES), F32),
        ),
        in_specs=[smem] + [full] * 5,
        out_specs=[full] * 2,
        name="norm_parts",
    )(index, near_memory(half), near_memory(other), near_memory(pack), near_memory(cols_own), near_memory(rows))
    pair = parts + swap(parts, "chan", shards, 1)
    totals = [pair[0:1]] + [swap(pair, "chan", shards, 2 * m)[0:1] for m in range(1, chips)]
    totals = jnp.concatenate(totals, axis=0)

    def like(value, dtype=F32):
        return jax.ShapeDtypeStruct(value.shape, dtype)

    arranged_shape = (
        [pltpu.VMEM(weight1.T.shape, F32)] * 2
        + [pltpu.VMEM((rows_own, channels), F32)]
        + [pltpu.VMEM(weight3.shape, F32)] * 2
        + [pltpu.VMEM(biases.shape, F32)]
        + [jax.ShapeDtypeStruct((1, rows_own), F32), jax.ShapeDtypeStruct((1, 27), F32)]
        + [jax.ShapeDtypeStruct((1, channels), F32), jax.ShapeDtypeStruct((1, rows_own), F32)]
        + [jax.ShapeDtypeStruct((1, 3), F32), jax.ShapeDtypeStruct((9, rows_own), F32)]
    )
    state = (
        weight1.T, moment_w1.T, second_w1.T, weight2.T, moment_w2.T, second_w2.T, weight3, moment_w3, second_w3,
    )
    arranged_shape = [pltpu.VMEM(value.shape, F32) for value in state] + arranged_shape
    arranged = pl.pallas_call(
        functools.partial(arrange_kernel, channels=channels),
        out_shape=arranged_shape,
        in_specs=[full] * 12,
        out_specs=[full] * len(arranged_shape),
        name="arrange_gradients",
    )(near_memory(grad), near_memory(cols_own), near_memory(rows), *state)
    state, arranged = arranged[:9], arranged[9:]
    vectors = arranged[6:]
    out_shape = (
        [jax.ShapeDtypeStruct((1, 1), F32)]
        + [like(weight1.T)] * 3
        + [like(weight2.T)] * 3
        + [like(weight3)] * 3
        + [like(biases)] * 3
        + [like(small_params)] * 3
        + [like(weight1.T, BF16), like(weight2.T, BF16), like(weight3, BF16)]
    )
    done = pl.pallas_call(
        functools.partial(update_kernel, channels=channels),
        out_shape=out_shape,
        in_specs=[full] * 23,
        out_specs=[full] * len(out_shape),
        name="adam_update",
    )(
        *[near_memory(values) for values in (totals, rows, grad, *arranged[:6])],
        *[near_memory(values) for values in state], moment_bias, second_bias, small_params, moment_small, second_small,
    )
    norm, updates = done[0], list(done[1:])
    for slot in (0, 1, 2, 3, 4, 5, 15, 16):
        updates[slot] = updates[slot].T
    return (
        z_out,
        logdet,
        grad_input,
        norm.reshape(()),
        *updates,
        vectors[0].reshape(rows_own),
        vectors[1].reshape(27),
        vectors[2].reshape(channels),
        vectors[3].reshape(rows_own),
        vectors[4].reshape(3),
        vectors[5],
    )


def solution(mesh):
    chan_rows = P("chan", None)
    chan_cols = P(None, "chan")
    return jax.shard_map(
        local,
        mesh=mesh,
        in_specs=(
            P(None, "dp"), P("dp"), P("dp", None), P(None, "dp"), P(None, "dp"), P("dp", None),
            chan_rows, chan_cols, chan_cols, chan_cols, P(), P("chan"), P(), P(),
            chan_rows, chan_rows, chan_cols, chan_cols, chan_cols, chan_cols, chan_cols, chan_cols, P(), P(),
        ),
        out_specs=(
            P(None, "dp"), P("dp", None), P(None, "dp"), P(),
            chan_rows, chan_rows, chan_rows, chan_cols, chan_cols, chan_cols, chan_cols, chan_cols, chan_cols,
            chan_cols, chan_cols, chan_cols, P(), P(), P(), chan_rows, chan_cols, chan_cols,
            P("chan"), P(), P(), P("chan"), P(), chan_cols,
        ),
        check_vma=False,
    )
```

```python
import functools

import jax
import jax.numpy as jnp
from jax import lax
from jax.experimental import pallas as pl
from jax.experimental.pallas import tpu as pltpu
from jax.sharding import PartitionSpec as P

NMAX = 4
STEP = 7
SHRINK = 0.98
LR_RATE = 0.05
BETA_ONE = 0.5
BETA_TWO = 0.55
ADAM_EPS = 1e-08
DECAY = 0.01
CLIP_LIMIT = 1.0

WIDTH = 64
FRAME = 4096
BLOCK = 256
HALO = 2 * NMAX * WIDTH
LANES = 128
TAP_ROWS = 72
F32 = jnp.float32
BF16 = jnp.bfloat16
HIGH = lax.Precision.HIGHEST


def iota(shape, dim):
    return lax.broadcasted_iota(jnp.int32, shape, dim)


def dot_nn(left, right, precision=None):
    return lax.dot_general(
        left, right, (((1,), (0,)), ((), ())), precision=precision, preferred_element_type=F32
    )


def dot_nt(left, right, precision=None):
    return lax.dot_general(
        left, right, (((1,), (1,)), ((), ())), precision=precision, preferred_element_type=F32
    )


def dot_tn(left, right, precision=None):
    return lax.dot_general(
        left, right, (((0,), (0,)), ((), ())), precision=precision, preferred_element_type=F32
    )


def spread_one():
    row = iota((27, LANES), 0)
    return (iota((27, LANES), 1) == (row % 9) * 8 + row // 9).astype(F32)


def spread_three():
    row = iota((27, LANES), 0)
    return (iota((27, LANES), 1) == (8 - row % 9) * 8 + 4 + row // 9).astype(F32)


def lane_is_one(lane):
    return (lane % 8 < 3) & (lane < TAP_ROWS)


def lane_is_three(lane):
    return (lane % 8 >= 4) & (lane % 8 < 7) & (lane < TAP_ROWS)


def pack_kernel(w1_ref, w2_ref, w3_ref, bias_ref, u1_ref, out_ref):
    channels = w2_ref.shape[1]
    out_ref[:, 0:channels] = w2_ref[...]
    tile = dot_tn(w1_ref[...], spread_one(), HIGH) + dot_tn(w3_ref[...], spread_three(), HIGH)
    lane = iota((1, LANES), 1)
    for index, row in enumerate((u1_ref[...], bias_ref[0:1, :], bias_ref[1:2, :])):
        column = jnp.broadcast_to(row, (8, row.shape[1])).T[:, 0:1]
        tile = jnp.where(lane == TAP_ROWS + index, column, tile)
    out_ref[:, channels:] = tile


def col_taps(state, masks):
    size = state.shape[1]
    row_up, row_down, col_left, col_right = masks
    left = col_left * pltpu.roll(state, 1, 1)
    right = col_right * pltpu.roll(state, size - 1, 1)
    pieces = []
    for shift_y in (-1, 0, 1):
        for plane in (left, state, right):
            if shift_y == -1:
                plane = row_up * pltpu.roll(plane, WIDTH, 1)
            if shift_y == 1:
                plane = row_down * pltpu.roll(plane, size - WIDTH, 1)
            pieces.append(plane)
    return pieces


def comb_taps(q_ref, lanes, masks):
    size = lanes.size
    row_up, row_down, col_left, col_right = masks
    result = None
    for shift_y in (-1, 0, 1):
        base = 24 * (shift_y + 1)
        line = (
            col_left * pltpu.roll(q_ref[base : base + 8, lanes], 1, 1)
            + q_ref[base + 8 : base + 16, lanes]
            + col_right * pltpu.roll(q_ref[base + 16 : base + 24, lanes], size - 1, 1)
        )
        if shift_y == -1:
            line = row_up * pltpu.roll(line, WIDTH, 1)
        if shift_y == 1:
            line = row_down * pltpu.roll(line, size - WIDTH, 1)
        result = line if result is None else result + line
    return result


def normed_by(values, square):
    return values / jnp.sqrt(square + 1e-12)


def visits(blocks):
    pairs = blocks // 2
    listed = [(2 * (blocks - 1), 2)] if blocks % 2 else []
    return listed + [(4 * j, 4) for j in [pairs - 1] + list(range(pairs - 1)) if pairs]


def margins(uses, valid):
    for extra in range(64):
        for before in range(extra + 1):
            size = extra + valid
            wrong = size < 4
            for first, blocks in uses:
                held = {}
                for at, n in visits(blocks):
                    place = min(max(first + at + before, 0), size - n)
                    for h in range(n):
                        held[place + h] = first + at + h
                wrong = wrong or any(held.get(before + c, c) != c for c in range(valid))
            if not wrong:
                return before, extra - before
    raise ValueError("no margins")


def buffer_plan(own):
    chunks = own // LANES
    blocks = own // BLOCK
    ring = chunks + 2
    return {
        "early": margins([(-4, blocks + 4)], chunks),
        "second": margins([(-3, blocks + 3)], chunks),
        "late": margins([(-2, blocks + 2), (-1, blocks + 1)], chunks),
        "kept": margins([(-2, blocks + 3), (0, blocks + 1), (-1, blocks + 2)], ring),
    }


def main_kernel(index_ref, u3_ref, u2_ref, planes_ref, small_ref, *refs, own, channels, chips):
    packs = refs[: 2 * chips]
    keep_ref, send_ref, og_ref, cols_ref, rows_ref = refs[2 * chips : 2 * chips + 5]
    (
        w_s, w13_s, w2_s, w2t_s, wout_s, bias_s, taps_s, sl1_s, sl2_s, cv1_s, cv2_s,
        lin1a_s, lin2a_s, gt1a_s, gt2a_s, lin1b_s, lin2b_s, gt1b_s, gt2b_s,
        part1_s, part2_s, mid1_s, mid2_s, tan1a_s, tan2a_s, g1a_s, g2a_s, tan1b_s, tan2b_s, g1b_s, g2b_s,
        tan1c_s, tan2c_s, g1c_s, g2c_s, hid1_s, hid2_s,
        q_s, q0_s, comb_s, tile_s, cols_s,
    ) = refs[2 * chips + 5 :]
    me = index_ref[0]
    rows_own = channels // (2 * chips)
    region = own + 2 * HALO
    all_sum = functools.partial(jnp.sum, keepdims=True)

    for shard, ref in enumerate(packs):
        w_s[jnp.bitwise_xor(me, shard)] = ref[...]
    tile = w_s[:, :, channels:].reshape(channels, LANES)
    w2t = w_s[:, :, 0:channels].reshape(channels, channels)
    lane = iota((1, LANES), 1)
    is_one = lane_is_one(lane)
    is_three = lane_is_three(lane)
    taps_one = jnp.where(is_one, tile, 0.0)
    taps_three = jnp.where(is_three, tile, 0.0)
    head = (lane % 8 == 4) & (lane < TAP_ROWS)
    u1 = tile[:, TAP_ROWS : TAP_ROWS + 1]
    u2 = u2_ref[...]
    gram = {}
    for gap in range(3):
        other = pltpu.roll(taps_three, LANES - gap, 1) if gap else taps_three
        line = all_sum(taps_three * other, axis=0)
        for shift in (64, 32, 16, 8):
            line = line + pltpu.roll(line, shift, 1)
        for o in range(3 - gap):
            gram[o, o + gap] = gram[o + gap, o] = line[:, 4 + o : 5 + o]
    u3 = [jnp.full((1, 1), u3_ref[o], F32) for o in range(3)]
    for _ in range(2):
        v1 = all_sum(taps_one * u1, axis=0)
        v2 = all_sum(w2t * u2, axis=1)
        before3 = u3
        m3 = [sum(gram[o, p] * u3[p] for p in range(3)) for o in range(3)]
        v3_square = jnp.maximum(sum(m3[o] * u3[o] for o in range(3)), 0.0)
        v1 = normed_by(v1, all_sum(v1 * v1))
        v2 = normed_by(v2, all_sum(v2 * v2))
        m3 = [normed_by(value, v3_square) for value in m3]
        m1 = all_sum(taps_one * v1, axis=1)
        m2 = all_sum(w2t * v2, axis=0)
        square1 = all_sum(m1 * m1)
        square2 = all_sum(m2 * m2)
        square3 = sum(value * value for value in m3)
        u1 = normed_by(m1, square1)
        u2 = normed_by(m2, square2)
        u3 = [normed_by(value, square3) for value in m3]
    def three_lanes(values):
        line = jnp.zeros((1, LANES), F32)
        for o in range(3):
            line = jnp.where(is_three & (lane % 8 == 4 + o), values[o], line)
        return line

    mixed = taps_three * normed_by(three_lanes(before3), v3_square)
    mixed = mixed + pltpu.roll(mixed, LANES - 1, 1) + pltpu.roll(mixed, LANES - 2, 1)
    v3 = jnp.where(head, mixed, 0.0)
    u3 = three_lanes(u3)
    sigma1 = jnp.sqrt(square1)
    sigma2 = jnp.sqrt(square2)
    sigma3 = jnp.sqrt(square3)
    cols_s[...] = jnp.where(lane == 0, u1, jnp.where(lane == 1, v2, v3)).reshape(cols_s.shape)
    cols_ref[...] = cols_s[me]
    sigma_row = jnp.where(lane == 0, sigma1, jnp.where(lane == 1, sigma2, sigma3))
    rows_ref[...] = jnp.zeros(rows_ref.shape, F32)
    rows_ref[0:1, :] = u2
    rows_ref[1:2, 0:LANES] = v1
    rows_ref[2:3, 0:LANES] = u3
    rows_ref[3:4, 0:LANES] = sigma_row

    scaled = taps_one * (SHRINK / sigma1) + taps_three * (SHRINK / sigma3)
    halved = jnp.where(is_one, 0.5 * scaled, 0.0)
    rest1 = 0.5 * tile[:, TAP_ROWS + 1 : TAP_ROWS + 2]
    for i in range(3):
        part = rest1.astype(BF16).astype(F32)
        halved = jnp.where(lane == TAP_ROWS + i, part, halved)
        rest1 = rest1 - part
    w13_s[0:channels] = halved.astype(BF16)
    w13_s[channels:] = jnp.where(is_three, 0.5 * scaled, 0.0).astype(BF16)
    flipped = scaled.T
    blocks = [pltpu.roll(flipped[(8 - t) * 8 : (9 - t) * 8], 4, 0) for t in range(9)]
    flipped = jnp.concatenate(blocks + [jnp.zeros((8, channels), F32)], axis=0)
    first_rows = iota((TAP_ROWS + 8, 1), 0) % 8 < 4
    wout_s[:, 0:channels] = jnp.where(first_rows, flipped, 0.0).astype(BF16)
    wout_s[:, channels:] = jnp.where(first_rows, 0.0, flipped).astype(BF16)
    w2t_scaled = w2t * (0.5 * SHRINK / sigma2)
    w2t_s[...] = w2t_scaled.astype(BF16)
    w2_s[...] = w2t_scaled.T.astype(BF16)
    bias_s[...] = jnp.broadcast_to(0.5 * tile[:, TAP_ROWS + 2 : TAP_ROWS + 3], (channels, LANES))

    shift8 = small_ref[:, 0:1]
    scale8 = small_ref[:, 1:2]
    bias8 = small_ref[:, 2:3]
    extra8 = small_ref[:, 3:4]
    upper = iota((8, 1), 0) >= 4
    probes8 = planes_ref[8:16]
    cot8 = planes_ref[16:24]

    def masks_at(lanes):
        return [planes_ref[32 + i : 33 + i, lanes] for i in range(4)]

    def put_taps(slot, pieces, lanes):
        ones = jnp.where(iota((8, lanes.size), 0) < 3, 1.0 if slot == 0 else 0.0, 0.0)
        full = jnp.concatenate(pieces + [ones], axis=0).astype(BF16)
        for c in range(lanes.size // LANES):
            chunk = lanes.start // LANES + c
            taps_s[slot, chunk] = full[:, c * LANES : (c + 1) * LANES]

    whole = pl.ds(0, region)
    h8 = (planes_ref[0:8] + shift8) * scale8
    sig8 = 0.5 + 0.5 * jnp.tanh(0.5 * h8)
    rest8 = 1.0 - sig8
    slope0 = (sig8 + h8 * sig8 * rest8) / 1.1
    curve0 = sig8 * rest8 * (2.0 + h8 * (1.0 - 2.0 * sig8)) / 1.1
    state = jnp.where(upper, cot8, h8 * sig8 / 1.1)
    put_taps(0, col_taps(state, masks_at(whole)), whole)
    state = probes8 * jnp.where(upper, planes_ref[24 + 7 : 24 + 8], slope0)
    put_taps(1, col_taps(state, masks_at(whole)), whole)

    own_blocks = own // BLOCK
    ring = own + BLOCK
    plan = buffer_plan(own)
    own_before = [plan[name][0] for name in ("early", "second", "late")]
    kept_before = plan["kept"][0]
    tan_s = (
        (tan1a_s, tan2a_s, g1a_s, g2a_s),
        (tan1b_s, tan2b_s, g1b_s, g2b_s),
        (tan1c_s, tan2c_s, g1c_s, g2c_s),
    )
    kept_s = ((lin1a_s, lin2a_s, gt1a_s, gt2a_s), (lin1b_s, lin2b_s, gt1b_s, gt2b_s))

    def over_blocks(count, body, carry=0):
        pairs = count // 2
        if count % 2:
            carry = body((count - 1) * BLOCK, BLOCK, carry)

        def turn(j, kept):
            return body(jnp.where(j == 0, pairs - 1, j - 1) * (2 * BLOCK), 2 * BLOCK, kept)

        return lax.fori_loop(0, pairs, turn, carry)

    def halves(start, size, base, width):
        places = []
        for h in range(size // LANES):
            chunk = start // LANES + h - base // LANES
            chunks = width // LANES
            places.append(jnp.where((chunk >= 0) & (chunk < chunks), chunk, chunks))
        return places

    def run_of(ref, start, size, base, before):
        first = start // LANES - base // LANES + before
        first = jnp.clip(first, 0, ref.shape[0] - size // LANES)
        return [first + h for h in range(size // LANES)]

    def put(ref, places, value):
        for h, place in enumerate(places):
            ref[place] = value[:, h * LANES : (h + 1) * LANES]

    def join(ref, first, count):
        return jnp.concatenate([ref[first + i] for i in range(count)], axis=1)

    def activation(half_act, slope_ref, curve_ref, lanes, ring_places):
        tanh = jnp.tanh(half_act)
        sig = (1.0 / 1.1) + (1.0 / 1.1) * tanh
        hidden = half_act * sig
        bent = tanh * hidden
        slope_ref[:, lanes] = (sig + hidden) - bent
        put(curve_ref, ring_places, ((1.0 - tanh) * (sig - bent)).astype(BF16))
        return hidden.astype(BF16)

    def start_body(at, size, carry):
        start = pl.multiple_of(at, LANES)
        lanes = pl.ds(start, size)
        count = size // LANES
        ring_places = halves(start, size, HALO - LANES, ring)
        own_places = run_of(hid1_s, start, size, HALO, own_before[0])
        act1 = dot_nn(w13_s[0:channels, 0 : TAP_ROWS + 8], join(taps_s.at[0], start // LANES, count))
        hidden1 = activation(act1, sl1_s, cv1_s, lanes, ring_places)
        put(hid1_s, own_places, hidden1)
        act2 = dot_nn(w2_s[...], hidden1)
        bias2 = bias_s[...]
        hidden2 = activation(
            act2 + jnp.concatenate([bias2] * count, axis=1), sl2_s, cv2_s, lanes, ring_places
        )
        put(hid2_s, own_places, hidden2)
        q0_s[:, lanes] = dot_nn(wout_s[:, 0:channels], hidden2)[0:TAP_ROWS]
        return carry

    over_blocks(own_blocks + 4, start_body)


    def series_stage(stage):
        offset = LANES * (stage - 1)
        count = own_blocks + 5 - stage
        tan_slot = min(stage, 3) - 1
        tan_refs = tan_s[tan_slot]

        def body(at, size, carry):
            start = pl.multiple_of(offset + at, LANES)
            lanes = pl.ds(start, size)
            own_places = run_of(tan_refs[0], start, size, HALO, own_before[tan_slot])
            if stage == 1:
                ring_places = halves(start, size, HALO - LANES, ring)
            else:
                ring_places = run_of(mid1_s, start, size, HALO - LANES, kept_before)
            shift = -kept_before if stage == 4 else 0

            def pair_up(value, save_to, partner, add_from, mix_to):
                for h, place in enumerate(ring_places):
                    part = value[:, h * LANES : (h + 1) * LANES]
                    if save_to is not None:
                        save_to[place] = part.astype(BF16)
                        continue
                    part = (part.astype(BF16) * partner[place + shift]).astype(F32)
                    if add_from is not None:
                        part = part + add_from[place].astype(F32)
                    mix_to[place] = part.astype(BF16)

            if stage <= 2:
                lin1_to, lin2_to, gt1_to, gt2_to = kept_s[stage - 1]
                moves = ((lin1_to,), (gt2_to,), (lin2_to,), (gt1_to,))
                moves = [(place, None, None, None) for (place,) in moves]
            else:
                lin1_of, lin2_of, gt1_of, gt2_of = kept_s[4 - stage]
                sum1, sum2 = (None, None) if stage == 3 else (mid1_s, mid2_s)
                end1, end2 = (mid1_s, mid2_s) if stage == 3 else (lin1b_s, lin2b_s)
                moves = (
                    (None, gt1_of, sum1, part1_s),
                    (None, lin2_of, sum2, part2_s),
                    (None, gt2_of, part2_s, end2),
                    (None, lin1_of, part1_s, end1),
                )
            taps = join(taps_s.at[stage], start // LANES, size // LANES)
            lin1 = dot_nn(w13_s[0:channels, 0 : TAP_ROWS + 8], taps)
            tan1 = (sl1_s[:, lanes] * lin1).astype(BF16)
            put(tan_refs[0], own_places, tan1)
            pair_up(lin1, *moves[0])
            gt2 = dot_nn(w13_s[channels:, 0 : TAP_ROWS + 8], taps)
            g2 = (sl2_s[:, lanes] * gt2).astype(BF16)
            put(tan_refs[3], own_places, g2)
            pair_up(gt2, *moves[1])
            lin2 = dot_nn(w2_s[...], tan1)
            tan2 = (sl2_s[:, lanes] * lin2).astype(BF16)
            put(tan_refs[1], own_places, tan2)
            pair_up(lin2, *moves[2])
            gt1 = dot_nn(w2t_s[...], g2)
            g1 = (sl1_s[:, lanes] * gt1).astype(BF16)
            put(tan_refs[2], own_places, g1)
            pair_up(gt1, *moves[3])
            q_fwd = dot_nn(wout_s[:, 0:channels], tan2)[0:TAP_ROWS]
            q_s[:, lanes] = q_fwd + dot_nn(wout_s[:, channels:], g1)[0:TAP_ROWS]
            return carry

        over_blocks(count, body)

        inside = pl.ds(offset, count * BLOCK)
        result = comb_taps(q_s, inside, masks_at(inside))
        core_from = HALO - offset
        comb_s[stage - 1] = result[:, core_from : core_from + own]
        if stage < NMAX:
            nxt = result[:, LANES : count * BLOCK - LANES]
            lanes = pl.ds(offset + LANES, (count - 1) * BLOCK)
            seed = probes8[:, offset + LANES : offset + LANES + (count - 1) * BLOCK]
            coef = planes_ref[24 + 4 + 3 - stage : 24 + 4 + 4 - stage, lanes]
            following = slope0[:, offset + LANES : offset + LANES + (count - 1) * BLOCK] * nxt
            following = following + jnp.where(upper, seed * coef, 0.0)
            put_taps(stage + 1, col_taps(following, masks_at(lanes)), lanes)

    def own_taps(slot):
        return join(taps_s.at[slot], HALO // LANES, own // LANES)

    def add_weight_grads(slot_pairs, tap_pairs, first):
        total = None
        for left, right in slot_pairs:
            part = dot_nt(left, right)
            total = part if total is None else total + part
        one = None
        three = None
        for left_one, left_three, slot in tap_pairs:
            taps = own_taps(slot)
            part_one = dot_nt(taps, left_one)
            part_three = dot_nt(taps, left_three)
            one = part_one if one is None else one + part_one
            three = part_three if three is None else three + part_three
        w2_part = total.reshape(2 * chips, rows_own, channels)
        tile_part = jnp.where(first_rows, one, three)
        if first:
            w_s[:, :, 0:channels] = w2_part
            tile_s[...] = tile_part
        else:
            w_s[:, :, 0:channels] = w_s[:, :, 0:channels] + w2_part
            tile_s[...] = tile_s[...] + tile_part

    def slot_of(kind, slot):
        return join(tan_s[slot][kind], own_before[slot], own // LANES)

    series_stage(1)
    series_stage(2)
    series_stage(3)
    add_weight_grads(
        ((slot_of(0, 1), slot_of(3, 2)), (slot_of(0, 2), slot_of(3, 1))),
        (
            (slot_of(2, 2), slot_of(1, 2), 2),
            (slot_of(2, 1), slot_of(1, 1), 3),
        ),
        True,
    )
    series_stage(4)
    add_weight_grads(
        ((slot_of(0, 0), slot_of(3, 2)), (slot_of(0, 2), slot_of(3, 0))),
        (
            (slot_of(2, 2), slot_of(1, 2), 1),
            (slot_of(2, 0), slot_of(1, 0), 4),
        ),
        False,
    )

    def final_body(at, size, carry):
        bias_one, bias_two = carry
        start = pl.multiple_of(HALO - LANES + at, LANES)
        lanes = pl.ds(start, size)
        count = size // LANES
        ring_from = at // LANES
        own_places = run_of(g1c_s, start, size, HALO, own_before[2])
        gs2 = dot_nn(w13_s[channels:, 0 : TAP_ROWS + 8], join(taps_s.at[0], start // LANES, count))
        acc2 = join(cv2_s, ring_from, count).astype(F32) * join(lin2b_s, ring_from + kept_before, count).astype(F32)
        ga2 = (acc2 + acc2) + sl2_s[:, lanes] * gs2
        low2 = ga2.astype(BF16)
        gs1 = dot_nn(w2t_s[...], low2)
        acc1 = join(cv1_s, ring_from, count).astype(F32) * join(lin1b_s, ring_from + kept_before, count).astype(F32)
        ga1 = (acc1 + acc1) + sl1_s[:, lanes] * gs1
        low1 = ga1.astype(BF16)
        q_s[:, lanes] = q0_s[:, lanes] + dot_nn(wout_s[:, channels:], low1)[0:TAP_ROWS]
        put(g2c_s, own_places, low2)
        put(g1c_s, own_places, low1)
        for c in range(count):
            chunk = (start - HALO) // LANES + c
            here = jnp.where((chunk >= 0) & (chunk < own // LANES), 1.0, 0.0)
            bias_one = bias_one + here * ga1[:, c * LANES : (c + 1) * LANES]
            bias_two = bias_two + here * ga2[:, c * LANES : (c + 1) * LANES]
        return bias_one, bias_two

    zero = jnp.zeros((channels, LANES), F32)
    bias_one, bias_two = over_blocks(own_blocks + 1, final_body, (zero, zero))
    add_weight_grads(
        ((join(hid1_s, own_before[0], own // LANES), slot_of(3, 2)),), ((slot_of(2, 2), join(hid2_s, own_before[0], own // LANES), 0),), False
    )

    inside = pl.ds(HALO - LANES, own + BLOCK)
    result = comb_taps(q_s, inside, masks_at(inside))[:, LANES : LANES + own]
    mine = slice(HALO, HALO + own)
    h_own = h8[:, mine]
    cot_own = cot8[:, mine]
    probes_own = probes8[:, mine]
    mixed = comb_s[0] * pltpu.roll(comb_s[2], 4, 0)
    mixed = mixed + comb_s[1] * pltpu.roll(comb_s[1], 4, 0)
    mixed = mixed + comb_s[2] * pltpu.roll(comb_s[0], 4, 0)
    mixed = mixed + comb_s[3] * probes_own
    grad_h = cot_own + slope0[:, mine] * result + curve0[:, mine] * mixed
    grad_in = grad_h * scale8
    density = planes_ref[24:25, mine] * comb_s[0]
    for k in range(1, NMAX):
        density = density + planes_ref[24 + k : 25 + k, mine] * comb_s[k]
    density = density * probes_own
    density = density[0:1] + density[1:2] + density[2:3]
    row8 = iota((8, 1), 0)
    high = density.astype(BF16).astype(F32)
    out = jnp.where(row8 < 3, h_own + result + bias8, jnp.where(row8 == 3, high, grad_in))
    out = jnp.where(row8 == 7, density - high, out)
    if own < channels:
        out = jnp.concatenate([out, jnp.zeros((8, channels - own), F32)], axis=1)
    lines = [out[:, c * channels : (c + 1) * channels] for c in range(out.shape[1] // channels)]
    if len(lines) == 1:
        lines.append(jnp.zeros((8, channels), F32))
    out = jnp.concatenate(lines, axis=0).astype(BF16)
    og_ref[...] = jnp.zeros(og_ref.shape, BF16)
    og_ref[:, 0:channels] = out
    send_ref[chips * rows_own :, 0:channels] = out
    send_ref[chips * rows_own :, channels:] = jnp.zeros((out.shape[0], LANES), BF16)

    sums = (
        all_sum(grad_in, axis=1),
        all_sum(grad_h * h_own, axis=1) + extra8,
        all_sum(cot_own, axis=1),
    )
    small_row = jnp.zeros((1, LANES), F32)
    for a, column in enumerate(sums):
        for i in range(3):
            small_row = jnp.where(lane == TAP_ROWS + 2 + 3 * a + i, column[4 + i : 5 + i], small_row)
    bias_one = all_sum(bias_one, axis=1)
    bias_two = all_sum(bias_two, axis=1)
    extras = jnp.where(lane == TAP_ROWS, bias_one, jnp.where(lane == TAP_ROWS + 1, bias_two, small_row))
    blank = jnp.zeros((LANES - TAP_ROWS - 8, channels), F32)
    flat = jnp.concatenate([tile_s[...], blank], axis=0).T
    extras = jnp.where(lane < TAP_ROWS, flat, extras)
    w_s[:, :, channels:] = extras.reshape(2 * chips, rows_own, LANES)

    core = jnp.bitwise_and(me, 1)
    chip = jnp.right_shift(me, 1)
    for m in range(chips):
        block = 2 * jnp.bitwise_xor(chip, m)
        keep_ref[m] = w_s[block + core]
        send_ref[m * rows_own : (m + 1) * rows_own] = w_s[block + 1 - core].astype(BF16)


def output_rows(own, channels):
    return max(8 * (own // channels), 16)


def call_main(me, u3, u2, planes, small, packs, own, channels, chips):
    rows_own = channels // (2 * chips)
    region = own + 2 * HALO
    wide = (own + BLOCK) // LANES + 1
    width = channels + LANES
    out_shape = (
        pltpu.VMEM((chips, rows_own, width), F32),
        pltpu.VMEM((chips * rows_own + output_rows(own, channels), width), BF16),
        pltpu.VMEM((output_rows(own, channels), width), BF16),
        pltpu.VMEM((rows_own, LANES), F32),
        pltpu.VMEM((8, channels), F32),
    )
    vmem = pltpu.VMEM
    plan = buffer_plan(own)

    def buffer(name, lanes):
        return vmem((lanes // LANES + sum(plan[name]), channels, LANES), BF16)

    scratch = [
        vmem((2 * chips, rows_own, width), F32),
        vmem((2 * channels, LANES), BF16),
        vmem((channels, channels), BF16),
        vmem((channels, channels), BF16),
        vmem((TAP_ROWS + 8, 2 * channels), BF16),
        vmem((channels, LANES), F32),
        vmem((NMAX + 1, region // LANES, TAP_ROWS + 8, LANES), BF16),
        vmem((channels, region), F32),
        vmem((channels, region), F32),
        *[vmem((wide, channels, LANES), BF16)] * 6,
        *[buffer("kept", own + BLOCK)] * 8,
        *[buffer("early", own)] * 4,
        *[buffer("second", own)] * 4,
        *[buffer("late", own)] * 4,
        *[buffer("early", own)] * 2,
        vmem((TAP_ROWS, region), F32),
        vmem((TAP_ROWS, region), F32),
        vmem((NMAX, 8, own), F32),
        vmem((TAP_ROWS + 8, channels), F32),
        vmem((2 * chips, rows_own, LANES), F32),
    ]
    full = pl.BlockSpec(memory_space=pltpu.VMEM)
    return pl.pallas_call(
        functools.partial(main_kernel, own=own, channels=channels, chips=chips),
        out_shape=out_shape,
        in_specs=[pl.BlockSpec(memory_space=pltpu.SMEM)] * 2 + [full] * (3 + 2 * chips),
        out_specs=[full] * 5,
        scratch_shapes=scratch,
        compiler_params=pltpu.CompilerParams(vmem_limit_bytes=61 * 1024 * 1024),
        name="flow_block",
    )(me, u3, u2, planes, small, *packs)


def assemble_kernel(index_ref, kinds_ref, small_ref, *refs, own, channels, chips, frames):
    count = chips + 1 + (chips > 1)
    pieces = refs[:count]
    z_ref, gin_ref, logdet_ref, dens_s = refs[count:]
    me = index_ref[0]
    lines = max(own // channels, 1)
    size = min(own, channels)
    rows = output_rows(own, channels)
    for m in range(chips):
        for b in range(2):
            shard = jnp.bitwise_xor(me, 2 * m + b)
            if b == 0:
                block = pieces[m][pieces[m].shape[0] - rows :]
            elif m == 0:
                block = pieces[chips][...]
            else:
                block = pieces[chips + 1][(m - 1) * rows : m * rows]
            block = block.astype(F32)
            for c in range(lines):
                lanes = pl.ds(pl.multiple_of(shard * own + c * size, LANES), size)
                piece = block[8 * c : 8 * c + 8, 0:size]
                z_ref[:, lanes] = piece[0:3]
                gin_ref[:, lanes] = piece[4:7]
                dens_s[:, lanes] = piece[3:4] + piece[7:8]
    scale_sum = small_ref[1, 0] + small_ref[1, 1] + small_ref[1, 2]
    pixel = iota((1, FRAME), 1)
    bottom = (pixel // (WIDTH * 32)) % 2
    right = (pixel // 32) % 2
    lane = iota((1, 4), 1)
    for f in range(frames):
        line = dens_s[:, f * FRAME : (f + 1) * FRAME]
        quads = jnp.zeros((1, 4), F32)
        total = jnp.zeros((1, 1), F32)
        for slot in range(4):
            picked = jnp.where(bottom * 2 + right == slot, line, 0.0)
            picked = jnp.sum(picked, axis=1, keepdims=True)
            quads = jnp.where(lane == slot, picked, quads)
            total = total + picked
        split = kinds_ref[f] == 2
        whole = jnp.where(lane == 0, total + 4096.0 * scale_sum, 0.0)
        logdet_ref[f : f + 1, :] = jnp.where(split, quads + 1024.0 * scale_sum, whole)


def norm_kernel(index_ref, a_ref, b_ref, pack_ref, cols_ref, rows_ref, grad_ref, out_ref, *, channels):
    grad = a_ref[...].astype(F32) + b_ref[...].astype(F32)
    grad_ref[...] = grad
    lane = iota((1, LANES), 1)
    is_one = lane_is_one(lane)
    is_three = lane_is_three(lane)
    tile = grad[:, channels:]
    weights = pack_ref[:, channels:]
    cols = cols_ref[...]
    u1 = cols[:, 0:1]
    v2 = cols[:, 1:2]
    spread = jnp.where((lane % 8 == 4) & (lane < TAP_ROWS), cols, 0.0)
    spread = spread + pltpu.roll(spread, 1, 1) + pltpu.roll(spread, 2, 1)
    outer_one = u1 * rows_ref[1:2, 0:LANES]
    outer_three = spread * rows_ref[2:3, 0:LANES]
    outer_two = v2 * rows_ref[0:1, :]
    grad_two = grad[:, 0:channels]
    weight_two = pack_ref[:, 0:channels]

    def total(values):
        return jnp.sum(jnp.sum(values, axis=0, keepdims=True), axis=1, keepdims=True)

    bias = (lane == TAP_ROWS) | (lane == TAP_ROWS + 1)
    parts = (
        total(jnp.where(is_one, tile * tile, 0.0)),
        total(grad_two * grad_two),
        total(jnp.where(is_three, tile * tile, 0.0)),
        total(jnp.where(is_one, tile * weights, 0.0)),
        total(grad_two * weight_two),
        total(jnp.where(is_three, tile * weights, 0.0)),
        total(jnp.where(is_one, tile * outer_one, 0.0)),
        total(grad_two * outer_two),
        total(jnp.where(is_three, tile * outer_three, 0.0)),
        total(jnp.where(is_one, outer_one * outer_one, 0.0)),
        total(outer_two * outer_two),
        total(jnp.where(is_three, outer_three * outer_three, 0.0)),
        total(jnp.where(bias, tile * tile, 0.0)),
    )
    row = jnp.zeros((1, LANES), F32)
    for index, part in enumerate(parts):
        row = jnp.where(lane == index, part, row)
    small = (lane >= TAP_ROWS + 2) & (lane < TAP_ROWS + 11) & (index_ref[0] == 0)
    row = jnp.where(small, tile[0:1], row)
    out_ref[...] = jnp.broadcast_to(row, out_ref.shape)


def moment_step(grad, moment, second):
    new_moment = BETA_ONE * moment + (1.0 - BETA_ONE) * grad
    new_second = BETA_TWO * second + (1.0 - BETA_TWO) * grad * grad
    return (new_moment, new_second)


def adam_step(param, grad, moment, second):
    new_moment, new_second = moment_step(grad, moment, second)
    fix_one = 1.0 - BETA_ONE**STEP
    fix_two = 1.0 - BETA_TWO**STEP
    update = new_moment / fix_one / (jnp.sqrt(new_second / fix_two) + ADAM_EPS) + DECAY * param
    return (param - LR_RATE * update, new_moment, new_second)


def arrange_kernel(grad_ref, cols_ref, rows_ref, *refs, channels):
    for source, kept in zip(refs[:9], refs[9:18]):
        kept[...] = source[...]
    arrange_gradients(grad_ref, cols_ref, rows_ref, *refs[18:], channels=channels)


def arrange_gradients(
    grad_ref, cols_ref, rows_ref,
    g1_out, o1_out, o2_out, g3_out, o3_out, bias_out, u1_out, v1_out, u2_out, v2_out, u3_out, v3_out, *, channels,
):
    lane = iota((1, LANES), 1)
    cols = cols_ref[...]
    tile = grad_ref[:, channels:]
    is_one = lane_is_one(lane)
    is_three = lane_is_three(lane)
    spread = jnp.where((lane % 8 == 4) & (lane < TAP_ROWS), cols, 0.0)
    spread = spread + pltpu.roll(spread, 1, 1) + pltpu.roll(spread, 2, 1)
    outer_one = jnp.where(is_one, cols[:, 0:1] * rows_ref[1:2, 0:LANES], 0.0)
    outer_three = jnp.where(is_three, spread * rows_ref[2:3, 0:LANES], 0.0)
    o2_out[...] = cols[:, 1:2] * rows_ref[0:1, :]
    g1_out[...] = dot_nt(spread_one(), jnp.where(is_one, tile, 0.0), HIGH)
    o1_out[...] = dot_nt(spread_one(), outer_one, HIGH)
    g3_out[...] = dot_nt(spread_three(), jnp.where(is_three, tile, 0.0), HIGH)
    o3_out[...] = dot_nt(spread_three(), outer_three, HIGH)
    bias_out[...] = tile.T[TAP_ROWS : TAP_ROWS + 2, :]
    flipped = cols.T
    u1_out[...] = flipped[0:1]
    v2_out[...] = flipped[1:2]
    tap = iota((9, LANES), 0)
    select = (iota((9, LANES), 1) == (8 - tap) * 8 + 4).astype(F32)
    v3_out[...] = dot_nn(select, flipped, HIGH)
    v1_out[...] = dot_nt(rows_ref[1:2, 0:LANES], spread_one(), HIGH)
    u2_out[...] = rows_ref[0:1, :]
    u3_out[...] = rows_ref[2:3, 4:7]


def update_kernel(
    totals_ref, rows_ref, grad_ref, g1_ref, o1_ref, o2_ref, g3_ref, o3_ref, bias_ref,
    w1_ref, m1_ref, s1_ref, w2_ref, m2_ref, s2_ref, w3_ref, m3_ref, s3_ref,
    mb_ref, sb_ref, small_ref, msmall_ref, ssmall_ref,
    norm_out, nw1, nm1, ns1, nw2, nm2, ns2, nw3, nm3, ns3, cb, nmb, nsb, nsm, nmsm, nssm, lw1, lw2, lw3, *, channels,
):
    lane = iota((1, LANES), 1)
    lines = [totals_ref[m : m + 1] for m in range(totals_ref.shape[0])]
    while len(lines) > 1:
        lines = [lines[m] + lines[m + 1] for m in range(0, len(lines), 2)]
    row = lines[0]

    def pick(index):
        return row[:, index : index + 1]

    small_row = jnp.where((lane >= TAP_ROWS + 2) & (lane < TAP_ROWS + 11), row, 0.0)
    square = pick(12) + jnp.sum(small_row * small_row, axis=1, keepdims=True)
    scales = []
    for j in range(3):
        sigma = rows_ref[3:4, j : j + 1]
        ratio = SHRINK / sigma
        factor = pick(3 + j) / sigma
        fixed = pick(j) - 2.0 * factor * pick(6 + j) + factor * factor * pick(9 + j)
        square = square + ratio * ratio * jnp.maximum(fixed, 0.0)
        scales.append((ratio, factor))
    norm = jnp.sqrt(square)
    norm_out[...] = norm
    clip = jnp.minimum(1.0, CLIP_LIMIT / (norm + 1e-06))

    for index, grad, outer, w_ref, m_ref, s_ref, nw, nm, ns, lw in (
        (0, g1_ref[...], o1_ref, w1_ref, m1_ref, s1_ref, nw1, nm1, ns1, lw1),
        (1, grad_ref[:, 0:channels], o2_ref, w2_ref, m2_ref, s2_ref, nw2, nm2, ns2, lw2),
        (2, g3_ref[...], o3_ref, w3_ref, m3_ref, s3_ref, nw3, nm3, ns3, lw3),
    ):
        ratio, factor = scales[index]
        fixed = (clip * ratio) * (grad - factor * outer[...])
        new, moment, second = adam_step(w_ref[...], fixed, m_ref[...], s_ref[...])
        nw[...] = new
        nm[...] = moment
        ns[...] = second
        lw[...] = new.astype(BF16)

    bias = bias_ref[...] * clip
    cb[...] = bias
    moment, second = moment_step(bias, mb_ref[...], sb_ref[...])
    nmb[...] = moment
    nsb[...] = second

    small_row = small_row * clip
    lane3 = iota((1, 3), 1)
    rows = []
    for a in range(3):
        line = jnp.zeros((1, 3), F32)
        for i in range(3):
            at = TAP_ROWS + 2 + 3 * a + i
            line = jnp.where(lane3 == i, small_row[:, at : at + 1], line)
        rows.append(line)
    small_grad = jnp.concatenate(rows, axis=0)
    new, moment, second = adam_step(small_ref[...], small_grad, msmall_ref[...], ssmall_ref[...])
    nsm[...] = new
    nmsm[...] = moment
    nssm[...] = second


def prepare_kernel(
    index_ref, kinds_ref, len_ref, cot_ref, params_ref, images_ref, probes_ref, cot_z_ref,
    planes_ref, small_ref, *, own, frames,
):
    region = planes_ref.shape[1]
    pixels = images_ref.shape[1]
    me = index_ref[0]
    first = me * own - HALO
    planes_ref[...] = jnp.zeros(planes_ref.shape, F32)
    for chunk in range(region // LANES):
        start = first + chunk * LANES
        source = pl.ds(pl.multiple_of(jnp.clip(start, 0, pixels - LANES), LANES), LANES)
        lanes = pl.ds(chunk * LANES, LANES)
        inside = (start >= 0) & (start < pixels)
        for row, ref in ((0, images_ref), (4, images_ref), (8, probes_ref), (12, probes_ref), (20, cot_z_ref)):
            planes_ref[row : row + 3, lanes] = jnp.where(inside, ref[:, source], 0.0)

    position = first + iota((1, region), 1)
    frame = jnp.right_shift(position, 12)
    pixel = jnp.bitwise_and(position, FRAME - 1)
    row = jnp.right_shift(pixel, 6)
    col = jnp.bitwise_and(pixel, WIDTH - 1)
    half = WIDTH // 2
    quad = 2 * jnp.right_shift(row, 5) + jnp.right_shift(col, 5)
    split = jnp.zeros((1, region), jnp.int32)
    for f in range(frames):
        split = jnp.where(frame == f, jnp.where(kinds_ref[f] == 2, 1, 0), split)
    slot = 4 * frame + jnp.where(split == 1, quad, 0)
    length = jnp.zeros((1, region), jnp.int32)
    weight = jnp.zeros((1, region), F32)
    for f in range(frames):
        for q in range(4):
            here = slot == 4 * f + q
            length = jnp.where(here, len_ref[f, q], length)
            weight = jnp.where(here, cot_ref[f, q], weight)
    for k in range(NMAX):
        coef = jnp.where(length >= k + 1, (-1.0) ** k / (k + 1), 0.0)
        planes_ref[24 + k : 25 + k] = coef
        planes_ref[24 + NMAX + k : 25 + NMAX + k] = coef * weight
    for index, line in enumerate((row, col)):
        low = (line == 0) | ((split == 1) & (line == half))
        high = (line == WIDTH - 1) | ((split == 1) & (line == half - 1))
        planes_ref[32 + 2 * index : 33 + 2 * index] = jnp.where(low, 0.0, 1.0)
        planes_ref[33 + 2 * index : 34 + 2 * index] = jnp.where(high, 0.0, 1.0)

    extra = jnp.float32(0.0)
    for f in range(frames):
        whole = 4096.0 * cot_ref[f, 0]
        quads = 1024.0 * (cot_ref[f, 0] + cot_ref[f, 1] + cot_ref[f, 2] + cot_ref[f, 3])
        extra = extra + jnp.where(kinds_ref[f] == 2, quads, whole)
    extra = jnp.where(me == 0, extra, 0.0)
    row8 = iota((8, LANES), 0)
    lane = iota((8, LANES), 1)
    values = []
    for a in range(3):
        value = jnp.zeros((8, LANES), F32)
        for i in range(3):
            value = jnp.where(row8 % 4 == i, params_ref[a, i], value)
        values.append(value)
    result = jnp.where(lane == 0, values[0], jnp.where(lane == 1, jnp.exp(values[1]), values[2]))
    small_ref[...] = jnp.where(row8 % 4 == 3, 0.0, jnp.where(lane == 3, extra, result))


def local(
    images, frame_kinds, series_len, probes, cot_z, cot_logdet, weight1, weight2, weight3, biases,
    small_params, power_u1, power_u2, power_u3, moment_w1, second_w1, moment_w2, second_w2,
    moment_w3, second_w3, moment_bias, second_bias, moment_small, second_small,
):
    shards = lax.axis_size("chan")
    replicas = lax.axis_size("dp")
    chips = shards // 2
    me = lax.axis_index("chan")
    channels = weight2.shape[0]
    rows_own = weight1.shape[0]
    pixels = images.shape[1]
    frames = frame_kinds.shape[0]
    own = pixels // shards
    width = channels + LANES
    full = pl.BlockSpec(memory_space=pltpu.VMEM)
    smem = pl.BlockSpec(memory_space=pltpu.SMEM)
    index = me.reshape(1).astype(jnp.int32)

    def near_memory(values):
        return pltpu.with_memory_space_constraint(values, pltpu.VMEM)

    def swap(values, axis, size, bits):
        return lax.ppermute(values, axis, [(j, j ^ bits) for j in range(size)])

    pack = pl.pallas_call(
        pack_kernel,
        out_shape=pltpu.VMEM((rows_own, width), F32),
        in_specs=[full] * 5,
        out_specs=full,
        name="pack_weights",
    )(weight1.T, weight2.T, weight3, biases, power_u1.reshape(1, rows_own))
    near = [pack] + [swap(pack, "chan", shards, 2 * m) for m in range(1, chips)]
    planes, small = pl.pallas_call(
        functools.partial(prepare_kernel, own=own, frames=frames),
        out_shape=(
            pltpu.VMEM((40, own + 2 * HALO), F32),
            pltpu.VMEM((8, LANES), F32),
        ),
        in_specs=[smem] * 5 + [full] * 3,
        out_specs=[full] * 2,
        name="prepare_planes",
    )(index, frame_kinds, series_len, cot_logdet, small_params, images, probes, cot_z)

    near[-1], planes = lax.optimization_barrier((near[-1], planes))
    packs = []
    for values in near:
        packs += [values, swap(values, "chan", shards, 1)]

    keep, send, og, cols_own, rows = call_main(
        index, power_u3, power_u2.reshape(1, channels), near_memory(planes), near_memory(small),
        [near_memory(values) for values in packs], own, channels, chips
    )

    got = swap(send, "chan", shards, 1)
    og_other = got[chips * rows_own :]
    summed = keep + got[: chips * rows_own].reshape(keep.shape).astype(F32)
    total = summed[0]
    near_og = [og]
    for m in range(1, chips):
        message = jnp.concatenate([summed[m].astype(BF16), og], axis=0)
        message = swap(message, "chan", shards, 2 * m)
        total = total + message[:rows_own].astype(F32)
        near_og.append(message)
    tails = [message[rows_own:] for message in near_og[1:]]
    pieces = near_og + [og_other]
    if tails:
        pieces.append(swap(jnp.concatenate(tails, axis=0), "chan", shards, 1))
    half = total.astype(BF16)
    assembled = pl.pallas_call(
        functools.partial(assemble_kernel, own=own, channels=channels, chips=chips, frames=frames),
        out_shape=(
            jax.ShapeDtypeStruct((3, pixels), F32),
            jax.ShapeDtypeStruct((3, pixels), F32),
            jax.ShapeDtypeStruct((frames, 4), F32),
        ),
        in_specs=[smem] * 3 + [full] * len(pieces),
        out_specs=[full] * 3,
        scratch_shapes=[pltpu.VMEM((1, pixels), F32)],
        name="assemble_outputs",
    )(index, frame_kinds, small_params, *[near_memory(piece) for piece in pieces])
    bits = 1
    while 2 * bits < replicas:
        half = (half.astype(F32) + swap(half, "dp", replicas, bits).astype(F32)).astype(BF16)
        bits *= 2
    other = swap(half, "dp", replicas, bits) if replicas > 1 else jnp.zeros_like(half)
    other, assembled = lax.optimization_barrier((other, assembled))
    z_out, grad_input, logdet = assembled


    grad, parts = pl.pallas_call(
        functools.partial(norm_kernel, channels=channels),
        out_shape=(
            pltpu.VMEM((rows_own, width), F32),
            pltpu.VMEM((8, LANES), F32),
        ),
        in_specs=[smem] + [full] * 5,
        out_specs=[full] * 2,
        name="norm_parts",
    )(index, near_memory(half), near_memory(other), near_memory(pack), near_memory(cols_own), near_memory(rows))
    pair = parts + swap(parts, "chan", shards, 1)
    totals = [pair[0:1]] + [swap(pair, "chan", shards, 2 * m)[0:1] for m in range(1, chips)]
    totals = jnp.concatenate(totals, axis=0)

    def like(value, dtype=F32):
        return jax.ShapeDtypeStruct(value.shape, dtype)

    arranged_shape = (
        [pltpu.VMEM(weight1.T.shape, F32)] * 2
        + [pltpu.VMEM((rows_own, channels), F32)]
        + [pltpu.VMEM(weight3.shape, F32)] * 2
        + [pltpu.VMEM(biases.shape, F32)]
        + [jax.ShapeDtypeStruct((1, rows_own), F32), jax.ShapeDtypeStruct((1, 27), F32)]
        + [jax.ShapeDtypeStruct((1, channels), F32), jax.ShapeDtypeStruct((1, rows_own), F32)]
        + [jax.ShapeDtypeStruct((1, 3), F32), jax.ShapeDtypeStruct((9, rows_own), F32)]
    )
    state = (
        weight1.T, moment_w1.T, second_w1.T, weight2.T, moment_w2.T, second_w2.T, weight3, moment_w3, second_w3,
    )
    arranged_shape = [pltpu.VMEM(value.shape, F32) for value in state] + arranged_shape
    arranged = pl.pallas_call(
        functools.partial(arrange_kernel, channels=channels),
        out_shape=arranged_shape,
        in_specs=[full] * 12,
        out_specs=[full] * len(arranged_shape),
        name="arrange_gradients",
    )(near_memory(grad), near_memory(cols_own), near_memory(rows), *state)
    state, arranged = arranged[:9], arranged[9:]
    vectors = arranged[6:]
    out_shape = (
        [jax.ShapeDtypeStruct((1, 1), F32)]
        + [like(weight1.T)] * 3
        + [like(weight2.T)] * 3
        + [like(weight3)] * 3
        + [like(biases)] * 3
        + [like(small_params)] * 3
        + [like(weight1.T, BF16), like(weight2.T, BF16), like(weight3, BF16)]
    )
    done = pl.pallas_call(
        functools.partial(update_kernel, channels=channels),
        out_shape=out_shape,
        in_specs=[full] * 23,
        out_specs=[full] * len(out_shape),
        name="adam_update",
    )(
        *[near_memory(values) for values in (totals, rows, grad, *arranged[:6])],
        *[near_memory(values) for values in state], moment_bias, second_bias, small_params, moment_small, second_small,
    )
    norm, updates = done[0], list(done[1:])
    for slot in (0, 1, 2, 3, 4, 5, 15, 16):
        updates[slot] = updates[slot].T
    return (
        z_out,
        logdet,
        grad_input,
        norm.reshape(()),
        *updates,
        vectors[0].reshape(rows_own),
        vectors[1].reshape(27),
        vectors[2].reshape(channels),
        vectors[3].reshape(rows_own),
        vectors[4].reshape(3),
        vectors[5],
    )


def solution(mesh):
    chan_rows = P("chan", None)
    chan_cols = P(None, "chan")
    return jax.shard_map(
        local,
        mesh=mesh,
        in_specs=(
            P(None, "dp"), P("dp"), P("dp", None), P(None, "dp"), P(None, "dp"), P("dp", None),
            chan_rows, chan_cols, chan_cols, chan_cols, P(), P("chan"), P(), P(),
            chan_rows, chan_rows, chan_cols, chan_cols, chan_cols, chan_cols, chan_cols, chan_cols, P(), P(),
        ),
        out_specs=(
            P(None, "dp"), P("dp", None), P(None, "dp"), P(),
            chan_rows, chan_rows, chan_rows, chan_cols, chan_cols, chan_cols, chan_cols, chan_cols, chan_cols,
            chan_cols, chan_cols, chan_cols, P(), P(), P(), chan_rows, chan_cols, chan_cols,
            P("chan"), P(), P(), P("chan"), P(), chan_cols,
        ),
        check_vma=False,
    )
```
